32 devices in a mesh: state: 4 (over y, x), space: 8 (over z, core).
Axes of the slice: x: 2, y: 2, z: 4, core: 2. Of those that a mesh axis runs over, the one named last changes fastest.
Arguments:
- states_in: bfloat16 [384, 8192], P('state', 'space'), may hold values from -12 to 12
- cell_matrices: bfloat16 [16, 512, 512], P('space'), may hold values from -0.5 to 1.5, as said below
- connectivity: int32 [16, 512], P('space'), may hold values from 0 to 8191, as said below
- potential: float32 [8192], P('space'), may hold values from 0.2 to 1.2
Outputs:
- filtered: bfloat16 [384, 8192], P('state', 'space')
- intersection: float32 [384, 384], P('state', 'space')
- projected: float32 [384, 384], P('state', 'space')
The draws below stay inside these ranges and needn't reach their ends.
Inputs may be any that keep to these rules, and one draw needn't show every extreme that they name: `cell_matrices`: each cell's matrix is symmetric. `connectivity`: the cells of rows s * 2 to (s + 1) * 2 - 1 name only nodes from s * 1024 - 128 to (s + 1) * 1024 + 127. A node may be named by several cells, or twice in one cell, or by none.
All inputs are finite; a program needn't handle non-finite values.
Results may differ from the reference program's by a relative error of at most 0.019.
Values may be sent and summed in bfloat16 or wider, within the bound.
No kernel may reach another device: no remote copies, remote signals or barrier semaphores. Data moves between devices by JAX's collectives and lax.ppermute only.
A program may use at most 64 MiB of HBM per device.

```python
import jax
import jax.numpy as jnp
from jax import lax

CELL_NODES = 512
CELLS_DEV = 2
DEGREE = 4
NSTATES = 384
NODE_DEV = 1024
NODES = 8192
CELLS = 16
RIM = 128


def draw_states_in(key, part):
    mode_count = NSTATES // 2
    first_key = jax.random.fold_in(key, 11)
    second_key = jax.random.fold_in(key, 12)
    third_key = jax.random.fold_in(key, 13)
    base = jax.random.normal(first_key, (NSTATES, NODES), jnp.float32)
    mixing = jax.random.normal(third_key, (NSTATES, mode_count), jnp.float32)
    shared_modes = jax.random.normal(second_key, (mode_count, NODES), jnp.float32)
    shared = jnp.dot(mixing, shared_modes) * (1.5 / mode_count ** 0.5)
    ramp = jnp.sqrt(1.0 + 2.0 * jnp.arange(NODES, dtype=jnp.float32) / NODES)
    values = (base + shared) * ramp[None, :]
    return jnp.clip(values, -12.0, 12.0).astype(jnp.bfloat16)


def draw_cell_matrices(key, part):
    first_key = jax.random.fold_in(key, 21)
    second_key = jax.random.fold_in(key, 22)
    spread = 0.35 / CELL_NODES ** 0.5
    random_part = jnp.clip(jax.random.normal(first_key, (CELLS, CELL_NODES, CELL_NODES), jnp.float32), -4.0, 4.0) * spread
    diagonal = jax.random.uniform(second_key, (CELLS, 1, CELL_NODES), jnp.float32, 0.3, 1.0)
    identity = jnp.eye(CELL_NODES, dtype=jnp.float32)[None, :, :]
    return (random_part + jnp.swapaxes(random_part, 1, 2) + identity * diagonal).astype(jnp.bfloat16)


def draw_connectivity(key, part):
    shard = jnp.arange(CELLS, dtype=jnp.int32) // CELLS_DEV
    lower = jnp.maximum(shard * NODE_DEV - RIM, 0)
    upper = jnp.minimum((shard + 1) * NODE_DEV + RIM, NODES)
    return jax.random.randint(jax.random.fold_in(key, 31), (CELLS, CELL_NODES), lower[:, None], upper[:, None], jnp.int32)


def steps_of(own_key, shape, split, low, top_value):
    factor_of, own = 1.0, jax.random.fold_in(own_key, 6)
    for dim, blocks in split:
        steps = jnp.exp(jax.random.uniform(jax.random.fold_in(own, dim), (blocks,), jnp.float32, low / len(split), top_value / len(split)))
        factor_of = factor_of * jnp.repeat(steps, shape[dim] // blocks).reshape([-1 if axis == dim else 1 for axis in range(len(shape))])
    return factor_of


def setup_inputs(seed: int = 0) -> dict:
    key_of = jax.random.split(jax.random.key(seed), 5)
    return {
        "states_in": draw_states_in(jax.random.fold_in(key_of[4], 71), 0),
        "cell_matrices": draw_cell_matrices(jax.random.fold_in(key_of[4], 71), 0),
        "connectivity": draw_connectivity(jax.random.fold_in(key_of[4], 71), 0),
        "potential": jnp.clip(0.2 + 1 * jax.random.uniform(key_of[3], (NODES,), jnp.float32) ** steps_of(key_of[3], (NODES,), ((0, 8),), -0.2, 0.2), 0.2, 1.2),
    }


spectrum_center = 3.0
spectrum_half = 3.5


def apply_hamiltonian(states, cell_matrices, connectivity, potential):
    picked = states[:, connectivity].astype(jnp.float32)
    products = jnp.einsum("scp,cpq->scq", picked, cell_matrices.astype(jnp.float32), precision=lax.Precision.HIGHEST)
    summed = jnp.zeros(states.shape, jnp.float32)
    summed = summed.at[:, connectivity.reshape(-1)].add(products.reshape(states.shape[0], -1))
    return summed + potential[None, :] * states.astype(jnp.float32)


def reference(states_in, cell_matrices, connectivity, potential):
    earlier = states_in
    first = (apply_hamiltonian(earlier, cell_matrices, connectivity, potential) - spectrum_center * earlier.astype(jnp.float32)) / spectrum_half
    current = first.astype(jnp.bfloat16)
    for section_index in range(DEGREE - 1):
        image = apply_hamiltonian(current, cell_matrices, connectivity, potential)
        following = 2.0 * (image - spectrum_center * current.astype(jnp.float32)) / spectrum_half - earlier.astype(jnp.float32)
        earlier = current
        current = following.astype(jnp.bfloat16)
    filtered = current
    energy = apply_hamiltonian(filtered, cell_matrices, connectivity, potential)
    intersection = jnp.dot(filtered, filtered.T, preferred_element_type=jnp.float32) / NODES
    projected = jnp.dot(energy, filtered.astype(jnp.float32).T, precision=lax.Precision.HIGHEST) / NODES
    return filtered, intersection, projected
```

```python
import functools

import jax
import jax.numpy as jnp
from jax import lax
from jax.experimental import pallas as pl
from jax.experimental.pallas import tpu as pltpu
from jax.sharding import PartitionSpec as P

DEGREE = 4

spectrum_center = 3.0
spectrum_half = 3.5

BF16 = jnp.bfloat16
F32 = jnp.float32


def call(body, outs, flops, n_in, smem_first=True, aliases=None, scratch=(), moved=4 << 20):
    specs = [pl.BlockSpec(memory_space=pltpu.VMEM)] * n_in
    if smem_first:
        specs = [pl.BlockSpec(memory_space=pltpu.SMEM)] + specs
    return pl.pallas_call(
        body,
        out_shape=outs,
        in_specs=specs,
        out_specs=jax.tree.map(lambda _: pl.BlockSpec(memory_space=pltpu.VMEM), outs),
        scratch_shapes=list(scratch),
        input_output_aliases=aliases or {},
        compiler_params=pltpu.CompilerParams(vmem_limit_bytes=24 << 20),
        cost_estimate=pl.CostEstimate(flops=flops, bytes_accessed=moved, transcendentals=0),
    )


def assemble_body(cells_ref, row_ref, col_ref, matrix_ref, diagonal_ref, wide_ref):
    cells, nodes, _ = cells_ref.shape
    extent = matrix_ref.shape[0]
    step = 256
    for c in range(cells):
        hot = lax.broadcasted_iota(jnp.int32, (extent, nodes), 0) == row_ref[c : c + 1, :]
        half = jnp.dot(hot.astype(BF16), cells_ref[c], preferred_element_type=F32)
        wide_ref[:, c * nodes : (c + 1) * nodes] = half.astype(BF16)
    spread = lax.broadcasted_iota(jnp.int32, (cells * nodes, extent), 1) == col_ref[...]
    spread = spread.astype(BF16)
    for start in range(0, extent, step):
        rows = jnp.dot(wide_ref[start : start + step, :], spread, preferred_element_type=F32)
        own = lax.broadcasted_iota(jnp.int32, rows.shape, 0) + start == lax.broadcasted_iota(
            jnp.int32, rows.shape, 1
        )
        piece = jnp.where(own, rows, 0.0)
        diagonal_ref[:, start : start + step] = jnp.sum(
            piece[:, start : start + step], axis=0, keepdims=True
        )
        matrix_ref[start : start + step, :] = jnp.where(own, 0.0, rows).astype(BF16)


def assemble(cell_matrices, local_index, extent):
    cells, nodes, _ = cell_matrices.shape
    outs = (
        jax.ShapeDtypeStruct((extent, extent), BF16),
        jax.ShapeDtypeStruct((1, extent), F32),
    )
    return call(
        assemble_body,
        outs,
        2 * extent * nodes * cells * (nodes + extent),
        3,
        smem_first=False,
        scratch=[pltpu.VMEM((extent, cells * nodes), BF16)],
    )(cell_matrices, local_index, local_index.reshape(-1, 1))


def pick(low_first, low, high):
    return jnp.where(low_first, low, high)


def apply_to(level_ref, matrix_ref, diagonal_ref):
    level = level_ref[...]
    sums = jnp.dot(level, matrix_ref[...], preferred_element_type=F32)
    return sums + diagonal_ref[...] * level.astype(F32)


def finish_zones(place, width, own_ref, got_a_ref, got_b_ref, shift_ref, mid_ref, old_ref, scale, level_ref):
    extent = level_ref.shape[1]
    odd, first, last = place[0] == 1, place[1] == 1, place[2] == 1
    got_a, got_b = got_a_ref[...].astype(F32), got_b_ref[...].astype(F32)
    got_low = jnp.where(first, 0.0, jnp.where(odd, got_a, got_b))
    got_high = jnp.where(last, 0.0, jnp.where(odd, got_b, got_a))
    for got, mine, at in ((got_low, 0, 0), (got_high, width, extent - width)):
        here = slice(at, at + width)
        total = own_ref[:, mine : mine + width] + got
        value = (total + shift_ref[:, here] * mid_ref[:, here].astype(F32)) * scale
        if old_ref is not None:
            value = value - old_ref[:, here].astype(F32)
        level_ref[:, here] = value.astype(BF16)


def advance(place, width, level_ref, old_ref, matrix_ref, diagonal_ref, shift_ref, scale, following_ref, own_ref, give_a_ref, give_b_ref):
    extent = level_ref.shape[1]
    sums = apply_to(level_ref, matrix_ref, diagonal_ref)
    inside = slice(width, extent - width)
    value = (sums[:, inside] + shift_ref[:, inside] * level_ref[:, inside].astype(F32)) * scale
    if old_ref is not None:
        value = value - old_ref[:, inside].astype(F32)
    following_ref[:, inside] = value.astype(BF16)
    low, high = sums[:, :width], sums[:, extent - width :]
    own_ref[:, :width] = low
    own_ref[:, width:] = high
    odd = place[0] == 1
    give_a_ref[...] = jnp.where(odd, low, high).astype(BF16)
    give_b_ref[...] = jnp.where(odd, high, low).astype(BF16)


def first_body(place, states_ref, halo_a_ref, halo_b_ref, potential_ref, matrix_ref, diagonal_ref,
               level_ref, shift_ref, following_ref, own_ref, give_a_ref, give_b_ref):
    count, owned = states_ref.shape
    extent = level_ref.shape[1]
    rim = (extent - owned) // 2
    odd, first, last = place[0] == 1, place[1] == 1, place[2] == 1
    got_a, got_b = halo_a_ref[...].astype(F32), halo_b_ref[...].astype(F32)
    got_low = jnp.where(first, 0.0, jnp.where(odd, got_a, got_b))
    got_high = jnp.where(last, 0.0, jnp.where(odd, got_b, got_a))
    level_ref[:, rim : rim + owned] = states_ref[...]
    level_ref[:, :rim] = got_low[:count].astype(BF16)
    level_ref[:, rim + owned :] = got_high[:count].astype(BF16)
    shift_ref[:, rim : rim + owned] = potential_ref[...] - spectrum_center
    for got, at in ((got_low, 0), (got_high, rim + owned)):
        parts = got[count : count + 8]
        value = parts[0:1] + parts[1:2] + parts[2:3]
        shift_ref[:, at : at + rim] = value - spectrum_center
    advance(place, 2 * rim, level_ref, None, matrix_ref, diagonal_ref, shift_ref, 1.0 / spectrum_half,
            following_ref, own_ref, give_a_ref, give_b_ref)


def middle_body(with_old, place, own_ref, got_a_ref, got_b_ref, open_ref, mid_ref, *rest):
    if with_old:
        old_ref, *rest = rest
    else:
        old_ref = None
    (shift_ref, matrix_ref, diagonal_ref,
     level_ref, following_ref, next_own_ref, give_a_ref, give_b_ref) = rest
    width = got_a_ref.shape[1]
    extent = mid_ref.shape[1]
    scale = (2.0 if with_old else 1.0) / spectrum_half
    inside = slice(width, extent - width)
    level_ref[:, inside] = open_ref[:, inside]
    finish_zones(place, width, own_ref, got_a_ref, got_b_ref, shift_ref, mid_ref, old_ref, scale, level_ref)
    advance(place, width, level_ref, mid_ref, matrix_ref, diagonal_ref, shift_ref, 2.0 / spectrum_half,
            following_ref, next_own_ref, give_a_ref, give_b_ref)


def last_body(place, own_ref, got_a_ref, got_b_ref, open_ref, mid_ref, old_ref, shift_ref, level_ref, filtered_ref):
    width = got_a_ref.shape[1]
    extent = mid_ref.shape[1]
    rim = width // 2
    inside = slice(width, extent - width)
    level_ref[:, inside] = open_ref[:, inside]
    finish_zones(place, width, own_ref, got_a_ref, got_b_ref, shift_ref, mid_ref, old_ref,
                 2.0 / spectrum_half, level_ref)
    filtered_ref[...] = level_ref[:, rim : extent - rim]


def energy_body(place, level_ref, matrix_ref, diagonal_ref, shift_ref, energy_ref, give_a_ref, give_b_ref):
    extent = level_ref.shape[1]
    owned = energy_ref.shape[1]
    rim = (extent - owned) // 2
    sums = apply_to(level_ref, matrix_ref, diagonal_ref)
    here = slice(rim, rim + owned)
    energy_ref[...] = sums[:, here] + (shift_ref[:, here] + spectrum_center) * level_ref[:, here].astype(F32)
    low, high = sums[:, :rim], sums[:, rim + owned :]
    odd = place[0] == 1
    give_a_ref[...] = jnp.where(odd, low, high).astype(BF16)
    give_b_ref[...] = jnp.where(odd, high, low).astype(BF16)


def project_body(total_nodes, groups, place, energy_ref, got_a_ref, got_b_ref, *refs):
    blocks, out_ref, pair_ref = refs[:groups], refs[groups], refs[groups + 1]
    count, owned = energy_ref.shape
    rim = got_a_ref.shape[1]
    odd, first, last = place[0] == 1, place[1] == 1, place[2] == 1
    got_a, got_b = got_a_ref[...].astype(F32), got_b_ref[...].astype(F32)
    got_low = jnp.where(first, 0.0, jnp.where(odd, got_a, got_b))
    got_high = jnp.where(last, 0.0, jnp.where(odd, got_b, got_a))
    pair_ref[:count, :] = blocks[0][...]
    pair_ref[count:, :rim] = (energy_ref[:, :rim] + got_low).astype(BF16)
    pair_ref[count:, rim : owned - rim] = energy_ref[:, rim : owned - rim].astype(BF16)
    pair_ref[count:, owned - rim :] = (energy_ref[:, owned - rim :] + got_high).astype(BF16)
    group = place[3]
    pair = pair_ref[...]
    for distance in range(groups):
        part = lax.dot_general(
            blocks[distance][...], pair, (((1,), (1,)), ((), ())), preferred_element_type=F32
        )
        at = pl.multiple_of((group ^ distance) * count, count)
        out_ref[pl.ds(at, count), :] = (part * (1.0 / total_nodes)).astype(BF16)


def halve_body(place, mine_ref, got_ref, sum_ref):
    core = place[0]
    for j in range(sum_ref.shape[0]):
        mine = jnp.where(core == 1, mine_ref[j, 1].astype(F32), mine_ref[j, 0].astype(F32))
        sum_ref[j] = (mine + got_ref[j].astype(F32)).astype(BF16)


def final_body(count, *refs):
    parts, (first_ref, second_ref) = refs[:-2], refs[-2:]
    total = parts[0][...].astype(F32)
    for part in parts[1:]:
        total = total + part[...].astype(F32)
    first_ref[...] = total[:, :count].T
    second_ref[...] = total[:, count:].T


def swap(block, n_state, n_space, lead):
    route = []
    for s in range(n_state):
        for i in range(n_space):
            j = i + 1 if (i - lead) % 2 == 0 else i - 1
            if 0 <= j < n_space:
                route.append((s * n_space + i, s * n_space + j))
            elif (s ^ 1) < n_state:
                route.append((s * n_space + i, (s ^ 1) * n_space + i))
    return lax.ppermute(block, ("state", "space"), route)


def exchange(pair, n_state, n_space):
    give_a, give_b = pair
    got_b = swap(give_b, n_state, n_space, 1)
    got_a = swap(give_a, n_state, n_space, 0)
    return got_a, got_b


def across(block, axis, distance):
    return lax.ppermute(block, axis, [(i, i ^ distance) for i in range(lax.axis_size(axis))])


def three_parts(row):
    high = lax.reduce_precision(row, 8, 7)
    mid = lax.reduce_precision(row - high, 8, 7)
    low = (row - high) - mid
    return jnp.concatenate([high, mid, low], axis=0).astype(BF16)


def per_device(states_in, cell_matrices, connectivity, potential):
    count, owned = states_in.shape
    rim = cell_matrices.shape[1] // 4
    extent = owned + 2 * rim
    n_state, n_space = lax.axis_size("state"), lax.axis_size("space")
    me = lax.axis_index("space")
    group = lax.axis_index("state")
    odd = me % 2
    place = jnp.stack(
        [odd, (me == 0).astype(jnp.int32), (me == n_space - 1).astype(jnp.int32), group]
    ).astype(jnp.int32)
    local_index = connectivity - (me * owned - rim)

    row = potential.reshape(1, owned)
    parts = three_parts(row)
    parts = jnp.concatenate([parts, jnp.zeros((13, owned), BF16)], axis=0)
    low = jnp.concatenate([states_in[:, :rim], parts[:, :rim]], axis=0)
    high = jnp.concatenate([states_in[:, owned - rim :], parts[:, owned - rim :]], axis=0)
    halo = exchange(
        (jnp.where(odd == 1, low, high), jnp.where(odd == 1, high, low)), n_state, n_space
    )
    matrix, diagonal = assemble(cell_matrices, local_index, extent)

    shape = jax.ShapeDtypeStruct
    wide, line = shape((count, extent), BF16), shape((1, extent), F32)
    own, give = shape((count, 4 * rim), F32), shape((count, 2 * rim), BF16)
    flops = 2 * count * extent * extent
    start, shift, opened, sums, *gave = call(
        first_body, (wide, line, wide, own, give, give), flops, 6
    )(place, states_in, *halo, row, matrix, diagonal)
    levels = [start]
    for k in range(1, DEGREE):
        got = exchange(gave, n_state, n_space)
        older = levels[-2:-1]
        level, opened, sums, *gave = call(
            functools.partial(middle_body, bool(older)),
            (wide, wide, own, give, give), flops, 8 + len(older),
        )(place, sums, *got, opened, levels[-1], *older, shift, matrix, diagonal)
        levels.append(level)
    got = exchange(gave, n_state, n_space)
    level, filtered = call(last_body, (wide, shape((count, owned), BF16)), 0, 7)(
        place, sums, *got, opened, levels[-1], levels[-2], shift
    )
    rim_give = shape((count, rim), BF16)
    energy, *gave = call(
        energy_body, (shape((count, owned), F32), rim_give, rim_give), flops, 4
    )(place, level, matrix, diagonal, shift)
    blocks = [filtered] + [across(filtered, "state", d) for d in range(1, n_state)]
    got = exchange(gave, n_state, n_space)
    total_states = count * n_state
    partial = call(
        functools.partial(project_body, owned * n_space, n_state),
        shape((total_states, 2 * count), BF16), 2 * total_states * 2 * count * owned, 3 + n_state,
        scratch=[pltpu.VMEM((2 * count, owned), BF16)],
    )(place, energy, *got, *blocks)

    columns = total_states // n_space
    partial = partial.reshape(n_space // 2, 2, columns, 2 * count)
    give = jnp.where(odd == 1, partial[:, 0], partial[:, 1])
    got = swap(give, n_state, n_space, 0)
    halved = call(halve_body, shape(give.shape, BF16), 0, 2)(place, partial, got)
    chip = me // 2
    pieces = [
        lax.dynamic_index_in_dim(halved, chip ^ d, 0, keepdims=False) for d in range(n_space // 2)
    ]
    pieces = [pieces[0]] + [across(p, "space", 2 * d) for d, p in enumerate(pieces) if d]
    square = shape((count, columns), F32)
    intersection, projected = call(
        functools.partial(final_body, count), (square, square), 0, len(pieces), smem_first=False
    )(*pieces)
    return filtered, intersection, projected


def solution(mesh):
    return jax.shard_map(
        per_device,
        mesh=mesh,
        in_specs=(P("state", "space"), P("space", None, None), P("space", None), P("space")),
        out_specs=(P("state", "space"), P("state", "space"), P("state", "space")),
        check_vma=False,
    )
```

```python
import functools

import jax
import jax.numpy as jnp
from jax import lax
from jax.experimental import pallas as pl
from jax.experimental.pallas import tpu as pltpu
from jax.sharding import PartitionSpec as P


DEGREE = 4

spectrum_center = 3.0
spectrum_half = 3.5

BF16 = jnp.bfloat16
F32 = jnp.float32
SHAPE = jax.ShapeDtypeStruct


ODD, FIRST, LAST, GROUP, CHIP, OFFSET = range(6)


def call(body, outs, ins, flops, scratch=(), raw=()):
    where = [pl.BlockSpec(memory_space=pltpu.SMEM)]
    for i in range(1, len(ins)):
        where.append(pl.BlockSpec(memory_space=pltpu.HBM if i in raw else pltpu.VMEM))
    ins = [pltpu.with_memory_space_constraint(x, pltpu.HBM) if i in raw else x for i, x in enumerate(ins)]
    return pl.pallas_call(
        body,
        out_shape=outs,
        in_specs=where,
        out_specs=jax.tree.map(lambda _: pl.BlockSpec(memory_space=pltpu.VMEM), outs),
        scratch_shapes=list(scratch),
        compiler_params=pltpu.CompilerParams(vmem_limit_bytes=24 << 20),
        cost_estimate=pl.CostEstimate(flops=flops, bytes_accessed=4 << 20, transcendentals=0),
    )(*ins)


def mm(a, b):
    return jnp.dot(a, b, preferred_element_type=F32)


def mm_nt(a, b):
    return lax.dot_general(a, b, (((1,), (1,)), ((), ())), preferred_element_type=F32)


def sort_out(place, got_a, got_b):
    odd = place[ODD] == 1
    got_a, got_b = got_a.astype(F32), got_b.astype(F32)
    low = jnp.where(place[FIRST] == 1, 0.0, jnp.where(odd, got_a, got_b))
    high = jnp.where(place[LAST] == 1, 0.0, jnp.where(odd, got_b, got_a))
    return low, high


def hand_out(place, low, high, give_a_ref, give_b_ref):
    odd = place[ODD] == 1
    give_a_ref[...] = jnp.where(odd, low, high).astype(give_a_ref.dtype)
    give_b_ref[...] = jnp.where(odd, high, low).astype(give_b_ref.dtype)


def halo_body(place, states_ref, potential_ref, index_ref,
              give_a_ref, give_b_ref, local_ref, low_ref, high_ref, row_ref, sem):
    count, owned = states_ref.shape
    rim = low_ref.shape[1]
    copies = [
        pltpu.make_async_copy(states_ref.at[:, pl.ds(0, rim)], low_ref, sem.at[0]),
        pltpu.make_async_copy(states_ref.at[:, pl.ds(owned - rim, rim)], high_ref, sem.at[1]),
        pltpu.make_async_copy(potential_ref, row_ref, sem.at[2]),
        pltpu.make_async_copy(index_ref, local_ref, sem.at[3]),
    ]
    for copy in copies:
        copy.start()
    for copy in copies:
        copy.wait()
    odd = place[ODD] == 1
    low, high = low_ref[...].astype(F32), high_ref[...].astype(F32)
    give_a_ref[:count, :] = jnp.where(odd, low, high).astype(BF16)
    give_b_ref[:count, :] = jnp.where(odd, high, low).astype(BF16)
    for take, give_ref in ((odd, give_a_ref), (jnp.logical_not(odd), give_b_ref)):
        row = jnp.where(take, row_ref[:, :rim], row_ref[:, owned - rim :])
        row = jnp.broadcast_to(row, (16, rim))
        at = lax.broadcasted_iota(jnp.int32, row.shape, 0)
        first = row.astype(BF16).astype(F32)
        second = (row - first).astype(BF16).astype(F32)
        third = (row - first) - second
        give_ref[count:, :] = jnp.where(
            at == 0, first, jnp.where(at == 1, second, jnp.where(at == 2, third, 0.0))
        ).astype(BF16)


def spread_body(place, index_ref, cells_ref, hot_ref, wide_ref, cells, sem):
    copy = pltpu.make_async_copy(cells_ref, cells, sem)
    copy.start()
    number, nodes, _ = cells_ref.shape
    extent = hot_ref.shape[0]
    for c in range(number):
        index = index_ref[c : c + 1, :] - place[OFFSET]
        hot = lax.broadcasted_iota(jnp.int32, (extent, nodes), 0) == index
        hot_ref[:, c * nodes : (c + 1) * nodes] = hot.astype(BF16)
    copy.wait()
    for c in range(number):
        here = slice(c * nodes, (c + 1) * nodes)
        wide_ref[:, here] = mm(hot_ref[:, here], cells[c]).astype(BF16)


def first_zone_body(place, states_ref, halo_a_ref, halo_b_ref, potential_ref, hot_ref, wide_ref,
                    inner_ref, zone_ref, shift_inner_ref, shift_zone_ref, picked_ref, sums_ref, give_a_ref, give_b_ref):
    count, owned = states_ref.shape
    rim = halo_a_ref.shape[1]
    width, extent = 2 * rim, owned + 2 * rim
    low, high = sort_out(place, halo_a_ref[...], halo_b_ref[...])
    zone_ref[:, :rim] = low[:count].astype(BF16)
    zone_ref[:, rim:width] = states_ref[:, :rim]
    zone_ref[:, width : width + rim] = states_ref[:, owned - rim :]
    zone_ref[:, width + rim :] = high[:count].astype(BF16)
    inner_ref[...] = states_ref[:, rim : owned - rim]
    row = potential_ref[...] - spectrum_center
    shift_inner_ref[...] = row[:, rim : owned - rim]
    shift_zone_ref[:, rim:width] = row[:, :rim]
    shift_zone_ref[:, width : width + rim] = row[:, owned - rim :]
    for got, at in ((low, 0), (high, width + rim)):
        part = got[count : count + 8]
        shift_zone_ref[:, at : at + rim] = (part[0:1] + part[1:2] + part[2:3]) - spectrum_center
    picked = (
        mm(inner_ref[...], hot_ref[width : extent - width, :])
        + mm(zone_ref[:, :width], hot_ref[:width, :])
        + mm(zone_ref[:, width:], hot_ref[extent - width :, :])
    ).astype(BF16)
    picked_ref[...] = picked
    low, high = mm_nt(picked, wide_ref[:width, :]), mm_nt(picked, wide_ref[extent - width :, :])
    sums_ref[:, :width] = low
    sums_ref[:, width:] = high
    hand_out(place, low, high, give_a_ref, give_b_ref)


def first_inner_body(place, inner_ref, picked_ref, shift_inner_ref, hot_ref, wide_ref,
                     next_ref, matrix_ref, diagonal_ref, part_ref):
    extent = matrix_ref.shape[0]
    width = (extent - inner_ref.shape[1]) // 2
    inside = slice(width, extent - width)
    value = mm_nt(picked_ref[...], wide_ref[inside, :]) + shift_inner_ref[...] * inner_ref[...].astype(F32)
    following = (value * (1.0 / spectrum_half)).astype(BF16)
    next_ref[...] = following
    step = 256
    for start in range(0, extent, step):
        rows = mm_nt(wide_ref[start : start + step, :], hot_ref[...])
        same = lax.broadcasted_iota(jnp.int32, (step, step), 0) == lax.broadcasted_iota(
            jnp.int32, (step, step), 1
        )
        square = rows[:, start : start + step]
        diagonal_ref[:, start : start + step] = jnp.sum(
            jnp.where(same, square, 0.0), axis=0, keepdims=True
        )
        matrix_ref[start : start + step, :] = rows.astype(BF16)
        matrix_ref[start : start + step, start : start + step] = jnp.where(same, 0.0, square).astype(BF16)
    part_ref[...] = mm(following, matrix_ref[inside, :])


def close_zones(place, sums_ref, got_a_ref, got_b_ref, shift_zone_ref, mid_ref, old_ref, scale, zone_ref):
    width = got_a_ref.shape[1]
    low, high = sort_out(place, got_a_ref[...], got_b_ref[...])
    for got, here in ((low, slice(0, width)), (high, slice(width, 2 * width))):
        value = sums_ref[:, here] + got + shift_zone_ref[:, here] * mid_ref[:, here].astype(F32)
        value = value * scale
        if old_ref is not None:
            value = value - old_ref[:, here].astype(F32)
        zone_ref[:, here] = value.astype(BF16)


def zone_sums(zone_ref, part_ref, matrix_ref, diagonal_ref):
    extent = matrix_ref.shape[0]
    width = zone_ref.shape[1] // 2
    low, high = zone_ref[:, :width], zone_ref[:, width:]
    out = []
    for here, own in ((slice(0, width), low), (slice(extent - width, extent), high)):
        out.append(
            part_ref[:, here]
            + mm(low, matrix_ref[:width, here])
            + mm(high, matrix_ref[extent - width :, here])
            + diagonal_ref[:, here] * own.astype(F32)
        )
    return out


def zone_body(has_old, scale, place, sums_ref, got_a_ref, got_b_ref, shift_zone_ref, mid_ref, *rest):
    old_ref, rest = (rest[0], rest[1:]) if has_old else (None, rest)
    part_ref, matrix_ref, diagonal_ref, zone_ref, next_sums_ref, give_a_ref, give_b_ref = rest
    close_zones(place, sums_ref, got_a_ref, got_b_ref, shift_zone_ref, mid_ref, old_ref, scale, zone_ref)
    low, high = zone_sums(zone_ref, part_ref, matrix_ref, diagonal_ref)
    width = low.shape[1]
    next_sums_ref[:, :width] = low
    next_sums_ref[:, width:] = high
    hand_out(place, low, high, give_a_ref, give_b_ref)


def inner_sums(zone_ref, inner_ref, part_ref, matrix_ref, diagonal_ref):
    extent = matrix_ref.shape[0]
    width = zone_ref.shape[1] // 2
    inside = slice(width, extent - width)
    return (
        part_ref[:, inside]
        + mm(zone_ref[:, :width], matrix_ref[:width, inside])
        + mm(zone_ref[:, width:], matrix_ref[extent - width :, inside])
        + diagonal_ref[:, inside] * inner_ref[...].astype(F32)
    )


def inner_body(place, zone_ref, inner_ref, old_ref, part_ref, shift_inner_ref, matrix_ref, diagonal_ref,
               next_ref, *next_part):
    sums = inner_sums(zone_ref, inner_ref, part_ref, matrix_ref, diagonal_ref)
    value = (sums + shift_inner_ref[...] * inner_ref[...].astype(F32)) * (2.0 / spectrum_half)
    following = (value - old_ref[...].astype(F32)).astype(BF16)
    next_ref[...] = following
    if next_part:
        part_body(place, next_ref, matrix_ref, *next_part)


def part_body(place, inner_ref, matrix_ref, part_ref):
    extent = matrix_ref.shape[0]
    width = (extent - inner_ref.shape[1]) // 2
    part_ref[...] = mm(inner_ref[...], matrix_ref[width : extent - width, :])


def energy_zone_body(place, sums_ref, got_a_ref, got_b_ref, shift_zone_ref, mid_ref, old_ref,
                     part_ref, matrix_ref, diagonal_ref, zone_ref, rim_ref, energy_ref, give_a_ref, give_b_ref):
    close_zones(place, sums_ref, got_a_ref, got_b_ref, shift_zone_ref, mid_ref, old_ref,
                2.0 / spectrum_half, zone_ref)
    width = got_a_ref.shape[1]
    rim = width // 2
    rim_ref[...] = zone_ref[:, rim : width + rim]
    low, high = zone_sums(zone_ref, part_ref, matrix_ref, diagonal_ref)
    own = shift_zone_ref[:, rim : width + rim] + spectrum_center
    own = own * rim_ref[...].astype(F32)
    energy_ref[:, :rim] = low[:, rim:] + own[:, :rim]
    energy_ref[:, rim:] = high[:, :rim] + own[:, rim:]
    hand_out(place, low[:, :rim], high[:, rim:], give_a_ref, give_b_ref)


def energy_inner_body(place, zone_ref, inner_ref, part_ref, shift_inner_ref, matrix_ref, diagonal_ref,
                      energy_ref, filtered_ref):
    sums = inner_sums(zone_ref, inner_ref, part_ref, matrix_ref, diagonal_ref)
    own = (shift_inner_ref[...] + spectrum_center) * inner_ref[...].astype(F32)
    energy_ref[...] = (sums + own).astype(BF16)
    width = zone_ref.shape[1] // 2
    rim = width // 2
    owned = filtered_ref.shape[1]
    filtered_ref[:, :rim] = zone_ref[:, rim:width]
    filtered_ref[:, rim : owned - rim] = inner_ref[...]
    filtered_ref[:, owned - rim :] = zone_ref[:, width : width + rim]


def project_body(scale, place, energy_rim_ref, got_a_ref, got_b_ref, energy_inner_ref, *refs):
    *blocks, out_ref, give_ref, stack_ref, pair_ref = refs
    count, inside = energy_inner_ref.shape
    rim = got_a_ref.shape[1]
    low, high = sort_out(place, got_a_ref[...], got_b_ref[...])
    group = place[GROUP]
    groups = len(blocks) // 2
    for distance in range(groups):
        inner_ref, rim_ref = blocks[2 * distance : 2 * distance + 2]
        at = pl.multiple_of((group ^ distance) * count, count)
        stack_ref[pl.ds(at, count), :inside] = inner_ref[...]
        stack_ref[pl.ds(at, count), inside:] = rim_ref[...]
    pair_ref[:count, :inside] = blocks[0][...]
    pair_ref[:count, inside:] = blocks[1][...]
    pair_ref[count:, :inside] = energy_inner_ref[...]
    pair_ref[count:, inside : inside + rim] = (energy_rim_ref[:, :rim] + low).astype(BF16)
    pair_ref[count:, inside + rim :] = (energy_rim_ref[:, rim:] + high).astype(BF16)
    both = mm_nt(stack_ref[...], pair_ref[...]) * scale
    chips, _, columns, _ = out_ref.shape
    odd = place[ODD] == 1
    for chip in range(chips):
        parts = [both[(2 * chip + core) * columns : (2 * chip + core + 1) * columns] for core in range(2)]
        for core in range(2):
            out_ref[chip, core] = parts[core].astype(BF16)
        give_ref[chip] = jnp.where(odd, parts[0], parts[1]).astype(BF16)


def halve_body(place, mine_ref, got_ref, *pieces):
    for distance, piece_ref in enumerate(pieces):
        chip = place[CHIP] ^ distance
        total = mine_ref[chip, place[ODD]].astype(F32) + got_ref[chip].astype(F32)
        piece_ref[...] = total.astype(BF16)


def final_body(count, place, *refs):
    parts, (first_ref, second_ref) = refs[:-2], refs[-2:]
    total = parts[0][...].astype(F32)
    for part in parts[1:]:
        total = total + part[...].astype(F32)
    first_ref[...] = total[:, :count]
    second_ref[...] = total[:, count:]


def swap(block, n_state, n_space, lead):
    route = []
    for s in range(n_state):
        for i in range(n_space):
            j = i + 1 if (i - lead) % 2 == 0 else i - 1
            if 0 <= j < n_space:
                route.append((s * n_space + i, s * n_space + j))
            elif (s ^ 1) < n_state:
                route.append((s * n_space + i, (s ^ 1) * n_space + i))
    return lax.ppermute(block, ("state", "space"), route)


def exchange(give_a, give_b, n_state, n_space):
    got_a = swap(give_a, n_state, n_space, 0)
    got_b = swap(give_b, n_state, n_space, 1)
    return got_a, got_b


def across(block, axis, distance):
    return lax.ppermute(block, axis, [(i, i ^ distance) for i in range(lax.axis_size(axis))])


def program(states_in, cell_matrices, connectivity, potential):
    count, owned = states_in.shape
    cells, nodes, _ = cell_matrices.shape
    rim = nodes // 4
    extent, inside = owned + 2 * rim, owned - 2 * rim
    n_state, n_space = lax.axis_size("state"), lax.axis_size("space")
    me = lax.axis_index("space")
    place = jnp.stack(
        [
            me & 1,
            (me == 0).astype(jnp.int32),
            (me == n_space - 1).astype(jnp.int32),
            lax.axis_index("state"),
            me >> 1,
            me * owned - rim,
        ]
    ).astype(jnp.int32)
    row = potential.reshape(1, owned)
    work = 2 * count * extent * extent
    inner, part = SHAPE((count, inside), BF16), SHAPE((count, extent), F32)
    zone, sums_of = SHAPE((count, 4 * rim), BF16), SHAPE((count, 4 * rim), F32)
    give, give_rim = SHAPE((count, 2 * rim), BF16), SHAPE((count, rim), BF16)

    halo = SHAPE((count + 16, rim), BF16)
    *gave, local = call(
        halo_body, (halo, halo, SHAPE(connectivity.shape, connectivity.dtype)),
        (place, states_in, row, connectivity), 0, raw=(1, 2, 3),
        scratch=[
            pltpu.VMEM((count, rim), BF16), pltpu.VMEM((count, rim), BF16),
            pltpu.VMEM((1, owned), F32), pltpu.SemaphoreType.DMA((4,)),
        ],
    )
    got = exchange(*gave, n_state, n_space)
    table = SHAPE((extent, cells * nodes), BF16)
    hot, wide = call(
        spread_body, (table, table), (place, local, cell_matrices),
        2 * extent * cells * nodes * nodes, raw=(2,),
        scratch=[pltpu.VMEM(cell_matrices.shape, BF16), pltpu.SemaphoreType.DMA],
    )
    inner_0, zone_0, shift_inner, shift_zone, picked, sums, *gave = call(
        first_zone_body,
        (inner, zone, SHAPE((1, inside), F32), SHAPE((1, 4 * rim), F32),
         SHAPE((count, cells * nodes), BF16), sums_of, give, give),
        (place, states_in, *got, row, hot, wide), work,
    )
    got = exchange(*gave, n_state, n_space)
    inner_1, matrix, diagonal, partial = call(
        first_inner_body,
        (inner, SHAPE((extent, extent), BF16), SHAPE((1, extent), F32), part),
        (place, inner_0, picked, shift_inner, hot, wide), 2 * extent * extent * cells * nodes,
    )
    inners, zones = [inner_0, inner_1], [zone_0]
    for k in range(1, DEGREE):
        older = zones[-2:-1]
        scale = (2.0 if older else 1.0) / spectrum_half
        zone_k, sums, *gave = call(
            functools.partial(zone_body, bool(older), scale),
            (zone, sums_of, give, give),
            (place, sums, *got, shift_zone, zones[-1], *older, partial, matrix, diagonal), work // 6,
        )
        zones.append(zone_k)
        got = exchange(*gave, n_state, n_space)
        ins = (place, zone_k, inners[-1], inners[-2], partial, shift_inner, matrix, diagonal)
        if k < DEGREE - 1:
            inner_k, partial = call(inner_body, (inner, part), ins, work)
        else:
            inner_k = call(inner_body, inner, ins, work // 4)
            partial = call(part_body, part, (place, inner_k, matrix), work // 2)
        inners.append(inner_k)
    distances = range(1, n_state)
    blocks = [inner_k] + [across(inner_k, "state", d) for d in distances]
    zone_k, rims, energy_rim, *gave = call(
        energy_zone_body,
        (zone, give, SHAPE((count, 2 * rim), F32), give_rim, give_rim),
        (place, sums, *got, shift_zone, zones[-1], zones[-2], partial, matrix, diagonal), work // 6,
    )
    rim_blocks = [rims] + [across(rims, "state", d) for d in distances]
    got = exchange(*gave, n_state, n_space)
    energy_inner, filtered = call(
        energy_inner_body, (inner, SHAPE((count, owned), BF16)),
        (place, zone_k, inner_k, partial, shift_inner, matrix, diagonal), work // 4,
    )
    total_states = count * n_state
    columns = total_states // n_space
    chips = n_space // 2
    mine, give_half = call(
        functools.partial(project_body, 1.0 / (owned * n_space)),
        (SHAPE((chips, 2, columns, 2 * count), BF16), SHAPE((chips, columns, 2 * count), BF16)),
        (place, energy_rim, *got, energy_inner, *(b for pair in zip(blocks, rim_blocks) for b in pair)),
        4 * total_states * count * owned,
        scratch=[pltpu.VMEM((total_states, owned), BF16), pltpu.VMEM((2 * count, owned), BF16)],
    )
    got_half = swap(give_half, n_state, n_space, 0)
    piece = SHAPE((columns, 2 * count), BF16)
    pieces = call(halve_body, (piece,) * chips, (place, mine, got_half), 0)
    pieces = [pieces[0]] + [across(p, "space", 2 * d) for d, p in enumerate(pieces) if d]
    turned = SHAPE((columns, count), F32)
    intersection, projected = call(
        functools.partial(final_body, count), (turned, turned), (place, *pieces), 0
    )
    return filtered, intersection.T, projected.T


def solution(mesh):
    return jax.shard_map(
        program,
        mesh=mesh,
        in_specs=(P("state", "space"), P("space", None, None), P("space", None), P("space")),
        out_specs=(P("state", "space"), P("state", "space"), P("state", "space")),
        check_vma=False,
    )
```

```python
import functools

import jax
import jax.numpy as jnp
from jax import lax
from jax.experimental import pallas as pl
from jax.experimental.pallas import tpu as pltpu
from jax.sharding import PartitionSpec as P


DEGREE = 4

spectrum_center = 3.0
spectrum_half = 3.5

BF16 = jnp.bfloat16
F32 = jnp.float32
SHAPE = jax.ShapeDtypeStruct


def call(body, outs, ins, flops, scratch=(), raw=()):
    where = [
        pl.BlockSpec(memory_space=pltpu.HBM if i in raw else pltpu.VMEM) for i in range(len(ins))
    ]
    ins = [pltpu.with_memory_space_constraint(x, pltpu.HBM) if i in raw else x for i, x in enumerate(ins)]
    return pl.pallas_call(
        body,
        out_shape=outs,
        in_specs=where,
        out_specs=jax.tree.map(lambda _: pl.BlockSpec(memory_space=pltpu.VMEM), outs),
        scratch_shapes=list(scratch),
        compiler_params=pltpu.CompilerParams(vmem_limit_bytes=24 << 20),
        cost_estimate=pl.CostEstimate(flops=flops, bytes_accessed=4 << 20, transcendentals=0),
    )(*ins)


def mm(a, b):
    return jnp.dot(a, b, preferred_element_type=F32)


def mm_nt(a, b):
    return lax.dot_general(a, b, (((1,), (1,)), ((), ())), preferred_element_type=F32)


def is_odd():
    return (lax.axis_index("space") & 1) == 1


def sort_out(got_a, got_b):
    me, odd = lax.axis_index("space"), is_odd()
    got_a, got_b = got_a.astype(F32), got_b.astype(F32)
    low = jnp.where(me == 0, 0.0, jnp.where(odd, got_a, got_b))
    high = jnp.where(me == lax.axis_size("space") - 1, 0.0, jnp.where(odd, got_b, got_a))
    return low, high


def hand_out(low, high, give_a_ref, give_b_ref):
    odd = is_odd()
    give_a_ref[...] = jnp.where(odd, low, high).astype(give_a_ref.dtype)
    give_b_ref[...] = jnp.where(odd, high, low).astype(give_b_ref.dtype)


def halo_body(states_ref, potential_ref, index_ref,
              give_a_ref, give_b_ref, local_ref, low_ref, high_ref, row_ref, sem):
    count, owned = states_ref.shape
    rim = low_ref.shape[1]
    copies = [
        pltpu.make_async_copy(states_ref.at[:, pl.ds(0, rim)], low_ref, sem.at[0]),
        pltpu.make_async_copy(states_ref.at[:, pl.ds(owned - rim, rim)], high_ref, sem.at[1]),
        pltpu.make_async_copy(potential_ref, row_ref, sem.at[2]),
        pltpu.make_async_copy(index_ref, local_ref, sem.at[3]),
    ]
    for copy in copies:
        copy.start()
    for copy in copies:
        copy.wait()
    odd = is_odd()
    low, high = low_ref[...].astype(F32), high_ref[...].astype(F32)
    give_a_ref[:count, :] = jnp.where(odd, low, high).astype(BF16)
    give_b_ref[:count, :] = jnp.where(odd, high, low).astype(BF16)
    for take, give_ref in ((odd, give_a_ref), (jnp.logical_not(odd), give_b_ref)):
        row = jnp.where(take, row_ref[:, :rim], row_ref[:, owned - rim :])
        row = jnp.broadcast_to(row, (16, rim))
        at = lax.broadcasted_iota(jnp.int32, row.shape, 0)
        first = row.astype(BF16).astype(F32)
        second = (row - first).astype(BF16).astype(F32)
        third = (row - first) - second
        give_ref[count:, :] = jnp.where(
            at == 0, first, jnp.where(at == 1, second, jnp.where(at == 2, third, 0.0))
        ).astype(BF16)


def spread_body(index_ref, cells_ref, hot_ref, wide_ref, cells, sem):
    copy = pltpu.make_async_copy(cells_ref, cells, sem)
    copy.start()
    number, nodes, _ = cells_ref.shape
    extent = hot_ref.shape[0]
    rim = nodes // 4
    offset = lax.axis_index("space") * (extent - 2 * rim) - rim
    for c in range(number):
        index = index_ref[c : c + 1, :] - offset
        hot = lax.broadcasted_iota(jnp.int32, (extent, nodes), 0) == index
        hot_ref[:, c * nodes : (c + 1) * nodes] = hot.astype(BF16)
    copy.wait()
    for c in range(number):
        here = slice(c * nodes, (c + 1) * nodes)
        wide_ref[:, here] = mm(hot_ref[:, here], cells[c]).astype(BF16)


def first_zone_body(states_ref, halo_a_ref, halo_b_ref, potential_ref, hot_ref, wide_ref,
                    inner_ref, zone_ref, shift_inner_ref, shift_zone_ref, picked_ref, sums_ref, give_a_ref, give_b_ref):
    count, owned = states_ref.shape
    rim = halo_a_ref.shape[1]
    width, extent = 2 * rim, owned + 2 * rim
    low, high = sort_out(halo_a_ref[...], halo_b_ref[...])
    zone_ref[:, :rim] = low[:count].astype(BF16)
    zone_ref[:, rim:width] = states_ref[:, :rim]
    zone_ref[:, width : width + rim] = states_ref[:, owned - rim :]
    zone_ref[:, width + rim :] = high[:count].astype(BF16)
    inner_ref[...] = states_ref[:, rim : owned - rim]
    row = potential_ref[...] - spectrum_center
    shift_inner_ref[...] = row[:, rim : owned - rim]
    shift_zone_ref[:, rim:width] = row[:, :rim]
    shift_zone_ref[:, width : width + rim] = row[:, owned - rim :]
    for got, at in ((low, 0), (high, width + rim)):
        part = got[count : count + 8]
        shift_zone_ref[:, at : at + rim] = (part[0:1] + part[1:2] + part[2:3]) - spectrum_center
    picked = (
        mm(inner_ref[...], hot_ref[width : extent - width, :])
        + mm(zone_ref[:, :width], hot_ref[:width, :])
        + mm(zone_ref[:, width:], hot_ref[extent - width :, :])
    ).astype(BF16)
    picked_ref[...] = picked
    low, high = mm_nt(picked, wide_ref[:width, :]), mm_nt(picked, wide_ref[extent - width :, :])
    sums_ref[:, :width] = low
    sums_ref[:, width:] = high
    hand_out(low, high, give_a_ref, give_b_ref)


def take_diagonal(rows, start, matrix_ref, diagonal_ref, at):
    size = rows.shape[0]
    same = lax.broadcasted_iota(jnp.int32, (size, size), 0) == lax.broadcasted_iota(
        jnp.int32, (size, size), 1
    )
    square = rows[:, at : at + size]
    diagonal_ref[:, at : at + size] = jnp.sum(jnp.where(same, square, 0.0), axis=0, keepdims=True)
    matrix_ref[start : start + size, :] = rows.astype(BF16)
    matrix_ref[start : start + size, at : at + size] = jnp.where(same, 0.0, square).astype(BF16)


def first_inner_body(inner_ref, picked_ref, shift_inner_ref, hot_ref, wide_ref,
                     next_ref, border_ref, diagonal_ref, part_ref, columns_ref):
    extent = border_ref.shape[0]
    width = border_ref.shape[1] // 2
    inside = slice(width, extent - width)
    value = mm_nt(picked_ref[...], wide_ref[inside, :]) + shift_inner_ref[...] * inner_ref[...].astype(F32)
    following = (value * (1.0 / spectrum_half)).astype(BF16)
    next_ref[...] = following
    columns_ref[:width, :] = hot_ref[:width, :]
    columns_ref[width:, :] = hot_ref[extent - width :, :]
    border_ref[inside, :] = mm_nt(wide_ref[inside, :], columns_ref[...]).astype(BF16)
    for start, at in ((0, 0), (extent - width, width)):
        rows = mm_nt(wide_ref[start : start + width, :], columns_ref[...])
        take_diagonal(rows, start, border_ref, diagonal_ref, at)
    part_ref[...] = mm(following, border_ref[inside, :])


def close_zones(sums_ref, got_a_ref, got_b_ref, shift_zone_ref, mid_ref, old_ref, scale, zone_ref):
    width = got_a_ref.shape[1]
    low, high = sort_out(got_a_ref[...], got_b_ref[...])
    for got, here in ((low, slice(0, width)), (high, slice(width, 2 * width))):
        value = sums_ref[:, here] + got + shift_zone_ref[:, here] * mid_ref[:, here].astype(F32)
        value = value * scale
        if old_ref is not None:
            value = value - old_ref[:, here].astype(F32)
        zone_ref[:, here] = value.astype(BF16)


def zone_sums(zone_ref, part_ref, border_ref, border_diagonal_ref):
    extent = border_ref.shape[0]
    width = zone_ref.shape[1] // 2
    sums = (
        part_ref[...]
        + mm(zone_ref[:, :width], border_ref[:width, :])
        + mm(zone_ref[:, width:], border_ref[extent - width :, :])
        + border_diagonal_ref[...] * zone_ref[...].astype(F32)
    )
    return sums[:, :width], sums[:, width:]


def zone_body(has_old, scale, sums_ref, got_a_ref, got_b_ref, shift_zone_ref, mid_ref, *rest):
    old_ref, rest = (rest[0], rest[1:]) if has_old else (None, rest)
    part_ref, border_ref, border_diagonal_ref, zone_ref, next_sums_ref, give_a_ref, give_b_ref = rest
    close_zones(sums_ref, got_a_ref, got_b_ref, shift_zone_ref, mid_ref, old_ref, scale, zone_ref)
    low, high = zone_sums(zone_ref, part_ref, border_ref, border_diagonal_ref)
    width = low.shape[1]
    next_sums_ref[:, :width] = low
    next_sums_ref[:, width:] = high
    hand_out(low, high, give_a_ref, give_b_ref)


def inner_sums(zone_ref, inner_ref, border_ref, square_ref, diagonal_ref):
    width = zone_ref.shape[1] // 2
    inside = slice(width, width + square_ref.shape[0])
    return (
        mm_nt(zone_ref[...], border_ref[inside, :])
        + mm(inner_ref[...], square_ref[...])
        + diagonal_ref[...] * inner_ref[...].astype(F32)
    )


def inner_body(zone_ref, inner_ref, old_ref, shift_inner_ref, border_ref, square_ref, diagonal_ref, next_ref, part_ref):
    sums = inner_sums(zone_ref, inner_ref, border_ref, square_ref, diagonal_ref)
    value = (sums + shift_inner_ref[...] * inner_ref[...].astype(F32)) * (2.0 / spectrum_half)
    next_ref[...] = (value - old_ref[...].astype(F32)).astype(BF16)
    width = zone_ref.shape[1] // 2
    part_ref[...] = mm(next_ref[...], border_ref[width : width + next_ref.shape[1], :])


def square_body(zone_ref, inner_ref, old_ref, shift_inner_ref, border_ref, hot_ref, wide_ref,
                square_ref, diagonal_ref, next_ref, part_ref):
    size = square_ref.shape[0]
    width = (hot_ref.shape[0] - size) // 2
    for start in range(0, size, 256):
        rows = mm_nt(wide_ref[width + start : width + start + 256, :], hot_ref[width : width + size, :])
        take_diagonal(rows, start, square_ref, diagonal_ref, start)
    inner_body(zone_ref, inner_ref, old_ref, shift_inner_ref, border_ref, square_ref, diagonal_ref, next_ref, part_ref)


def energy_zone_body(sums_ref, got_a_ref, got_b_ref, shift_zone_ref, mid_ref, old_ref,
                     part_ref, border_ref, border_diagonal_ref, zone_ref, rim_ref, energy_ref, give_a_ref, give_b_ref):
    close_zones(sums_ref, got_a_ref, got_b_ref, shift_zone_ref, mid_ref, old_ref,
                2.0 / spectrum_half, zone_ref)
    width = got_a_ref.shape[1]
    rim = width // 2
    rim_ref[...] = zone_ref[:, rim : width + rim]
    low, high = zone_sums(zone_ref, part_ref, border_ref, border_diagonal_ref)
    own = shift_zone_ref[:, rim : width + rim] + spectrum_center
    own = own * rim_ref[...].astype(F32)
    energy_ref[:, :rim] = low[:, rim:] + own[:, :rim]
    energy_ref[:, rim:] = high[:, :rim] + own[:, rim:]
    hand_out(low[:, :rim], high[:, rim:], give_a_ref, give_b_ref)


def energy_inner_body(zone_ref, inner_ref, shift_inner_ref, border_ref, square_ref, diagonal_ref,
                      energy_ref, filtered_ref):
    sums = inner_sums(zone_ref, inner_ref, border_ref, square_ref, diagonal_ref)
    own = (shift_inner_ref[...] + spectrum_center) * inner_ref[...].astype(F32)
    energy_ref[...] = (sums + own).astype(BF16)
    width = zone_ref.shape[1] // 2
    rim = width // 2
    owned = filtered_ref.shape[1]
    filtered_ref[:, :rim] = zone_ref[:, rim:width]
    filtered_ref[:, rim : owned - rim] = inner_ref[...]
    filtered_ref[:, owned - rim :] = zone_ref[:, width : width + rim]


def project_body(scale, energy_rim_ref, got_a_ref, got_b_ref, energy_inner_ref, *refs):
    *blocks, out_ref, give_ref, stack_ref, pair_ref = refs
    count, inside = energy_inner_ref.shape
    rim = got_a_ref.shape[1]
    low, high = sort_out(got_a_ref[...], got_b_ref[...])
    group = lax.axis_index("state")
    groups = len(blocks) // 2
    for distance in range(groups):
        inner_ref, rim_ref = blocks[2 * distance : 2 * distance + 2]
        at = pl.multiple_of((group ^ distance) * count, count)
        stack_ref[pl.ds(at, count), :inside] = inner_ref[...]
        stack_ref[pl.ds(at, count), inside:] = rim_ref[...]
    pair_ref[:count, :inside] = blocks[0][...]
    pair_ref[:count, inside:] = blocks[1][...]
    pair_ref[count:, :inside] = energy_inner_ref[...]
    pair_ref[count:, inside : inside + rim] = (energy_rim_ref[:, :rim] + low).astype(BF16)
    pair_ref[count:, inside + rim :] = (energy_rim_ref[:, rim:] + high).astype(BF16)
    both = mm_nt(stack_ref[...], pair_ref[...]) * scale
    chips, _, columns, _ = out_ref.shape
    odd = is_odd()
    for chip in range(chips):
        parts = [both[(2 * chip + core) * columns : (2 * chip + core + 1) * columns] for core in range(2)]
        for core in range(2):
            out_ref[chip, core] = parts[core].astype(BF16)
        give_ref[chip] = jnp.where(odd, parts[0], parts[1]).astype(BF16)


def halve_body(mine_ref, got_ref, *pieces):
    for distance, piece_ref in enumerate(pieces):
        chip = (lax.axis_index("space") >> 1) ^ distance
        total = mine_ref[chip, lax.axis_index("space") & 1].astype(F32) + got_ref[chip].astype(F32)
        piece_ref[...] = total.astype(BF16)


def final_body(count, *refs):
    parts, (first_ref, second_ref) = refs[:-2], refs[-2:]
    total = parts[0][...].astype(F32)
    for part in parts[1:]:
        total = total + part[...].astype(F32)
    first_ref[...] = total[:, :count]
    second_ref[...] = total[:, count:]


def swap(block, n_state, n_space, lead):
    route = []
    for s in range(n_state):
        for i in range(n_space):
            j = i + 1 if (i - lead) % 2 == 0 else i - 1
            if 0 <= j < n_space:
                route.append((s * n_space + i, s * n_space + j))
            elif (s ^ 1) < n_state:
                route.append((s * n_space + i, (s ^ 1) * n_space + i))
    return lax.ppermute(block, ("state", "space"), route)


def exchange(give_a, give_b, n_state, n_space):
    got_a = swap(give_a, n_state, n_space, 0)
    got_b = swap(give_b, n_state, n_space, 1)
    return got_a, got_b


def across(block, axis, distance):
    return lax.ppermute(block, axis, [(i, i ^ distance) for i in range(lax.axis_size(axis))])


def program(states_in, cell_matrices, connectivity, potential):
    count, owned = states_in.shape
    cells, nodes, _ = cell_matrices.shape
    rim = nodes // 4
    extent, inside = owned + 2 * rim, owned - 2 * rim
    n_state, n_space = lax.axis_size("state"), lax.axis_size("space")
    row = potential.reshape(1, owned)
    work = 2 * count * extent * extent
    inner = SHAPE((count, inside), BF16)
    zone, sums_of = SHAPE((count, 4 * rim), BF16), SHAPE((count, 4 * rim), F32)
    give, give_rim = SHAPE((count, 2 * rim), BF16), SHAPE((count, rim), BF16)

    halo = SHAPE((count + 16, rim), BF16)
    *gave, local = call(
        halo_body, (halo, halo, SHAPE(connectivity.shape, connectivity.dtype)),
        (states_in, row, connectivity), 0, raw=(0, 1, 2),
        scratch=[
            pltpu.VMEM((count, rim), BF16), pltpu.VMEM((count, rim), BF16),
            pltpu.VMEM((1, owned), F32), pltpu.SemaphoreType.DMA((4,)),
        ],
    )
    got = exchange(*gave, n_state, n_space)
    table = SHAPE((extent, cells * nodes), BF16)
    hot, wide = call(
        spread_body, (table, table), (local, cell_matrices),
        2 * extent * cells * nodes * nodes, raw=(1,),
        scratch=[pltpu.VMEM(cell_matrices.shape, BF16), pltpu.SemaphoreType.DMA],
    )
    inner_0, zone_0, shift_inner, shift_zone, picked, sums, *gave = call(
        first_zone_body,
        (inner, zone, SHAPE((1, inside), F32), SHAPE((1, 4 * rim), F32),
         SHAPE((count, cells * nodes), BF16), sums_of, give, give),
        (states_in, *got, row, hot, wide), work,
    )
    got = exchange(*gave, n_state, n_space)
    border_line, line = SHAPE((1, 4 * rim), F32), SHAPE((1, inside), F32)
    inner_1, border, border_diagonal, partial = call(
        first_inner_body,
        (inner, SHAPE((extent, 4 * rim), BF16), border_line, sums_of),
        (inner_0, picked, shift_inner, hot, wide), 8 * extent * rim * cells * nodes,
        scratch=[pltpu.VMEM((4 * rim, cells * nodes), BF16)],
    )
    inners, zones = [inner_0, inner_1], [zone_0]
    for k in range(1, DEGREE):
        older = zones[-2:-1]
        scale = (2.0 if older else 1.0) / spectrum_half
        zone_k, sums, *gave = call(
            functools.partial(zone_body, bool(older), scale),
            (zone, sums_of, give, give),
            (sums, *got, shift_zone, zones[-1], *older, partial, border, border_diagonal), work // 6,
        )
        zones.append(zone_k)
        got = exchange(*gave, n_state, n_space)
        ins = (zone_k, inners[-1], inners[-2], shift_inner, border)
        if k == 1:
            square, diagonal, inner_k, partial = call(
                square_body, (SHAPE((inside, inside), BF16), line, inner, sums_of), (*ins, hot, wide),
                2 * inside * inside * cells * nodes,
            )
        else:
            inner_k, partial = call(inner_body, (inner, sums_of), (*ins, square, diagonal), work)
        inners.append(inner_k)
    distances = range(1, n_state)
    blocks = [inner_k] + [across(inner_k, "state", d) for d in distances]
    zone_k, rims, energy_rim, *gave = call(
        energy_zone_body,
        (zone, give, SHAPE((count, 2 * rim), F32), give_rim, give_rim),
        (sums, *got, shift_zone, zones[-1], zones[-2], partial, border, border_diagonal), work // 6,
    )
    rim_blocks = [rims] + [across(rims, "state", d) for d in distances]
    got = exchange(*gave, n_state, n_space)
    energy_inner, filtered = call(
        energy_inner_body, (inner, SHAPE((count, owned), BF16)),
        (zone_k, inner_k, shift_inner, border, square, diagonal), work // 4,
    )
    total_states = count * n_state
    columns = total_states // n_space
    chips = n_space // 2
    mine, give_half = call(
        functools.partial(project_body, 1.0 / (owned * n_space)),
        (SHAPE((chips, 2, columns, 2 * count), BF16), SHAPE((chips, columns, 2 * count), BF16)),
        (energy_rim, *got, energy_inner, *(b for pair in zip(blocks, rim_blocks) for b in pair)),
        4 * total_states * count * owned,
        scratch=[pltpu.VMEM((total_states, owned), BF16), pltpu.VMEM((2 * count, owned), BF16)],
    )
    got_half = swap(give_half, n_state, n_space, 0)
    piece = SHAPE((columns, 2 * count), BF16)
    pieces = call(halve_body, (piece,) * chips, (mine, got_half), 0)
    pieces = [pieces[0]] + [across(p, "space", 2 * d) for d, p in enumerate(pieces) if d]
    turned = SHAPE((columns, count), F32)
    intersection, projected = call(
        functools.partial(final_body, count), (turned, turned), tuple(pieces), 0
    )
    return filtered, intersection.T, projected.T


def solution(mesh):
    return jax.shard_map(
        program,
        mesh=mesh,
        in_specs=(P("state", "space"), P("space", None, None), P("space", None), P("space")),
        out_specs=(P("state", "space"), P("state", "space"), P("state", "space")),
        check_vma=False,
    )
```

```python
import functools

import jax
import jax.numpy as jnp
from jax import lax
from jax.experimental import pallas as pl
from jax.experimental.pallas import tpu as pltpu
from jax.sharding import PartitionSpec as P


DEGREE = 4

spectrum_center = 3.0
spectrum_half = 3.5

BF16 = jnp.bfloat16
F32 = jnp.float32
SHAPE = jax.ShapeDtypeStruct


def call(body, outs, ins, flops, scratch=(), raw=()):
    where = [
        pl.BlockSpec(memory_space=pltpu.HBM if i in raw else pltpu.VMEM) for i in range(len(ins))
    ]
    ins = [pltpu.with_memory_space_constraint(x, pltpu.HBM) if i in raw else x for i, x in enumerate(ins)]
    return pl.pallas_call(
        body,
        out_shape=outs,
        in_specs=where,
        out_specs=jax.tree.map(lambda _: pl.BlockSpec(memory_space=pltpu.VMEM), outs),
        scratch_shapes=list(scratch),
        compiler_params=pltpu.CompilerParams(vmem_limit_bytes=24 << 20),
        cost_estimate=pl.CostEstimate(flops=flops, bytes_accessed=4 << 20, transcendentals=0),
    )(*ins)


def mm(a, b):
    return jnp.dot(a, b, preferred_element_type=F32)


def mm_nt(a, b):
    return lax.dot_general(a, b, (((1,), (1,)), ((), ())), preferred_element_type=F32)


def is_odd():
    return (lax.axis_index("space") & 1) == 1


def sort_out(got_a, got_b):
    me, odd = lax.axis_index("space"), is_odd()
    got_a, got_b = got_a.astype(F32), got_b.astype(F32)
    low = jnp.where(me == 0, 0.0, jnp.where(odd, got_a, got_b))
    high = jnp.where(me == lax.axis_size("space") - 1, 0.0, jnp.where(odd, got_b, got_a))
    return low, high


def hand_out(low, high, give_a_ref, give_b_ref):
    odd = is_odd()
    give_a_ref[...] = jnp.where(odd, low, high).astype(give_a_ref.dtype)
    give_b_ref[...] = jnp.where(odd, high, low).astype(give_b_ref.dtype)


def halo_body(states_ref, potential_ref, index_ref,
              give_a_ref, give_b_ref, local_ref, low_ref, high_ref, row_ref, sem):
    count, owned = states_ref.shape
    rim = low_ref.shape[1]
    copies = [
        pltpu.make_async_copy(states_ref.at[:, pl.ds(0, rim)], low_ref, sem.at[0]),
        pltpu.make_async_copy(states_ref.at[:, pl.ds(owned - rim, rim)], high_ref, sem.at[1]),
        pltpu.make_async_copy(potential_ref, row_ref, sem.at[2]),
        pltpu.make_async_copy(index_ref, local_ref, sem.at[3]),
    ]
    for copy in copies:
        copy.start()
    for copy in copies:
        copy.wait()
    odd = is_odd()
    low, high = low_ref[...].astype(F32), high_ref[...].astype(F32)
    give_a_ref[:count, :] = jnp.where(odd, low, high).astype(BF16)
    give_b_ref[:count, :] = jnp.where(odd, high, low).astype(BF16)
    for take, give_ref in ((odd, give_a_ref), (jnp.logical_not(odd), give_b_ref)):
        row = jnp.where(take, row_ref[:, :rim], row_ref[:, owned - rim :])
        row = jnp.broadcast_to(row, (16, rim))
        at = lax.broadcasted_iota(jnp.int32, row.shape, 0)
        first = row.astype(BF16).astype(F32)
        second = (row - first).astype(BF16).astype(F32)
        third = (row - first) - second
        give_ref[count:, :] = jnp.where(
            at == 0, first, jnp.where(at == 1, second, jnp.where(at == 2, third, 0.0))
        ).astype(BF16)


def spread_body(index_ref, cells_ref, hot_ref, wide_ref, cells, sem):
    copy = pltpu.make_async_copy(cells_ref, cells, sem)
    copy.start()
    number, nodes, _ = cells_ref.shape
    extent = hot_ref.shape[0]
    rim = nodes // 4
    offset = lax.axis_index("space") * (extent - 2 * rim) - rim
    for c in range(number):
        index = index_ref[c : c + 1, :] - offset
        hot = lax.broadcasted_iota(jnp.int32, (extent, nodes), 0) == index
        hot_ref[:, c * nodes : (c + 1) * nodes] = hot.astype(BF16)
    copy.wait()
    for c in range(number):
        here = slice(c * nodes, (c + 1) * nodes)
        wide_ref[:, here] = mm(hot_ref[:, here], cells[c]).astype(BF16)


def first_zone_body(states_ref, halo_a_ref, halo_b_ref, potential_ref, hot_ref, wide_ref,
                    inner_ref, zone_ref, shift_inner_ref, shift_zone_ref, picked_ref, sums_ref, give_a_ref, give_b_ref):
    count, owned = states_ref.shape
    rim = halo_a_ref.shape[1]
    width, extent = 2 * rim, owned + 2 * rim
    low, high = sort_out(halo_a_ref[...], halo_b_ref[...])
    zone_ref[:, :rim] = low[:count].astype(BF16)
    zone_ref[:, rim:width] = states_ref[:, :rim]
    zone_ref[:, width : width + rim] = states_ref[:, owned - rim :]
    zone_ref[:, width + rim :] = high[:count].astype(BF16)
    inner_ref[...] = states_ref[:, rim : owned - rim]
    row = potential_ref[...] - spectrum_center
    shift_inner_ref[...] = row[:, rim : owned - rim]
    shift_zone_ref[:, rim:width] = row[:, :rim]
    shift_zone_ref[:, width : width + rim] = row[:, owned - rim :]
    for got, at in ((low, 0), (high, width + rim)):
        part = got[count : count + 8]
        shift_zone_ref[:, at : at + rim] = (part[0:1] + part[1:2] + part[2:3]) - spectrum_center
    picked = (
        mm(inner_ref[...], hot_ref[width : extent - width, :])
        + mm(zone_ref[:, :width], hot_ref[:width, :])
        + mm(zone_ref[:, width:], hot_ref[extent - width :, :])
    ).astype(BF16)
    picked_ref[...] = picked
    low, high = mm_nt(picked, wide_ref[:width, :]), mm_nt(picked, wide_ref[extent - width :, :])
    sums_ref[:, :width] = low
    sums_ref[:, width:] = high
    hand_out(low, high, give_a_ref, give_b_ref)


def take_diagonal(rows, start, matrix_ref, diagonal_ref, at):
    size = rows.shape[0]
    same = lax.broadcasted_iota(jnp.int32, (size, size), 0) == lax.broadcasted_iota(
        jnp.int32, (size, size), 1
    )
    square = rows[:, at : at + size]
    diagonal_ref[:, at : at + size] = jnp.sum(jnp.where(same, square, 0.0), axis=0, keepdims=True)
    matrix_ref[start : start + size, :] = rows.astype(BF16)
    matrix_ref[start : start + size, at : at + size] = jnp.where(same, 0.0, square).astype(BF16)


def first_inner_body(inner_ref, picked_ref, shift_inner_ref, hot_ref, wide_ref,
                     next_ref, border_ref, diagonal_ref, part_ref, columns_ref):
    extent = border_ref.shape[0]
    width = border_ref.shape[1] // 2
    inside = slice(width, extent - width)
    value = mm_nt(picked_ref[...], wide_ref[inside, :]) + shift_inner_ref[...] * inner_ref[...].astype(F32)
    following = (value * (1.0 / spectrum_half)).astype(BF16)
    next_ref[...] = following
    columns_ref[:width, :] = hot_ref[:width, :]
    columns_ref[width:, :] = hot_ref[extent - width :, :]
    border_ref[inside, :] = mm_nt(wide_ref[inside, :], columns_ref[...]).astype(BF16)
    for start, at in ((0, 0), (extent - width, width)):
        rows = mm_nt(wide_ref[start : start + width, :], columns_ref[...])
        take_diagonal(rows, start, border_ref, diagonal_ref, at)
    part_ref[...] = mm(following, border_ref[inside, :])


def close_zones(sums_ref, got_a_ref, got_b_ref, shift_zone_ref, mid_ref, old_ref, scale, zone_ref):
    width = got_a_ref.shape[1]
    low, high = sort_out(got_a_ref[...], got_b_ref[...])
    for got, here in ((low, slice(0, width)), (high, slice(width, 2 * width))):
        value = sums_ref[:, here] + got + shift_zone_ref[:, here] * mid_ref[:, here].astype(F32)
        value = value * scale
        if old_ref is not None:
            value = value - old_ref[:, here].astype(F32)
        zone_ref[:, here] = value.astype(BF16)


def zone_sums(zone_ref, part_ref, border_ref, border_diagonal_ref):
    extent = border_ref.shape[0]
    width = zone_ref.shape[1] // 2
    sums = (
        part_ref[...]
        + mm(zone_ref[:, :width], border_ref[:width, :])
        + mm(zone_ref[:, width:], border_ref[extent - width :, :])
        + border_diagonal_ref[...] * zone_ref[...].astype(F32)
    )
    return sums[:, :width], sums[:, width:]


def zone_body(has_old, scale, sums_ref, got_a_ref, got_b_ref, shift_zone_ref, mid_ref, *rest):
    old_ref, rest = (rest[0], rest[1:]) if has_old else (None, rest)
    part_ref, border_ref, border_diagonal_ref, zone_ref, next_sums_ref, give_a_ref, give_b_ref = rest
    close_zones(sums_ref, got_a_ref, got_b_ref, shift_zone_ref, mid_ref, old_ref, scale, zone_ref)
    low, high = zone_sums(zone_ref, part_ref, border_ref, border_diagonal_ref)
    width = low.shape[1]
    next_sums_ref[:, :width] = low
    next_sums_ref[:, width:] = high
    hand_out(low, high, give_a_ref, give_b_ref)


def inner_sums(zone_ref, inner_ref, border_ref, square_ref, diagonal_ref):
    width = zone_ref.shape[1] // 2
    inside = slice(width, width + square_ref.shape[0])
    return (
        mm_nt(zone_ref[...], border_ref[inside, :])
        + mm(inner_ref[...], square_ref[...])
        + diagonal_ref[...] * inner_ref[...].astype(F32)
    )


def inner_body(zone_ref, inner_ref, old_ref, shift_inner_ref, border_ref, square_ref, diagonal_ref, next_ref, part_ref):
    sums = inner_sums(zone_ref, inner_ref, border_ref, square_ref, diagonal_ref)
    value = (sums + shift_inner_ref[...] * inner_ref[...].astype(F32)) * (2.0 / spectrum_half)
    next_ref[...] = (value - old_ref[...].astype(F32)).astype(BF16)
    width = zone_ref.shape[1] // 2
    part_ref[...] = mm(next_ref[...], border_ref[width : width + next_ref.shape[1], :])


def square_body(zone_ref, inner_ref, old_ref, shift_inner_ref, border_ref, hot_ref, wide_ref,
                square_ref, diagonal_ref, next_ref, part_ref):
    size = square_ref.shape[0]
    width = (hot_ref.shape[0] - size) // 2
    for start in range(0, size, 256):
        rows = mm_nt(wide_ref[width + start : width + start + 256, :], hot_ref[width : width + size, :])
        take_diagonal(rows, start, square_ref, diagonal_ref, start)
    inner_body(zone_ref, inner_ref, old_ref, shift_inner_ref, border_ref, square_ref, diagonal_ref, next_ref, part_ref)


def last_zone_body(sums_ref, got_a_ref, got_b_ref, shift_zone_ref, mid_ref, old_ref, zone_ref):
    close_zones(sums_ref, got_a_ref, got_b_ref, shift_zone_ref, mid_ref, old_ref,
                2.0 / spectrum_half, zone_ref)


def zone_energy(zone_ref, part_ref, shift_zone_ref, border_ref, border_diagonal_ref, energy_ref):
    low, high = zone_sums(zone_ref, part_ref, border_ref, border_diagonal_ref)
    width = low.shape[1]
    rim = width // 2
    own = (shift_zone_ref[:, rim : width + rim] + spectrum_center) * zone_ref[:, rim : width + rim].astype(F32)
    energy_ref[:, :rim] = low[:, :rim].astype(energy_ref.dtype)
    energy_ref[:, rim:width] = (low[:, rim:] + own[:, :rim]).astype(energy_ref.dtype)
    energy_ref[:, width : width + rim] = (high[:, :rim] + own[:, rim:]).astype(energy_ref.dtype)
    energy_ref[:, width + rim :] = high[:, rim:].astype(energy_ref.dtype)


def energy_body(zone_ref, inner_ref, part_ref, shift_inner_ref, shift_zone_ref,
                border_ref, border_diagonal_ref, square_ref, diagonal_ref, energy_ref, energy_zone_ref, filtered_ref):
    sums = inner_sums(zone_ref, inner_ref, border_ref, square_ref, diagonal_ref)
    own = (shift_inner_ref[...] + spectrum_center) * inner_ref[...].astype(F32)
    energy_ref[...] = (sums + own).astype(BF16)
    zone_energy(zone_ref, part_ref, shift_zone_ref, border_ref, border_diagonal_ref, energy_zone_ref)
    width = zone_ref.shape[1] // 2
    rim = width // 2
    owned = filtered_ref.shape[1]
    filtered_ref[:, :rim] = zone_ref[:, rim:width]
    filtered_ref[:, rim : owned - rim] = inner_ref[...]
    filtered_ref[:, owned - rim :] = zone_ref[:, width : width + rim]


def neighbour_body(inner_ref, shift_inner_ref, border_ref, square_ref, diagonal_ref, open_ref, part_ref):
    inner = inner_ref[...]
    width = border_ref.shape[1] // 2
    line = diagonal_ref[...] + (shift_inner_ref[...] + spectrum_center)
    open_ref[...] = mm(inner, square_ref[...]) + line * inner.astype(F32)
    part_ref[...] = mm(inner, border_ref[width : width + inner.shape[1], :])


def fill_pair(pair_ref, inner_ref, zone_ref):
    count, inside = inner_ref.shape
    rim = zone_ref.shape[1] // 4
    none = jnp.zeros((count, rim), BF16)
    pair_ref[:count, :inside] = inner_ref[...]
    pair_ref[:count, inside : inside + rim] = none
    pair_ref[:count, inside + rim : inside + 3 * rim] = zone_ref[:, rim : 3 * rim]
    pair_ref[:count, inside + 3 * rim :] = none


def project_body(square_of_four, scale, energy_ref, energy_zone_ref, *refs):
    if square_of_four:
        (open_ref, part_ref, shift_zone_ref, border_ref, border_diagonal_ref), refs = refs[:5], refs[5:]
        *blocks, out_ref, give_ref, stack_ref, pair_ref, other_ref, other_zone_ref = refs
    else:
        *blocks, out_ref, give_ref, stack_ref, pair_ref = refs
    count, inside = energy_ref.shape
    group = lax.axis_index("state")
    odd = is_odd()
    for place in range(len(blocks) // 2):
        stack_ref[place * count : (place + 1) * count, :inside] = blocks[2 * place][...]
        stack_ref[place * count : (place + 1) * count, inside:] = blocks[2 * place + 1][...]
    fill_pair(pair_ref, blocks[0], blocks[1])
    pair_ref[count:, :inside] = energy_ref[...]
    pair_ref[count:, inside:] = energy_zone_ref[...]
    both = mm_nt(stack_ref[...], pair_ref[...]) * scale
    found = [(place, both[place * count : (place + 1) * count]) for place in range(len(blocks) // 2)]
    if square_of_four:
        beside, beside_zone = blocks[2], blocks[3]
        width = beside_zone.shape[1] // 2
        fill_pair(other_ref, beside, beside_zone)
        rest = mm_nt(beside_zone[...], border_ref[width : width + inside, :])
        other_ref[count:, :inside] = (open_ref[...] + rest).astype(BF16)
        zone_energy(beside_zone, part_ref, shift_zone_ref, border_ref, border_diagonal_ref, other_zone_ref)
        other_ref[count:, inside:] = other_zone_ref[...]
        found.append((3, mm_nt(stack_ref[2 * count :, :], other_ref[...]) * scale))
    columns = out_ref.shape[2]
    for distance, block in found:
        at = group ^ distance
        parts = [block[:columns], block[columns:]]
        for core in range(2):
            out_ref[at, core] = parts[core].astype(BF16)
        give_ref[at] = jnp.where(odd, parts[0], parts[1]).astype(BF16)


def halve_body(mine_ref, got_ref, *pieces):
    for distance, piece_ref in enumerate(pieces):
        chip = (lax.axis_index("space") >> 1) ^ distance
        total = mine_ref[chip, lax.axis_index("space") & 1].astype(F32) + got_ref[chip].astype(F32)
        piece_ref[...] = total.astype(BF16)


def final_body(square_of_four, count, mine_ref, *refs):
    parts, (first_ref, second_ref) = refs[:-2], refs[-2:]
    total = mine_ref[...].astype(F32)
    if square_of_four:
        made_elsewhere = (lax.axis_index("space") >> 1) == (lax.axis_index("state") ^ 3)
        total = jnp.where(made_elsewhere, parts[0][...].astype(F32), total)
        parts = parts[1:]
    for part in parts:
        total = total + part[...].astype(F32)
    first_ref[...] = total[:, :count]
    second_ref[...] = total[:, count:]


def swap(block, n_state, n_space, lead):
    route = []
    for s in range(n_state):
        for i in range(n_space):
            j = i + 1 if (i - lead) % 2 == 0 else i - 1
            if 0 <= j < n_space:
                route.append((s * n_space + i, s * n_space + j))
            elif (s ^ 1) < n_state:
                route.append((s * n_space + i, (s ^ 1) * n_space + i))
    return lax.ppermute(block, ("state", "space"), route)


def exchange(give_a, give_b, n_state, n_space):
    got_a = swap(give_a, n_state, n_space, 0)
    got_b = swap(give_b, n_state, n_space, 1)
    return got_a, got_b


def across(block, axis, distance):
    return lax.ppermute(block, axis, [(i, i ^ distance) for i in range(lax.axis_size(axis))])


def share_out(block, distance, n_state, n_space, square_of_four):
    route = []
    for s in range(n_state):
        for i in range(n_space):
            to_group, to_chip = s, (i >> 1) ^ distance
            if square_of_four and (distance == 0 or to_chip == s ^ 3):
                to_group, to_chip = s ^ 1, to_chip ^ 1
            route.append((s * n_space + i, to_group * n_space + 2 * to_chip + (i & 1)))
    return lax.ppermute(block, ("state", "space"), route)


def program(states_in, cell_matrices, connectivity, potential):
    count, owned = states_in.shape
    cells, nodes, _ = cell_matrices.shape
    rim = nodes // 4
    extent, inside = owned + 2 * rim, owned - 2 * rim
    n_state, n_space = lax.axis_size("state"), lax.axis_size("space")
    row = potential.reshape(1, owned)
    work = 2 * count * extent * extent
    inner = SHAPE((count, inside), BF16)
    zone, sums_of = SHAPE((count, 4 * rim), BF16), SHAPE((count, 4 * rim), F32)
    give = SHAPE((count, 2 * rim), BF16)

    halo = SHAPE((count + 16, rim), BF16)
    *gave, local = call(
        halo_body, (halo, halo, SHAPE(connectivity.shape, connectivity.dtype)),
        (states_in, row, connectivity), 0, raw=(0, 1, 2),
        scratch=[
            pltpu.VMEM((count, rim), BF16), pltpu.VMEM((count, rim), BF16),
            pltpu.VMEM((1, owned), F32), pltpu.SemaphoreType.DMA((4,)),
        ],
    )
    got = exchange(*gave, n_state, n_space)
    table = SHAPE((extent, cells * nodes), BF16)
    hot, wide = call(
        spread_body, (table, table), (local, cell_matrices),
        2 * extent * cells * nodes * nodes, raw=(1,),
        scratch=[pltpu.VMEM(cell_matrices.shape, BF16), pltpu.SemaphoreType.DMA],
    )
    inner_0, zone_0, shift_inner, shift_zone, picked, sums, *gave = call(
        first_zone_body,
        (inner, zone, SHAPE((1, inside), F32), SHAPE((1, 4 * rim), F32),
         SHAPE((count, cells * nodes), BF16), sums_of, give, give),
        (states_in, *got, row, hot, wide), work,
    )
    got = exchange(*gave, n_state, n_space)
    border_line, line = SHAPE((1, 4 * rim), F32), SHAPE((1, inside), F32)
    inner_1, border, border_diagonal, partial = call(
        first_inner_body,
        (inner, SHAPE((extent, 4 * rim), BF16), border_line, sums_of),
        (inner_0, picked, shift_inner, hot, wide), 8 * extent * rim * cells * nodes,
        scratch=[pltpu.VMEM((4 * rim, cells * nodes), BF16)],
    )
    inners, zones = [inner_0, inner_1], [zone_0]
    for k in range(1, DEGREE):
        older = zones[-2:-1]
        scale = (2.0 if older else 1.0) / spectrum_half
        zone_k, sums, *gave = call(
            functools.partial(zone_body, bool(older), scale),
            (zone, sums_of, give, give),
            (sums, *got, shift_zone, zones[-1], *older, partial, border, border_diagonal), work // 6,
        )
        zones.append(zone_k)
        got = exchange(*gave, n_state, n_space)
        ins = (zone_k, inners[-1], inners[-2], shift_inner, border)
        if k == 1:
            square, diagonal, inner_k, partial = call(
                square_body, (SHAPE((inside, inside), BF16), line, inner, sums_of), (*ins, hot, wide),
                2 * inside * inside * cells * nodes,
            )
        else:
            inner_k, partial = call(inner_body, (inner, sums_of), (*ins, square, diagonal), work)
        inners.append(inner_k)
    square_of_four = four(n_state, n_space)
    distances = (1, 2) if square_of_four else range(1, n_state)
    inner_blocks = [inner_k] + [across(inner_k, "state", d) for d in distances]
    zone_k = call(
        last_zone_body, zone, (sums, *got, shift_zone, zones[-1], zones[-2]), 0
    )
    zone_blocks = [zone_k] + [across(zone_k, "state", d) for d in distances]
    energy, energy_zone, filtered = call(
        energy_body, (inner, zone, SHAPE((count, owned), BF16)),
        (zone_k, inner_k, partial, shift_inner, shift_zone, border, border_diagonal, square, diagonal), work,
    )
    blocks = [b for pair in zip(inner_blocks, zone_blocks) for b in pair]
    extra = ()
    scratch = [pltpu.VMEM((len(inner_blocks) * count, extent), BF16), pltpu.VMEM((2 * count, extent), BF16)]
    if square_of_four:
        opened, part_x = call(
            neighbour_body, (SHAPE((count, inside), F32), sums_of),
            (inner_blocks[1], shift_inner, border, square, diagonal), work // 2,
        )
        extra = (opened, part_x, shift_zone, border, border_diagonal)
        scratch += [pltpu.VMEM((2 * count, extent), BF16), pltpu.VMEM((count, 4 * rim), BF16)]
    columns = count * n_state // n_space
    chips = n_space // 2
    mine, give_half = call(
        functools.partial(project_body, square_of_four, 1.0 / (owned * n_space)),
        (SHAPE((chips, 2, columns, 2 * count), BF16), SHAPE((chips, columns, 2 * count), BF16)),
        (energy, energy_zone, *extra, *blocks), 4 * count * n_state * count * owned, scratch=scratch,
    )
    got_half = swap(give_half, n_state, n_space, 0)
    piece = SHAPE((columns, 2 * count), BF16)
    pieces = call(halve_body, (piece,) * chips, (mine, got_half), 0)
    shares = [share_out(p, d, n_state, n_space, square_of_four) for d, p in enumerate(pieces) if d or square_of_four]
    turned = SHAPE((columns, count), F32)
    intersection, projected = call(
        functools.partial(final_body, square_of_four, count), (turned, turned), (pieces[0], *shares), 0
    )
    return filtered, intersection.T, projected.T


def four(n_state, n_space):
    return n_state == 4 and n_space == 8


def solution(mesh):
    return jax.shard_map(
        program,
        mesh=mesh,
        in_specs=(P("state", "space"), P("space", None, None), P("space", None), P("space")),
        out_specs=(P("state", "space"), P("state", "space"), P("state", "space")),
        check_vma=False,
    )
```

```python
import functools

import jax
import jax.numpy as jnp
from jax import lax
from jax.experimental import pallas as pl
from jax.experimental.pallas import tpu as pltpu
from jax.sharding import PartitionSpec as P


DEGREE = 4

spectrum_center = 3.0
spectrum_half = 3.5

BF16 = jnp.bfloat16
F32 = jnp.float32
SHAPE = jax.ShapeDtypeStruct


def call(body, outs, ins, flops, scratch=(), raw=()):
    where = [
        pl.BlockSpec(memory_space=pltpu.HBM if i in raw else pltpu.VMEM) for i in range(len(ins))
    ]
    ins = [pltpu.with_memory_space_constraint(x, pltpu.HBM) if i in raw else x for i, x in enumerate(ins)]
    return pl.pallas_call(
        body,
        out_shape=outs,
        in_specs=where,
        out_specs=jax.tree.map(lambda _: pl.BlockSpec(memory_space=pltpu.VMEM), outs),
        scratch_shapes=list(scratch),
        compiler_params=pltpu.CompilerParams(vmem_limit_bytes=24 << 20),
        cost_estimate=pl.CostEstimate(flops=flops, bytes_accessed=4 << 20, transcendentals=0),
    )(*ins)


def mm(a, b):
    return jnp.dot(a, b, preferred_element_type=F32)


def mm_nt(a, b):
    return lax.dot_general(a, b, (((1,), (1,)), ((), ())), preferred_element_type=F32)


def is_odd():
    return (lax.axis_index("space") & 1) == 1


def sort_out(got_a, got_b):
    me, odd = lax.axis_index("space"), is_odd()
    got_a, got_b = got_a.astype(F32), got_b.astype(F32)
    low = jnp.where(me == 0, 0.0, jnp.where(odd, got_a, got_b))
    high = jnp.where(me == lax.axis_size("space") - 1, 0.0, jnp.where(odd, got_b, got_a))
    return low, high


def hand_out(low, high, give_a_ref, give_b_ref):
    odd = is_odd()
    give_a_ref[...] = jnp.where(odd, low, high).astype(give_a_ref.dtype)
    give_b_ref[...] = jnp.where(odd, high, low).astype(give_b_ref.dtype)


def halo_body(states_ref, potential_ref, index_ref,
              give_a_ref, give_b_ref, local_ref, low_ref, high_ref, row_ref, sem):
    count, owned = states_ref.shape
    rim = low_ref.shape[1]
    copies = [
        pltpu.make_async_copy(states_ref.at[:, pl.ds(0, rim)], low_ref, sem.at[0]),
        pltpu.make_async_copy(states_ref.at[:, pl.ds(owned - rim, rim)], high_ref, sem.at[1]),
        pltpu.make_async_copy(potential_ref, row_ref, sem.at[2]),
        pltpu.make_async_copy(index_ref, local_ref, sem.at[3]),
    ]
    for copy in copies:
        copy.start()
    for copy in copies:
        copy.wait()
    odd = is_odd()
    low, high = low_ref[...].astype(F32), high_ref[...].astype(F32)
    give_a_ref[:count, :] = jnp.where(odd, low, high).astype(BF16)
    give_b_ref[:count, :] = jnp.where(odd, high, low).astype(BF16)
    for take, give_ref in ((odd, give_a_ref), (jnp.logical_not(odd), give_b_ref)):
        row = jnp.where(take, row_ref[:, :rim], row_ref[:, owned - rim :])
        row = jnp.broadcast_to(row, (16, rim))
        at = lax.broadcasted_iota(jnp.int32, row.shape, 0)
        first = row.astype(BF16).astype(F32)
        second = (row - first).astype(BF16).astype(F32)
        third = (row - first) - second
        give_ref[count:, :] = jnp.where(
            at == 0, first, jnp.where(at == 1, second, jnp.where(at == 2, third, 0.0))
        ).astype(BF16)


def spread_body(index_ref, cells_ref, hot_ref, wide_ref, cells, sem):
    copy = pltpu.make_async_copy(cells_ref, cells, sem)
    copy.start()
    number, nodes, _ = cells_ref.shape
    extent = hot_ref.shape[0]
    rim = nodes // 4
    offset = lax.axis_index("space") * (extent - 2 * rim) - rim
    for c in range(number):
        index = index_ref[c : c + 1, :] - offset
        hot = lax.broadcasted_iota(jnp.int32, (extent, nodes), 0) == index
        hot_ref[:, c * nodes : (c + 1) * nodes] = hot.astype(BF16)
    copy.wait()
    for c in range(number):
        here = slice(c * nodes, (c + 1) * nodes)
        wide_ref[:, here] = mm(hot_ref[:, here], cells[c]).astype(BF16)


def first_zone_body(states_ref, halo_a_ref, halo_b_ref, potential_ref, hot_ref, wide_ref,
                    inner_ref, zone_ref, shift_inner_ref, shift_zone_ref, picked_ref, sums_ref, give_a_ref, give_b_ref):
    count, owned = states_ref.shape
    rim = halo_a_ref.shape[1]
    width, extent = 2 * rim, owned + 2 * rim
    low, high = sort_out(halo_a_ref[...], halo_b_ref[...])
    zone_ref[:, :rim] = low[:count].astype(BF16)
    zone_ref[:, rim:width] = states_ref[:, :rim]
    zone_ref[:, width : width + rim] = states_ref[:, owned - rim :]
    zone_ref[:, width + rim :] = high[:count].astype(BF16)
    inner_ref[...] = states_ref[:, rim : owned - rim]
    row = potential_ref[...] - spectrum_center
    shift_inner_ref[...] = row[:, rim : owned - rim]
    shift_zone_ref[:, rim:width] = row[:, :rim]
    shift_zone_ref[:, width : width + rim] = row[:, owned - rim :]
    for got, at in ((low, 0), (high, width + rim)):
        part = got[count : count + 8]
        shift_zone_ref[:, at : at + rim] = (part[0:1] + part[1:2] + part[2:3]) - spectrum_center
    picked = (
        mm(inner_ref[...], hot_ref[width : extent - width, :])
        + mm(zone_ref[:, :width], hot_ref[:width, :])
        + mm(zone_ref[:, width:], hot_ref[extent - width :, :])
    ).astype(BF16)
    picked_ref[...] = picked
    low, high = mm_nt(picked, wide_ref[:width, :]), mm_nt(picked, wide_ref[extent - width :, :])
    sums_ref[:, :width] = low
    sums_ref[:, width:] = high
    hand_out(low, high, give_a_ref, give_b_ref)


def take_diagonal(rows, start, matrix_ref, diagonal_ref, at):
    size = rows.shape[0]
    same = lax.broadcasted_iota(jnp.int32, (size, size), 0) == lax.broadcasted_iota(
        jnp.int32, (size, size), 1
    )
    square = rows[:, at : at + size]
    diagonal_ref[:, at : at + size] = jnp.sum(jnp.where(same, square, 0.0), axis=0, keepdims=True)
    matrix_ref[start : start + size, :] = rows.astype(BF16)
    matrix_ref[start : start + size, at : at + size] = jnp.where(same, 0.0, square).astype(BF16)


def first_inner_body(inner_ref, picked_ref, shift_inner_ref, hot_ref, wide_ref,
                     next_ref, border_ref, diagonal_ref, part_ref, columns_ref):
    extent = border_ref.shape[0]
    width = border_ref.shape[1] // 2
    inside = slice(width, extent - width)
    value = mm_nt(picked_ref[...], wide_ref[inside, :]) + shift_inner_ref[...] * inner_ref[...].astype(F32)
    following = (value * (1.0 / spectrum_half)).astype(BF16)
    next_ref[...] = following
    columns_ref[:width, :] = hot_ref[:width, :]
    columns_ref[width:, :] = hot_ref[extent - width :, :]
    border_ref[inside, :] = mm_nt(wide_ref[inside, :], columns_ref[...]).astype(BF16)
    for start, at in ((0, 0), (extent - width, width)):
        rows = mm_nt(wide_ref[start : start + width, :], columns_ref[...])
        take_diagonal(rows, start, border_ref, diagonal_ref, at)
    part_ref[...] = mm(following, border_ref[inside, :])


def close_zones(sums_ref, got_a_ref, got_b_ref, shift_zone_ref, mid_ref, old_ref, scale, zone_ref):
    width = got_a_ref.shape[1]
    low, high = sort_out(got_a_ref[...], got_b_ref[...])
    for got, here in ((low, slice(0, width)), (high, slice(width, 2 * width))):
        value = sums_ref[:, here] + got + shift_zone_ref[:, here] * mid_ref[:, here].astype(F32)
        value = value * scale
        if old_ref is not None:
            value = value - old_ref[:, here].astype(F32)
        zone_ref[:, here] = value.astype(BF16)


def zone_sums(zone_ref, part, border_ref, border_diagonal_ref):
    extent = border_ref.shape[0]
    width = zone_ref.shape[1] // 2
    sums = (
        part
        + mm(zone_ref[:, :width], border_ref[:width, :])
        + mm(zone_ref[:, width:], border_ref[extent - width :, :])
        + border_diagonal_ref[...] * zone_ref[...].astype(F32)
    )
    return sums[:, :width], sums[:, width:]


def zone_body(has_old, scale, sums_ref, got_a_ref, got_b_ref, shift_zone_ref, mid_ref, *rest):
    old_ref, rest = (rest[0], rest[1:]) if has_old else (None, rest)
    part_ref, border_ref, border_diagonal_ref, zone_ref, next_sums_ref, give_a_ref, give_b_ref = rest
    close_zones(sums_ref, got_a_ref, got_b_ref, shift_zone_ref, mid_ref, old_ref, scale, zone_ref)
    low, high = zone_sums(zone_ref, part_ref[...], border_ref, border_diagonal_ref)
    width = low.shape[1]
    next_sums_ref[:, :width] = low
    next_sums_ref[:, width:] = high
    hand_out(low, high, give_a_ref, give_b_ref)


def inner_sums(zone_ref, inner_ref, border_ref, square_ref, diagonal_ref):
    width = zone_ref.shape[1] // 2
    inside = slice(width, width + square_ref.shape[0])
    return (
        mm_nt(zone_ref[...], border_ref[inside, :])
        + mm(inner_ref[...], square_ref[...])
        + diagonal_ref[...] * inner_ref[...].astype(F32)
    )


def inner_body(zone_ref, inner_ref, old_ref, shift_inner_ref, border_ref, square_ref, diagonal_ref,
               next_ref, part_ref, *open_ref):
    sums = inner_sums(zone_ref, inner_ref, border_ref, square_ref, diagonal_ref)
    value = (sums + shift_inner_ref[...] * inner_ref[...].astype(F32)) * (2.0 / spectrum_half)
    next_ref[...] = (value - old_ref[...].astype(F32)).astype(BF16)
    width = zone_ref.shape[1] // 2
    part_ref[...] = mm(next_ref[...], border_ref[width : width + next_ref.shape[1], :])
    for ref in open_ref:
        line = diagonal_ref[...] + shift_inner_ref[...]
        ref[...] = mm(next_ref[...], square_ref[...]) + line * next_ref[...].astype(F32)


def last_inner_body(zone_ref, open_ref, old_ref, border_ref, next_ref):
    width = zone_ref.shape[1] // 2
    sums = open_ref[...] + mm_nt(zone_ref[...], border_ref[width : width + next_ref.shape[1], :])
    value = sums * (2.0 / spectrum_half) - old_ref[...].astype(F32)
    next_ref[...] = value.astype(BF16)


def square_body(zone_ref, inner_ref, old_ref, shift_inner_ref, border_ref, hot_ref, wide_ref,
                square_ref, diagonal_ref, next_ref, part_ref, *open_ref):
    size = square_ref.shape[0]
    width = (hot_ref.shape[0] - size) // 2
    for start in range(0, size, 256):
        rows = mm_nt(wide_ref[width + start : width + start + 256, :], hot_ref[width : width + size, :])
        take_diagonal(rows, start, square_ref, diagonal_ref, start)
    inner_body(zone_ref, inner_ref, old_ref, shift_inner_ref, border_ref, square_ref, diagonal_ref,
               next_ref, part_ref, *open_ref)


def last_zone_body(sums_ref, got_a_ref, got_b_ref, shift_zone_ref, mid_ref, old_ref, zone_ref):
    close_zones(sums_ref, got_a_ref, got_b_ref, shift_zone_ref, mid_ref, old_ref,
                2.0 / spectrum_half, zone_ref)


def zone_energy(zone_ref, part, shift_zone_ref, border_ref, border_diagonal_ref, energy_ref):
    low, high = zone_sums(zone_ref, part, border_ref, border_diagonal_ref)
    width = low.shape[1]
    rim = width // 2
    own = (shift_zone_ref[:, rim : width + rim] + spectrum_center) * zone_ref[:, rim : width + rim].astype(F32)
    energy_ref[:, :rim] = low[:, :rim].astype(energy_ref.dtype)
    energy_ref[:, rim:width] = (low[:, rim:] + own[:, :rim]).astype(energy_ref.dtype)
    energy_ref[:, width : width + rim] = (high[:, :rim] + own[:, rim:]).astype(energy_ref.dtype)
    energy_ref[:, width + rim :] = high[:, rim:].astype(energy_ref.dtype)


def energy_body(zone_ref, inner_ref, shift_inner_ref, shift_zone_ref,
                border_ref, border_diagonal_ref, square_ref, diagonal_ref, energy_ref, energy_zone_ref, filtered_ref):
    sums = inner_sums(zone_ref, inner_ref, border_ref, square_ref, diagonal_ref)
    own = (shift_inner_ref[...] + spectrum_center) * inner_ref[...].astype(F32)
    energy_ref[...] = (sums + own).astype(BF16)
    width = zone_ref.shape[1] // 2
    part = mm(inner_ref[...], border_ref[width : width + inner_ref.shape[1], :])
    zone_energy(zone_ref, part, shift_zone_ref, border_ref, border_diagonal_ref, energy_zone_ref)
    rim = width // 2
    owned = filtered_ref.shape[1]
    filtered_ref[:, :rim] = zone_ref[:, rim:width]
    filtered_ref[:, rim : owned - rim] = inner_ref[...]
    filtered_ref[:, owned - rim :] = zone_ref[:, width : width + rim]


def neighbour_body(inner_ref, beside_ref, across_ref, energy_ref, shift_inner_ref, border_ref, square_ref, diagonal_ref,
                   open_ref, part_ref, found_ref, other_ref):
    beside = beside_ref[...]
    width = border_ref.shape[1] // 2
    line = diagonal_ref[...] + (shift_inner_ref[...] + spectrum_center)
    open_ref[...] = mm(beside, square_ref[...]) + line * beside.astype(F32)
    part_ref[...] = mm(beside, border_ref[width : width + beside.shape[1], :])
    inner_found(found_ref, (inner_ref, beside_ref, across_ref), inner_ref, energy_ref)
    other_ref[...] = mm_nt(across_ref[...], beside)


def inner_found(found_ref, blocks, states_ref, energy_ref):
    count = states_ref.shape[0]
    for place, block in enumerate(blocks):
        here = slice(place * count, (place + 1) * count)
        found_ref[here, :count] = mm_nt(block[...], states_ref[...])
        found_ref[here, count:] = mm_nt(block[...], energy_ref[...])


def gram_body(*refs):
    *blocks, energy_ref, found_ref = refs
    inner_found(found_ref, blocks, blocks[0], energy_ref)


def zone_found(block_ref, zone_ref, energy_zone_ref):
    rim = zone_ref.shape[1] // 4
    here = slice(rim, 3 * rim)
    return mm_nt(block_ref[:, here], zone_ref[:, here]), mm_nt(block_ref[...], energy_zone_ref[...])


def project_body(square_of_four, scale, energy_zone_ref, found_ref, *refs):
    if square_of_four:
        (open_ref, part_ref, other_ref, across_ref, shift_zone_ref, border_ref, border_diagonal_ref), refs = refs[:7], refs[7:]
        *zones, out_ref, give_ref, other_zone_ref = refs
    else:
        *zones, out_ref, give_ref = refs
    count = energy_zone_ref.shape[0]
    columns = out_ref.shape[2] // 2
    group = lax.axis_index("state")
    odd = is_odd()

    def put(distance, states, energy):
        at = group ^ distance
        for block, there in ((states * scale, slice(0, columns)), (energy * scale, slice(columns, 2 * columns))):
            parts = [block[:columns], block[columns:]]
            for core in range(2):
                out_ref[at, core, there] = parts[core].astype(BF16)
            give_ref[at, there] = jnp.where(odd, parts[0], parts[1]).astype(BF16)

    for distance, zone in enumerate(zones):
        here = slice(distance * count, (distance + 1) * count)
        states, energy = zone_found(zone, zones[0], energy_zone_ref)
        put(distance, found_ref[here, :count] + states, found_ref[here, count:] + energy)
    if square_of_four:
        beside_zone = zones[1]
        width = beside_zone.shape[1] // 2
        rest = mm_nt(beside_zone[...], border_ref[width : width + open_ref.shape[1], :])
        energy_inner = (open_ref[...] + rest).astype(BF16)
        zone_energy(beside_zone, part_ref[...], shift_zone_ref, border_ref, border_diagonal_ref, other_zone_ref)
        states, energy = zone_found(zones[2], beside_zone, other_zone_ref)
        put(3, other_ref[...] + states, mm_nt(across_ref[...], energy_inner) + energy)


def halve_body(mine_ref, got_ref, *pieces):
    for distance, piece_ref in enumerate(pieces):
        chip = (lax.axis_index("space") >> 1) ^ distance
        total = mine_ref[chip, lax.axis_index("space") & 1].astype(F32) + got_ref[chip].astype(F32)
        piece_ref[...] = total.astype(BF16)


def final_body(square_of_four, mine_ref, *refs):
    parts, (first_ref, second_ref) = refs[:-2], refs[-2:]
    total = mine_ref[...].astype(F32)
    if square_of_four:
        made_elsewhere = (lax.axis_index("space") >> 1) == (lax.axis_index("state") ^ 3)
        total = jnp.where(made_elsewhere, parts[0][...].astype(F32), total)
        parts = parts[1:]
    for part in parts:
        total = total + part[...].astype(F32)
    columns = first_ref.shape[0]
    first_ref[...] = total[:columns]
    second_ref[...] = total[columns:]


def swap(block, n_state, n_space, lead):
    route = []
    for s in range(n_state):
        for i in range(n_space):
            j = i + 1 if (i - lead) % 2 == 0 else i - 1
            if 0 <= j < n_space:
                route.append((s * n_space + i, s * n_space + j))
            elif (s ^ 1) < n_state:
                route.append((s * n_space + i, (s ^ 1) * n_space + i))
    return lax.ppermute(block, ("state", "space"), route)


def exchange(give_a, give_b, n_state, n_space):
    got_a = swap(give_a, n_state, n_space, 0)
    got_b = swap(give_b, n_state, n_space, 1)
    return got_a, got_b


def across(block, axis, distance):
    return lax.ppermute(block, axis, [(i, i ^ distance) for i in range(lax.axis_size(axis))])


def share_out(block, distance, n_state, n_space, square_of_four):
    route = []
    for s in range(n_state):
        for i in range(n_space):
            to_group, to_chip = s, (i >> 1) ^ distance
            if square_of_four and (distance == 0 or to_chip == s ^ 3):
                to_group, to_chip = s ^ 1, to_chip ^ 1
            route.append((s * n_space + i, to_group * n_space + 2 * to_chip + (i & 1)))
    return lax.ppermute(block, ("state", "space"), route)


def program(states_in, cell_matrices, connectivity, potential):
    count, owned = states_in.shape
    cells, nodes, _ = cell_matrices.shape
    rim = nodes // 4
    extent, inside = owned + 2 * rim, owned - 2 * rim
    n_state, n_space = lax.axis_size("state"), lax.axis_size("space")
    row = potential.reshape(1, owned)
    work = 2 * count * extent * extent
    inner = SHAPE((count, inside), BF16)
    zone, sums_of = SHAPE((count, 4 * rim), BF16), SHAPE((count, 4 * rim), F32)
    give = SHAPE((count, 2 * rim), BF16)

    halo = SHAPE((count + 16, rim), BF16)
    *gave, local = call(
        halo_body, (halo, halo, SHAPE(connectivity.shape, connectivity.dtype)),
        (states_in, row, connectivity), 0, raw=(0, 1, 2),
        scratch=[
            pltpu.VMEM((count, rim), BF16), pltpu.VMEM((count, rim), BF16),
            pltpu.VMEM((1, owned), F32), pltpu.SemaphoreType.DMA((4,)),
        ],
    )
    got = exchange(*gave, n_state, n_space)
    table = SHAPE((extent, cells * nodes), BF16)
    hot, wide = call(
        spread_body, (table, table), (local, cell_matrices),
        2 * extent * cells * nodes * nodes, raw=(1,),
        scratch=[pltpu.VMEM(cell_matrices.shape, BF16), pltpu.SemaphoreType.DMA],
    )
    inner_0, zone_0, shift_inner, shift_zone, picked, sums, *gave = call(
        first_zone_body,
        (inner, zone, SHAPE((1, inside), F32), SHAPE((1, 4 * rim), F32),
         SHAPE((count, cells * nodes), BF16), sums_of, give, give),
        (states_in, *got, row, hot, wide), work,
    )
    got = exchange(*gave, n_state, n_space)
    border_line, line = SHAPE((1, 4 * rim), F32), SHAPE((1, inside), F32)
    inner_1, border, border_diagonal, partial = call(
        first_inner_body,
        (inner, SHAPE((extent, 4 * rim), BF16), border_line, sums_of),
        (inner_0, picked, shift_inner, hot, wide), 8 * extent * rim * cells * nodes,
        scratch=[pltpu.VMEM((4 * rim, cells * nodes), BF16)],
    )
    inners, zones = [inner_0, inner_1], [zone_0]
    for k in range(1, DEGREE):
        older = zones[-2:-1]
        scale = (2.0 if older else 1.0) / spectrum_half
        zone_k, sums, *gave = call(
            functools.partial(zone_body, bool(older), scale),
            (zone, sums_of, give, give),
            (sums, *got, shift_zone, zones[-1], *older, partial, border, border_diagonal), work // 6,
        )
        zones.append(zone_k)
        got = exchange(*gave, n_state, n_space)
        ins = (zone_k, inners[-1], inners[-2], shift_inner, border)
        outs = (inner, sums_of)
        if k == DEGREE - 2:
            outs += (SHAPE((count, inside), F32),)
        if k == 1:
            square, diagonal, inner_k, partial, *opened = call(
                square_body, (SHAPE((inside, inside), BF16), line, *outs), (*ins, hot, wide),
                2 * inside * inside * cells * nodes,
            )
        elif k < DEGREE - 1:
            inner_k, partial, *opened = call(inner_body, outs, (*ins, square, diagonal), work)
        else:
            inner_k = call(last_inner_body, inner, (zone_k, *opened, inners[-2], border), work // 4)
        inners.append(inner_k)
    square_of_four = four(n_state, n_space)
    distances = (1, 2) if square_of_four else range(1, n_state)
    inner_blocks = [inner_k] + [across(inner_k, "state", d) for d in distances]
    zone_k = call(
        last_zone_body, zone, (sums, *got, shift_zone, zones[-1], zones[-2]), 0
    )
    zone_blocks = [zone_k] + [across(zone_k, "state", d) for d in distances]
    energy, energy_zone, filtered = call(
        energy_body, (inner, zone, SHAPE((count, owned), BF16)),
        (zone_k, inner_k, shift_inner, shift_zone, border, border_diagonal, square, diagonal), work,
    )
    extra, scratch = (), []
    found_of = SHAPE((len(inner_blocks) * count, 2 * count), F32)
    if square_of_four:
        opened, part_x, found, other = call(
            neighbour_body,
            (SHAPE((count, inside), F32), sums_of, found_of, SHAPE((count, count), F32)),
            (*inner_blocks, energy, shift_inner, border, square, diagonal), work // 2,
        )
        extra = (opened, part_x, other, inner_blocks[2], shift_zone, border, border_diagonal)
        scratch = [pltpu.VMEM((count, 4 * rim), BF16)]
    else:
        found = call(gram_body, found_of, (*inner_blocks, energy), work)
    columns = count * n_state // n_space
    chips = n_space // 2
    mine, give_half = call(
        functools.partial(project_body, square_of_four, 1.0 / (owned * n_space)),
        (SHAPE((chips, 2, 2 * columns, count), BF16), SHAPE((chips, 2 * columns, count), BF16)),
        (energy_zone, found, *extra, *zone_blocks), work // 4, scratch=scratch,
    )
    got_half = swap(give_half, n_state, n_space, 0)
    piece = SHAPE((2 * columns, count), BF16)
    pieces = call(halve_body, (piece,) * chips, (mine, got_half), 0)
    shares = [share_out(p, d, n_state, n_space, square_of_four) for d, p in enumerate(pieces) if d or square_of_four]
    turned = SHAPE((columns, count), F32)
    intersection, projected = call(
        functools.partial(final_body, square_of_four), (turned, turned), (pieces[0], *shares), 0
    )
    return filtered, intersection.T, projected.T


def four(n_state, n_space):
    return n_state == 4 and n_space == 8


def solution(mesh):
    return jax.shard_map(
        program,
        mesh=mesh,
        in_specs=(P("state", "space"), P("space", None, None), P("space", None), P("space")),
        out_specs=(P("state", "space"), P("state", "space"), P("state", "space")),
        check_vma=False,
    )
```

```python
import functools

import jax
import jax.numpy as jnp
from jax import lax
from jax.experimental import pallas as pl
from jax.experimental.pallas import tpu as pltpu
from jax.sharding import PartitionSpec as P


DEGREE = 4

spectrum_center = 3.0
spectrum_half = 3.5

BF16 = jnp.bfloat16
F32 = jnp.float32
SHAPE = jax.ShapeDtypeStruct


def call(body, outs, ins, flops, scratch=(), raw=()):
    where = [
        pl.BlockSpec(memory_space=pltpu.HBM if i in raw else pltpu.VMEM) for i in range(len(ins))
    ]
    ins = [pltpu.with_memory_space_constraint(x, pltpu.HBM) if i in raw else x for i, x in enumerate(ins)]
    return pl.pallas_call(
        body,
        out_shape=outs,
        in_specs=where,
        out_specs=jax.tree.map(lambda _: pl.BlockSpec(memory_space=pltpu.VMEM), outs),
        scratch_shapes=list(scratch),
        compiler_params=pltpu.CompilerParams(vmem_limit_bytes=24 << 20),
        cost_estimate=pl.CostEstimate(flops=flops, bytes_accessed=4 << 20, transcendentals=0),
    )(*ins)


def mm(a, b):
    return jnp.dot(a, b, preferred_element_type=F32)


def mm_nt(a, b):
    return lax.dot_general(a, b, (((1,), (1,)), ((), ())), preferred_element_type=F32)


def is_odd():
    return (lax.axis_index("space") & 1) == 1


def sort_out(got_a, got_b):
    me, odd = lax.axis_index("space"), is_odd()
    got_a, got_b = got_a.astype(F32), got_b.astype(F32)
    low = jnp.where(me == 0, 0.0, jnp.where(odd, got_a, got_b))
    high = jnp.where(me == lax.axis_size("space") - 1, 0.0, jnp.where(odd, got_b, got_a))
    return low, high


def hand_out(low, high, give_a_ref, give_b_ref):
    odd = is_odd()
    give_a_ref[...] = jnp.where(odd, low, high).astype(give_a_ref.dtype)
    give_b_ref[...] = jnp.where(odd, high, low).astype(give_b_ref.dtype)


def halo_body(states_ref, potential_ref, index_ref,
              give_a_ref, give_b_ref, local_ref, low_ref, high_ref, row_ref, sem):
    count, owned = states_ref.shape
    rim = low_ref.shape[1]
    copies = [
        pltpu.make_async_copy(states_ref.at[:, pl.ds(0, rim)], low_ref, sem.at[0]),
        pltpu.make_async_copy(states_ref.at[:, pl.ds(owned - rim, rim)], high_ref, sem.at[1]),
        pltpu.make_async_copy(potential_ref, row_ref, sem.at[2]),
        pltpu.make_async_copy(index_ref, local_ref, sem.at[3]),
    ]
    for copy in copies:
        copy.start()
    for copy in copies:
        copy.wait()
    odd = is_odd()
    low, high = low_ref[...].astype(F32), high_ref[...].astype(F32)
    give_a_ref[:count, :] = jnp.where(odd, low, high).astype(BF16)
    give_b_ref[:count, :] = jnp.where(odd, high, low).astype(BF16)
    for take, give_ref in ((odd, give_a_ref), (jnp.logical_not(odd), give_b_ref)):
        row = jnp.where(take, row_ref[:, :rim], row_ref[:, owned - rim :])
        row = jnp.broadcast_to(row, (16, rim))
        at = lax.broadcasted_iota(jnp.int32, row.shape, 0)
        first = row.astype(BF16).astype(F32)
        second = (row - first).astype(BF16).astype(F32)
        third = (row - first) - second
        give_ref[count:, :] = jnp.where(
            at == 0, first, jnp.where(at == 1, second, jnp.where(at == 2, third, 0.0))
        ).astype(BF16)


def spread_body(index_ref, cells_ref, hot_ref, wide_ref, cells, sem):
    copy = pltpu.make_async_copy(cells_ref, cells, sem)
    copy.start()
    number, nodes, _ = cells_ref.shape
    extent = hot_ref.shape[0]
    rim = nodes // 4
    offset = lax.axis_index("space") * (extent - 2 * rim) - rim
    for c in range(number):
        index = index_ref[c : c + 1, :] - offset
        hot = lax.broadcasted_iota(jnp.int32, (extent, nodes), 0) == index
        hot_ref[:, c * nodes : (c + 1) * nodes] = hot.astype(BF16)
    copy.wait()
    for c in range(number):
        here = slice(c * nodes, (c + 1) * nodes)
        wide_ref[:, here] = mm(hot_ref[:, here], cells[c]).astype(BF16)


def first_zone_body(states_ref, halo_a_ref, halo_b_ref, potential_ref, hot_ref, wide_ref,
                    inner_ref, zone_ref, shift_inner_ref, shift_zone_ref, picked_ref, sums_ref, give_a_ref, give_b_ref):
    count, owned = states_ref.shape
    rim = halo_a_ref.shape[1]
    width, extent = 2 * rim, owned + 2 * rim
    low, high = sort_out(halo_a_ref[...], halo_b_ref[...])
    zone_ref[:, :rim] = low[:count].astype(BF16)
    zone_ref[:, rim:width] = states_ref[:, :rim]
    zone_ref[:, width : width + rim] = states_ref[:, owned - rim :]
    zone_ref[:, width + rim :] = high[:count].astype(BF16)
    inner_ref[...] = states_ref[:, rim : owned - rim]
    row = potential_ref[...] - spectrum_center
    shift_inner_ref[...] = row[:, rim : owned - rim]
    shift_zone_ref[:, rim:width] = row[:, :rim]
    shift_zone_ref[:, width : width + rim] = row[:, owned - rim :]
    for got, at in ((low, 0), (high, width + rim)):
        part = got[count : count + 8]
        shift_zone_ref[:, at : at + rim] = (part[0:1] + part[1:2] + part[2:3]) - spectrum_center
    picked = (
        mm(inner_ref[...], hot_ref[width : extent - width, :])
        + mm(zone_ref[:, :width], hot_ref[:width, :])
        + mm(zone_ref[:, width:], hot_ref[extent - width :, :])
    ).astype(BF16)
    picked_ref[...] = picked
    low, high = mm_nt(picked, wide_ref[:width, :]), mm_nt(picked, wide_ref[extent - width :, :])
    sums_ref[:, :width] = low
    sums_ref[:, width:] = high
    hand_out(low, high, give_a_ref, give_b_ref)


def take_diagonal(rows, start, matrix_ref, diagonal_ref, at):
    size = rows.shape[0]
    same = lax.broadcasted_iota(jnp.int32, (size, size), 0) == lax.broadcasted_iota(
        jnp.int32, (size, size), 1
    )
    square = rows[:, at : at + size]
    diagonal_ref[:, at : at + size] = jnp.sum(jnp.where(same, square, 0.0), axis=0, keepdims=True)
    matrix_ref[start : start + size, :] = rows.astype(BF16)
    matrix_ref[start : start + size, at : at + size] = jnp.where(same, 0.0, square).astype(BF16)


def first_inner_body(inner_ref, picked_ref, shift_inner_ref, hot_ref, wide_ref,
                     next_ref, border_ref, diagonal_ref, part_ref, columns_ref):
    extent = border_ref.shape[0]
    width = border_ref.shape[1] // 2
    inside = slice(width, extent - width)
    value = mm_nt(picked_ref[...], wide_ref[inside, :]) + shift_inner_ref[...] * inner_ref[...].astype(F32)
    following = (value * (1.0 / spectrum_half)).astype(BF16)
    next_ref[...] = following
    columns_ref[:width, :] = hot_ref[:width, :]
    columns_ref[width:, :] = hot_ref[extent - width :, :]
    border_ref[inside, :] = mm_nt(wide_ref[inside, :], columns_ref[...]).astype(BF16)
    for start, at in ((0, 0), (extent - width, width)):
        rows = mm_nt(wide_ref[start : start + width, :], columns_ref[...])
        take_diagonal(rows, start, border_ref, diagonal_ref, at)
    part_ref[...] = mm(following, border_ref[inside, :])


def close_zones(sums_ref, got_a_ref, got_b_ref, shift_zone_ref, mid_ref, old_ref, scale, zone_ref):
    width = got_a_ref.shape[1]
    low, high = sort_out(got_a_ref[...], got_b_ref[...])
    for got, here in ((low, slice(0, width)), (high, slice(width, 2 * width))):
        value = sums_ref[:, here] + got + shift_zone_ref[:, here] * mid_ref[:, here].astype(F32)
        value = value * scale
        if old_ref is not None:
            value = value - old_ref[:, here].astype(F32)
        zone_ref[:, here] = value.astype(BF16)


def zone_sums(zone_ref, part, border_ref, border_diagonal_ref):
    extent = border_ref.shape[0]
    width = zone_ref.shape[1] // 2
    sums = (
        part
        + mm(zone_ref[:, :width], border_ref[:width, :])
        + mm(zone_ref[:, width:], border_ref[extent - width :, :])
        + border_diagonal_ref[...] * zone_ref[...].astype(F32)
    )
    return sums[:, :width], sums[:, width:]


def zone_body(has_old, scale, sums_ref, got_a_ref, got_b_ref, shift_zone_ref, mid_ref, *rest):
    old_ref, rest = (rest[0], rest[1:]) if has_old else (None, rest)
    part_ref, border_ref, border_diagonal_ref, zone_ref, next_sums_ref, give_a_ref, give_b_ref = rest
    close_zones(sums_ref, got_a_ref, got_b_ref, shift_zone_ref, mid_ref, old_ref, scale, zone_ref)
    low, high = zone_sums(zone_ref, part_ref[...], border_ref, border_diagonal_ref)
    width = low.shape[1]
    next_sums_ref[:, :width] = low
    next_sums_ref[:, width:] = high
    hand_out(low, high, give_a_ref, give_b_ref)


def inner_sums(zone_ref, inner_ref, border_ref, square_ref, diagonal_ref):
    width = zone_ref.shape[1] // 2
    inside = slice(width, width + square_ref.shape[0])
    return (
        mm_nt(zone_ref[...], border_ref[inside, :])
        + mm(inner_ref[...], square_ref[...])
        + diagonal_ref[...] * inner_ref[...].astype(F32)
    )


def inner_body(zone_ref, inner_ref, old_ref, shift_inner_ref, border_ref, square_ref, diagonal_ref,
               next_ref, part_ref, *open_ref):
    sums = inner_sums(zone_ref, inner_ref, border_ref, square_ref, diagonal_ref)
    value = (sums + shift_inner_ref[...] * inner_ref[...].astype(F32)) * (2.0 / spectrum_half)
    next_ref[...] = (value - old_ref[...].astype(F32)).astype(BF16)
    width = zone_ref.shape[1] // 2
    part_ref[...] = mm(next_ref[...], border_ref[width : width + next_ref.shape[1], :])
    for ref in open_ref:
        line = diagonal_ref[...] + shift_inner_ref[...]
        ref[...] = mm(next_ref[...], square_ref[...]) + line * next_ref[...].astype(F32)


def last_inner_body(zone_ref, open_ref, old_ref, border_ref, next_ref):
    width = zone_ref.shape[1] // 2
    sums = open_ref[...] + mm_nt(zone_ref[...], border_ref[width : width + next_ref.shape[1], :])
    value = sums * (2.0 / spectrum_half) - old_ref[...].astype(F32)
    next_ref[...] = value.astype(BF16)


def square_body(zone_ref, inner_ref, old_ref, shift_inner_ref, border_ref, hot_ref, wide_ref,
                square_ref, diagonal_ref, next_ref, part_ref, *open_ref):
    size = square_ref.shape[0]
    width = (hot_ref.shape[0] - size) // 2
    for start in range(0, size, 256):
        rows = mm_nt(wide_ref[width + start : width + start + 256, :], hot_ref[width : width + size, :])
        take_diagonal(rows, start, square_ref, diagonal_ref, start)
    inner_body(zone_ref, inner_ref, old_ref, shift_inner_ref, border_ref, square_ref, diagonal_ref,
               next_ref, part_ref, *open_ref)


def last_zone_body(sums_ref, got_a_ref, got_b_ref, shift_zone_ref, mid_ref, old_ref, zone_ref):
    close_zones(sums_ref, got_a_ref, got_b_ref, shift_zone_ref, mid_ref, old_ref,
                2.0 / spectrum_half, zone_ref)


def zone_energy(zone_ref, part, shift_zone_ref, border_ref, border_diagonal_ref, energy_ref):
    low, high = zone_sums(zone_ref, part, border_ref, border_diagonal_ref)
    width = low.shape[1]
    rim = width // 2
    own = (shift_zone_ref[:, rim : width + rim] + spectrum_center) * zone_ref[:, rim : width + rim].astype(F32)
    energy_ref[:, :rim] = low[:, :rim].astype(energy_ref.dtype)
    energy_ref[:, rim:width] = (low[:, rim:] + own[:, :rim]).astype(energy_ref.dtype)
    energy_ref[:, width : width + rim] = (high[:, :rim] + own[:, rim:]).astype(energy_ref.dtype)
    energy_ref[:, width + rim :] = high[:, rim:].astype(energy_ref.dtype)


def energy_body(zone_ref, inner_ref, shift_inner_ref, shift_zone_ref,
                border_ref, border_diagonal_ref, square_ref, diagonal_ref, energy_ref, energy_zone_ref, filtered_ref):
    sums = inner_sums(zone_ref, inner_ref, border_ref, square_ref, diagonal_ref)
    own = (shift_inner_ref[...] + spectrum_center) * inner_ref[...].astype(F32)
    energy_ref[...] = (sums + own).astype(BF16)
    width = zone_ref.shape[1] // 2
    part = mm(inner_ref[...], border_ref[width : width + inner_ref.shape[1], :])
    zone_energy(zone_ref, part, shift_zone_ref, border_ref, border_diagonal_ref, energy_zone_ref)
    rim = width // 2
    owned = filtered_ref.shape[1]
    filtered_ref[:, :rim] = zone_ref[:, rim:width]
    filtered_ref[:, rim : owned - rim] = inner_ref[...]
    filtered_ref[:, owned - rim :] = zone_ref[:, width : width + rim]


def neighbour_body(inner_ref, beside_ref, across_ref, energy_ref, shift_inner_ref, border_ref, square_ref, diagonal_ref,
                   part_ref, found_ref, other_ref, other_energy_ref, toward_ref):
    beside, across = beside_ref[...], across_ref[...]
    width = border_ref.shape[1] // 2
    inside = border_ref[width : width + beside.shape[1], :]
    line = diagonal_ref[...] + (shift_inner_ref[...] + spectrum_center)
    energy = (mm(beside, square_ref[...]) + line * beside.astype(F32)).astype(BF16)
    part_ref[...] = mm(beside, inside)
    toward_ref[...] = mm(across, inside).astype(BF16)
    inner_found(found_ref, (inner_ref, beside_ref, across_ref), inner_ref, energy_ref)
    other_ref[...] = mm_nt(across, beside)
    other_energy_ref[...] = mm_nt(across, energy)


def inner_found(found_ref, blocks, states_ref, energy_ref):
    count = states_ref.shape[0]
    for place, block in enumerate(blocks):
        here = slice(place * count, (place + 1) * count)
        found_ref[here, :count] = mm_nt(block[...], states_ref[...])
        found_ref[here, count:] = mm_nt(block[...], energy_ref[...])


def gram_body(*refs):
    *blocks, energy_ref, found_ref = refs
    inner_found(found_ref, blocks, blocks[0], energy_ref)


def zone_found(block_ref, zone_ref, energy_zone_ref):
    rim = zone_ref.shape[1] // 4
    here = slice(rim, 3 * rim)
    return mm_nt(block_ref[:, here], zone_ref[:, here]), mm_nt(block_ref[...], energy_zone_ref[...])


def project_body(square_of_four, scale, energy_zone_ref, found_ref, *refs):
    if square_of_four:
        (part_ref, other_ref, other_energy_ref, toward_ref, shift_zone_ref, border_ref, border_diagonal_ref), refs = refs[:7], refs[7:]
        *zones, out_ref, give_ref, other_zone_ref = refs
    else:
        *zones, out_ref, give_ref = refs
    count = energy_zone_ref.shape[0]
    columns = out_ref.shape[2] // 2
    group = lax.axis_index("state")
    odd = is_odd()

    def put(distance, states, energy):
        at = group ^ distance
        for block, there in ((states * scale, slice(0, columns)), (energy * scale, slice(columns, 2 * columns))):
            parts = [block[:columns], block[columns:]]
            for core in range(2):
                out_ref[at, core, there] = parts[core].astype(BF16)
            give_ref[at, there] = jnp.where(odd, parts[0], parts[1]).astype(BF16)

    if square_of_four:
        zone_energy(zones[1], part_ref[...], shift_zone_ref, border_ref, border_diagonal_ref, other_zone_ref)
    for distance, zone in enumerate(zones):
        here = slice(distance * count, (distance + 1) * count)
        states, energy = zone_found(zone, zones[0], energy_zone_ref)
        put(distance, found_ref[here, :count] + states, found_ref[here, count:] + energy)
    if square_of_four:
        states, energy = zone_found(zones[2], zones[1], other_zone_ref)
        energy = energy + mm_nt(toward_ref[...], zones[1][...])
        put(3, other_ref[...] + states, other_energy_ref[...] + energy)


def halve_body(mine_ref, got_ref, *pieces):
    for distance, piece_ref in enumerate(pieces):
        chip = (lax.axis_index("space") >> 1) ^ distance
        total = mine_ref[chip, lax.axis_index("space") & 1].astype(F32) + got_ref[chip].astype(F32)
        piece_ref[...] = total.astype(BF16)


def final_body(square_of_four, mine_ref, *refs):
    parts, (first_ref, second_ref) = refs[:-2], refs[-2:]
    total = mine_ref[...].astype(F32)
    if square_of_four:
        made_elsewhere = (lax.axis_index("space") >> 1) == (lax.axis_index("state") ^ 3)
        total = jnp.where(made_elsewhere, parts[0][...].astype(F32), total)
        parts = parts[1:]
    for part in parts:
        total = total + part[...].astype(F32)
    columns = first_ref.shape[0]
    first_ref[...] = total[:columns]
    second_ref[...] = total[columns:]


def swap(block, n_state, n_space, lead):
    route = []
    for s in range(n_state):
        for i in range(n_space):
            j = i + 1 if (i - lead) % 2 == 0 else i - 1
            if 0 <= j < n_space:
                route.append((s * n_space + i, s * n_space + j))
            elif (s ^ 1) < n_state:
                route.append((s * n_space + i, (s ^ 1) * n_space + i))
    return lax.ppermute(block, ("state", "space"), route)


def exchange(give_a, give_b, n_state, n_space):
    got_a = swap(give_a, n_state, n_space, 0)
    got_b = swap(give_b, n_state, n_space, 1)
    return got_a, got_b


def across(block, axis, distance):
    return lax.ppermute(block, axis, [(i, i ^ distance) for i in range(lax.axis_size(axis))])


def share_out(block, distance, n_state, n_space, square_of_four):
    route = []
    for s in range(n_state):
        for i in range(n_space):
            to_group, to_chip = s, (i >> 1) ^ distance
            if square_of_four and (distance == 0 or to_chip == s ^ 3):
                to_group, to_chip = s ^ 1, to_chip ^ 1
            route.append((s * n_space + i, to_group * n_space + 2 * to_chip + (i & 1)))
    return lax.ppermute(block, ("state", "space"), route)


def program(states_in, cell_matrices, connectivity, potential):
    count, owned = states_in.shape
    cells, nodes, _ = cell_matrices.shape
    rim = nodes // 4
    extent, inside = owned + 2 * rim, owned - 2 * rim
    n_state, n_space = lax.axis_size("state"), lax.axis_size("space")
    row = potential.reshape(1, owned)
    work = 2 * count * extent * extent
    inner = SHAPE((count, inside), BF16)
    zone, sums_of = SHAPE((count, 4 * rim), BF16), SHAPE((count, 4 * rim), F32)
    give = SHAPE((count, 2 * rim), BF16)

    halo = SHAPE((count + 16, rim), BF16)
    *gave, local = call(
        halo_body, (halo, halo, SHAPE(connectivity.shape, connectivity.dtype)),
        (states_in, row, connectivity), 0, raw=(0, 1, 2),
        scratch=[
            pltpu.VMEM((count, rim), BF16), pltpu.VMEM((count, rim), BF16),
            pltpu.VMEM((1, owned), F32), pltpu.SemaphoreType.DMA((4,)),
        ],
    )
    got = exchange(*gave, n_state, n_space)
    table = SHAPE((extent, cells * nodes), BF16)
    hot, wide = call(
        spread_body, (table, table), (local, cell_matrices),
        2 * extent * cells * nodes * nodes, raw=(1,),
        scratch=[pltpu.VMEM(cell_matrices.shape, BF16), pltpu.SemaphoreType.DMA],
    )
    inner_0, zone_0, shift_inner, shift_zone, picked, sums, *gave = call(
        first_zone_body,
        (inner, zone, SHAPE((1, inside), F32), SHAPE((1, 4 * rim), F32),
         SHAPE((count, cells * nodes), BF16), sums_of, give, give),
        (states_in, *got, row, hot, wide), work,
    )
    got = exchange(*gave, n_state, n_space)
    border_line, line = SHAPE((1, 4 * rim), F32), SHAPE((1, inside), F32)
    inner_1, border, border_diagonal, partial = call(
        first_inner_body,
        (inner, SHAPE((extent, 4 * rim), BF16), border_line, sums_of),
        (inner_0, picked, shift_inner, hot, wide), 8 * extent * rim * cells * nodes,
        scratch=[pltpu.VMEM((4 * rim, cells * nodes), BF16)],
    )
    inners, zones = [inner_0, inner_1], [zone_0]
    for k in range(1, DEGREE):
        older = zones[-2:-1]
        scale = (2.0 if older else 1.0) / spectrum_half
        zone_k, sums, *gave = call(
            functools.partial(zone_body, bool(older), scale),
            (zone, sums_of, give, give),
            (sums, *got, shift_zone, zones[-1], *older, partial, border, border_diagonal), work // 6,
        )
        zones.append(zone_k)
        got = exchange(*gave, n_state, n_space)
        ins = (zone_k, inners[-1], inners[-2], shift_inner, border)
        outs = (inner, sums_of)
        if k == DEGREE - 2:
            outs += (SHAPE((count, inside), F32),)
        if k == 1:
            square, diagonal, inner_k, partial, *opened = call(
                square_body, (SHAPE((inside, inside), BF16), line, *outs), (*ins, hot, wide),
                2 * inside * inside * cells * nodes,
            )
        elif k < DEGREE - 1:
            inner_k, partial, *opened = call(inner_body, outs, (*ins, square, diagonal), work)
        else:
            inner_k = call(last_inner_body, inner, (zone_k, *opened, inners[-2], border), work // 4)
        inners.append(inner_k)
    square_of_four = four(n_state, n_space)
    distances = (1, 2) if square_of_four else range(1, n_state)
    inner_blocks = [inner_k] + [across(inner_k, "state", d) for d in distances]
    zone_k = call(
        last_zone_body, zone, (sums, *got, shift_zone, zones[-1], zones[-2]), 0
    )
    zone_blocks = [zone_k] + [across(zone_k, "state", d) for d in distances]
    energy, energy_zone, filtered = call(
        energy_body, (inner, zone, SHAPE((count, owned), BF16)),
        (zone_k, inner_k, shift_inner, shift_zone, border, border_diagonal, square, diagonal), work,
    )
    extra, scratch = (), []
    pair_of = SHAPE((count, count), F32)
    found_of = SHAPE((len(inner_blocks) * count, 2 * count), F32)
    if square_of_four:
        part_x, found, *other = call(
            neighbour_body, (sums_of, found_of, pair_of, pair_of, zone),
            (*inner_blocks, energy, shift_inner, border, square, diagonal), work // 2,
        )
        extra = (part_x, *other, shift_zone, border, border_diagonal)
        scratch = [pltpu.VMEM((count, 4 * rim), BF16)]
    else:
        found = call(gram_body, found_of, (*inner_blocks, energy), work)
    columns = count * n_state // n_space
    chips = n_space // 2
    mine, give_half = call(
        functools.partial(project_body, square_of_four, 1.0 / (owned * n_space)),
        (SHAPE((chips, 2, 2 * columns, count), BF16), SHAPE((chips, 2 * columns, count), BF16)),
        (energy_zone, found, *extra, *zone_blocks), work // 4, scratch=scratch,
    )
    got_half = swap(give_half, n_state, n_space, 0)
    piece = SHAPE((2 * columns, count), BF16)
    pieces = call(halve_body, (piece,) * chips, (mine, got_half), 0)
    shares = [share_out(p, d, n_state, n_space, square_of_four) for d, p in enumerate(pieces) if d or square_of_four]
    turned = SHAPE((columns, count), F32)
    intersection, projected = call(
        functools.partial(final_body, square_of_four), (turned, turned), (pieces[0], *shares), 0
    )
    return filtered, intersection.T, projected.T


def four(n_state, n_space):
    return n_state == 4 and n_space == 8


def solution(mesh):
    return jax.shard_map(
        program,
        mesh=mesh,
        in_specs=(P("state", "space"), P("space", None, None), P("space", None), P("space")),
        out_specs=(P("state", "space"), P("state", "space"), P("state", "space")),
        check_vma=False,
    )
```

```python
import functools

import jax
import jax.numpy as jnp
from jax import lax
from jax.experimental import pallas as pl
from jax.experimental.pallas import tpu as pltpu
from jax.sharding import PartitionSpec as P


DEGREE = 4

spectrum_center = 3.0
spectrum_half = 3.5

BF16 = jnp.bfloat16
F32 = jnp.float32
SHAPE = jax.ShapeDtypeStruct


def call(body, outs, ins, flops, scratch=(), raw=()):
    where = [
        pl.BlockSpec(memory_space=pltpu.HBM if i in raw else pltpu.VMEM) for i in range(len(ins))
    ]
    ins = [pltpu.with_memory_space_constraint(x, pltpu.HBM) if i in raw else x for i, x in enumerate(ins)]
    return pl.pallas_call(
        body,
        out_shape=outs,
        in_specs=where,
        out_specs=jax.tree.map(lambda _: pl.BlockSpec(memory_space=pltpu.VMEM), outs),
        scratch_shapes=list(scratch),
        compiler_params=pltpu.CompilerParams(vmem_limit_bytes=24 << 20),
        cost_estimate=pl.CostEstimate(flops=flops, bytes_accessed=4 << 20, transcendentals=0),
    )(*ins)


def mm(a, b):
    return jnp.dot(a, b, preferred_element_type=F32)


def mm_nt(a, b):
    return lax.dot_general(a, b, (((1,), (1,)), ((), ())), preferred_element_type=F32)


def is_odd():
    return (lax.axis_index("space") & 1) == 1


def sort_out(got_a, got_b):
    me, odd = lax.axis_index("space"), is_odd()
    got_a, got_b = got_a.astype(F32), got_b.astype(F32)
    low = jnp.where(me == 0, 0.0, jnp.where(odd, got_a, got_b))
    high = jnp.where(me == lax.axis_size("space") - 1, 0.0, jnp.where(odd, got_b, got_a))
    return low, high


def hand_out(low, high, give_a_ref, give_b_ref):
    odd = is_odd()
    give_a_ref[...] = jnp.where(odd, low, high).astype(give_a_ref.dtype)
    give_b_ref[...] = jnp.where(odd, high, low).astype(give_b_ref.dtype)


def halo_body(states_ref, potential_ref, index_ref,
              give_a_ref, give_b_ref, row_ref, local_ref, low_ref, high_ref, sem):
    count, owned = states_ref.shape
    rim = low_ref.shape[1]
    copies = [
        pltpu.make_async_copy(states_ref.at[:, pl.ds(0, rim)], low_ref, sem.at[0]),
        pltpu.make_async_copy(states_ref.at[:, pl.ds(owned - rim, rim)], high_ref, sem.at[1]),
        pltpu.make_async_copy(potential_ref, row_ref, sem.at[2]),
        pltpu.make_async_copy(index_ref, local_ref, sem.at[3]),
    ]
    for copy in copies:
        copy.start()
    for copy in copies:
        copy.wait()
    odd = is_odd()
    low, high = low_ref[...].astype(F32), high_ref[...].astype(F32)
    give_a_ref[:count, :] = jnp.where(odd, low, high).astype(BF16)
    give_b_ref[:count, :] = jnp.where(odd, high, low).astype(BF16)
    for take, give_ref in ((odd, give_a_ref), (jnp.logical_not(odd), give_b_ref)):
        row = jnp.where(take, row_ref[:, :rim], row_ref[:, owned - rim :])
        row = jnp.broadcast_to(row, (16, rim))
        at = lax.broadcasted_iota(jnp.int32, row.shape, 0)
        first = row.astype(BF16).astype(F32)
        second = (row - first).astype(BF16).astype(F32)
        third = (row - first) - second
        give_ref[count:, :] = jnp.where(
            at == 0, first, jnp.where(at == 1, second, jnp.where(at == 2, third, 0.0))
        ).astype(BF16)


def spread_body(index_ref, states_ref, cells_ref, hot_ref, wide_ref, picked_ref, here_ref, cells_out_ref, sem):
    states_copy = pltpu.make_async_copy(states_ref, here_ref, sem.at[0])
    cells_copy = pltpu.make_async_copy(cells_ref, cells_out_ref, sem.at[1])
    states_copy.start()
    cells_copy.start()
    number, nodes, _ = cells_ref.shape
    extent = hot_ref.shape[0]
    rim = nodes // 4
    width = 2 * rim
    offset = lax.axis_index("space") * (extent - width) - rim
    for c in range(number):
        index = index_ref[c : c + 1, :] - offset
        hot = lax.broadcasted_iota(jnp.int32, (extent, nodes), 0) == index
        hot_ref[:, c * nodes : (c + 1) * nodes] = hot.astype(BF16)
    states_copy.wait()
    picked_ref[...] = mm(here_ref[...], hot_ref[rim : extent - rim, :]).astype(BF16)
    cells_copy.wait()
    for c in range(number):
        here = slice(c * nodes, (c + 1) * nodes)
        wide_ref[:width, here] = mm(hot_ref[:width, here], cells_out_ref[c]).astype(BF16)
        wide_ref[width:, here] = mm(hot_ref[extent - width :, here], cells_out_ref[c]).astype(BF16)


def first_zone_body(states_ref, halo_a_ref, halo_b_ref, potential_ref, hot_ref, wide_ref, owned_ref,
                    inner_ref, zone_ref, shift_inner_ref, shift_zone_ref, picked_ref, sums_ref, give_a_ref, give_b_ref):
    count, owned = states_ref.shape
    rim = halo_a_ref.shape[1]
    width, extent = 2 * rim, owned + 2 * rim
    low, high = sort_out(halo_a_ref[...], halo_b_ref[...])
    zone_ref[:, :rim] = low[:count].astype(BF16)
    zone_ref[:, rim:width] = states_ref[:, :rim]
    zone_ref[:, width : width + rim] = states_ref[:, owned - rim :]
    zone_ref[:, width + rim :] = high[:count].astype(BF16)
    inner_ref[...] = states_ref[:, rim : owned - rim]
    row = potential_ref[...] - spectrum_center
    shift_inner_ref[...] = row[:, rim : owned - rim]
    shift_zone_ref[:, rim:width] = row[:, :rim]
    shift_zone_ref[:, width : width + rim] = row[:, owned - rim :]
    for got, at in ((low, 0), (high, width + rim)):
        part = got[count : count + 8]
        shift_zone_ref[:, at : at + rim] = (part[0:1] + part[1:2] + part[2:3]) - spectrum_center
    picked = (
        owned_ref[...].astype(F32)
        + mm(zone_ref[:, :rim], hot_ref[:rim, :])
        + mm(zone_ref[:, width + rim :], hot_ref[extent - rim :, :])
    ).astype(BF16)
    picked_ref[...] = picked
    sums = mm_nt(picked, wide_ref[...])
    sums_ref[...] = sums
    hand_out(sums[:, :width], sums[:, width:], give_a_ref, give_b_ref)


def take_diagonal(rows, start, matrix_ref, diagonal_ref, at):
    size = rows.shape[0]
    same = lax.broadcasted_iota(jnp.int32, (size, size), 0) == lax.broadcasted_iota(
        jnp.int32, (size, size), 1
    )
    square = rows[:, at : at + size]
    diagonal_ref[:, at : at + size] = jnp.sum(jnp.where(same, square, 0.0), axis=0, keepdims=True)
    matrix_ref[start : start + size, :] = rows.astype(BF16)
    matrix_ref[start : start + size, at : at + size] = jnp.where(same, 0.0, square).astype(BF16)


def first_inner_body(inner_ref, picked_ref, shift_inner_ref, hot_ref, wide_ref, cells_ref,
                     next_ref, wide_inner_ref, border_ref, diagonal_ref, part_ref, next_picked_ref, columns_ref):
    extent = hot_ref.shape[0]
    width = border_ref.shape[1] // 2
    inside = slice(width, extent - width)
    number, nodes, _ = cells_ref.shape
    for c in range(number):
        here = slice(c * nodes, (c + 1) * nodes)
        wide_inner_ref[:, here] = mm(hot_ref[inside, here], cells_ref[c]).astype(BF16)
    value = mm_nt(picked_ref[...], wide_inner_ref[...]) + shift_inner_ref[...] * inner_ref[...].astype(F32)
    next_ref[...] = (value * (1.0 / spectrum_half)).astype(BF16)
    columns_ref[:width, :] = hot_ref[:width, :]
    columns_ref[width:, :] = hot_ref[extent - width :, :]
    for at in (0, width):
        rows = mm_nt(wide_ref[at : at + width, :], columns_ref[...])
        take_diagonal(rows, at, border_ref, diagonal_ref, at)
    next_picked_ref[...] = mm(next_ref[...], hot_ref[inside, :]).astype(BF16)
    part_ref[...] = mm_nt(next_picked_ref[...], wide_ref[...])


def close_zones(sums_ref, got_a_ref, got_b_ref, shift_zone_ref, mid_ref, old_ref, scale, zone_ref):
    width = got_a_ref.shape[1]
    low, high = sort_out(got_a_ref[...], got_b_ref[...])
    for got, here in ((low, slice(0, width)), (high, slice(width, 2 * width))):
        value = sums_ref[:, here] + got + shift_zone_ref[:, here] * mid_ref[:, here].astype(F32)
        value = value * scale
        if old_ref is not None:
            value = value - old_ref[:, here].astype(F32)
        zone_ref[:, here] = value.astype(BF16)


def zone_sums(zone_ref, part, border_ref, border_diagonal_ref):
    width = zone_ref.shape[1] // 2
    sums = part + mm(zone_ref[...], border_ref[...]) + border_diagonal_ref[...] * zone_ref[...].astype(F32)
    return sums[:, :width], sums[:, width:]


def zone_body(has_old, scale, sums_ref, got_a_ref, got_b_ref, shift_zone_ref, mid_ref, *rest):
    old_ref, rest = (rest[0], rest[1:]) if has_old else (None, rest)
    part_ref, border_ref, border_diagonal_ref, zone_ref, next_sums_ref, give_a_ref, give_b_ref = rest
    close_zones(sums_ref, got_a_ref, got_b_ref, shift_zone_ref, mid_ref, old_ref, scale, zone_ref)
    low, high = zone_sums(zone_ref, part_ref[...], border_ref, border_diagonal_ref)
    width = low.shape[1]
    next_sums_ref[:, :width] = low
    next_sums_ref[:, width:] = high
    hand_out(low, high, give_a_ref, give_b_ref)


def inner_sums(zone_ref, inner_ref, columns_ref, square_ref, diagonal_ref):
    return (
        mm_nt(zone_ref[...], columns_ref[...])
        + mm(inner_ref[...], square_ref[...])
        + diagonal_ref[...] * inner_ref[...].astype(F32)
    )


def second_inner_body(zone_ref, inner_ref, old_ref, shift_inner_ref, picked_ref, hot_ref, wide_inner_ref,
                      next_ref, part_ref, columns_ref, square_ref, diagonal_ref, zone_hot_ref):
    extent = hot_ref.shape[0]
    width = zone_ref.shape[1] // 2
    zone_hot_ref[:width, :] = hot_ref[:width, :]
    zone_hot_ref[width:, :] = hot_ref[extent - width :, :]
    columns_ref[...] = mm_nt(wide_inner_ref[...], zone_hot_ref[...]).astype(BF16)
    picked = (picked_ref[...].astype(F32) + mm(zone_ref[...], zone_hot_ref[...])).astype(BF16)
    sums = mm_nt(picked, wide_inner_ref[...])
    value = (sums + shift_inner_ref[...] * inner_ref[...].astype(F32)) * (2.0 / spectrum_half)
    next_ref[...] = (value - old_ref[...].astype(F32)).astype(BF16)
    part_ref[...] = mm(next_ref[...], columns_ref[...])
    rows = mm_nt(wide_inner_ref[: square_ref.shape[0], :], hot_ref[width : extent - width, :])
    diagonal_ref[...] = jnp.zeros_like(diagonal_ref)
    take_diagonal(rows, 0, square_ref, diagonal_ref, 0)


def third_inner_body(zone_ref, inner_ref, old_ref, shift_inner_ref, columns_ref, begun_ref, begun_diagonal_ref,
                     hot_ref, wide_inner_ref, square_ref, diagonal_ref, next_ref, part_ref, open_ref):
    size, step = square_ref.shape[0], begun_ref.shape[0]
    width = (hot_ref.shape[0] - size) // 2
    square_ref[:step, :] = begun_ref[...]
    diagonal_ref[...] = begun_diagonal_ref[...]
    for start in range(step, size, step):
        rows = mm_nt(wide_inner_ref[start : start + step, :], hot_ref[width : width + size, :])
        take_diagonal(rows, start, square_ref, diagonal_ref, start)
    line = diagonal_ref[...] + shift_inner_ref[...]
    sums = (
        mm_nt(zone_ref[...], columns_ref[...])
        + mm(inner_ref[...], square_ref[...])
        + line * inner_ref[...].astype(F32)
    )
    next_ref[...] = (sums * (2.0 / spectrum_half) - old_ref[...].astype(F32)).astype(BF16)
    part_ref[...] = mm(next_ref[...], columns_ref[...])
    open_ref[...] = mm(next_ref[...], square_ref[...]) + line * next_ref[...].astype(F32)


def last_inner_body(zone_ref, open_ref, old_ref, columns_ref, next_ref):
    sums = open_ref[...] + mm_nt(zone_ref[...], columns_ref[...])
    value = sums * (2.0 / spectrum_half) - old_ref[...].astype(F32)
    next_ref[...] = value.astype(BF16)


def last_zone_body(sums_ref, got_a_ref, got_b_ref, shift_zone_ref, mid_ref, old_ref, zone_ref):
    close_zones(sums_ref, got_a_ref, got_b_ref, shift_zone_ref, mid_ref, old_ref,
                2.0 / spectrum_half, zone_ref)


def zone_energy(zone_ref, part, shift_zone_ref, border_ref, border_diagonal_ref, energy_ref):
    low, high = zone_sums(zone_ref, part, border_ref, border_diagonal_ref)
    width = low.shape[1]
    rim = width // 2
    own = (shift_zone_ref[:, rim : width + rim] + spectrum_center) * zone_ref[:, rim : width + rim].astype(F32)
    energy_ref[:, :rim] = low[:, :rim].astype(energy_ref.dtype)
    energy_ref[:, rim:width] = (low[:, rim:] + own[:, :rim]).astype(energy_ref.dtype)
    energy_ref[:, width : width + rim] = (high[:, :rim] + own[:, rim:]).astype(energy_ref.dtype)
    energy_ref[:, width + rim :] = high[:, rim:].astype(energy_ref.dtype)


def energy_body(zone_ref, inner_ref, shift_inner_ref, shift_zone_ref,
                border_ref, border_diagonal_ref, columns_ref, square_ref, diagonal_ref, energy_ref, energy_zone_ref, filtered_ref):
    sums = inner_sums(zone_ref, inner_ref, columns_ref, square_ref, diagonal_ref)
    own = (shift_inner_ref[...] + spectrum_center) * inner_ref[...].astype(F32)
    energy_ref[...] = (sums + own).astype(BF16)
    width = zone_ref.shape[1] // 2
    part = mm(inner_ref[...], columns_ref[...])
    zone_energy(zone_ref, part, shift_zone_ref, border_ref, border_diagonal_ref, energy_zone_ref)
    rim = width // 2
    owned = filtered_ref.shape[1]
    filtered_ref[:, :rim] = zone_ref[:, rim:width]
    filtered_ref[:, rim : owned - rim] = inner_ref[...]
    filtered_ref[:, owned - rim :] = zone_ref[:, width : width + rim]


def neighbour_body(inner_ref, beside_ref, across_ref, energy_ref, shift_inner_ref, columns_ref, square_ref, diagonal_ref,
                   part_ref, found_ref, other_ref, other_energy_ref, toward_ref):
    beside, across = beside_ref[...], across_ref[...]
    line = diagonal_ref[...] + (shift_inner_ref[...] + spectrum_center)
    energy = (mm(beside, square_ref[...]) + line * beside.astype(F32)).astype(BF16)
    part_ref[...] = mm(beside, columns_ref[...])
    toward_ref[...] = mm(across, columns_ref[...]).astype(BF16)
    inner_found(found_ref, (inner_ref, beside_ref, across_ref), inner_ref, energy_ref)
    other_ref[...] = mm_nt(across, beside)
    other_energy_ref[...] = mm_nt(across, energy)


def inner_found(found_ref, blocks, states_ref, energy_ref):
    count = states_ref.shape[0]
    for place, block in enumerate(blocks):
        here = slice(place * count, (place + 1) * count)
        found_ref[here, :count] = mm_nt(block[...], states_ref[...])
        found_ref[here, count:] = mm_nt(block[...], energy_ref[...])


def gram_body(*refs):
    *blocks, energy_ref, found_ref = refs
    inner_found(found_ref, blocks, blocks[0], energy_ref)


def zone_found(block_ref, zone_ref, energy_zone_ref):
    rim = zone_ref.shape[1] // 4
    here = slice(rim, 3 * rim)
    return mm_nt(block_ref[:, here], zone_ref[:, here]), mm_nt(block_ref[...], energy_zone_ref[...])


def project_body(square_of_four, scale, energy_zone_ref, found_ref, *refs):
    if square_of_four:
        (part_ref, other_ref, other_energy_ref, toward_ref, shift_zone_ref, border_ref, border_diagonal_ref), refs = refs[:7], refs[7:]
        *zones, out_ref, give_ref, other_zone_ref = refs
    else:
        *zones, out_ref, give_ref = refs
    count = energy_zone_ref.shape[0]
    columns = out_ref.shape[2] // 2
    group = lax.axis_index("state")
    odd = is_odd()

    def put(distance, states, energy):
        at = group ^ distance
        for block, there in ((states * scale, slice(0, columns)), (energy * scale, slice(columns, 2 * columns))):
            parts = [block[:columns], block[columns:]]
            for core in range(2):
                out_ref[at, core, there] = parts[core].astype(BF16)
            give_ref[at, there] = jnp.where(odd, parts[0], parts[1]).astype(BF16)

    if square_of_four:
        zone_energy(zones[1], part_ref[...], shift_zone_ref, border_ref, border_diagonal_ref, other_zone_ref)
    for distance, zone in enumerate(zones):
        here = slice(distance * count, (distance + 1) * count)
        states, energy = zone_found(zone, zones[0], energy_zone_ref)
        put(distance, found_ref[here, :count] + states, found_ref[here, count:] + energy)
    if square_of_four:
        states, energy = zone_found(zones[2], zones[1], other_zone_ref)
        energy = energy + mm_nt(toward_ref[...], zones[1][...])
        put(3, other_ref[...] + states, other_energy_ref[...] + energy)


def halve_body(mine_ref, got_ref, *pieces):
    for distance, piece_ref in enumerate(pieces):
        chip = (lax.axis_index("space") >> 1) ^ distance
        total = mine_ref[chip, lax.axis_index("space") & 1].astype(F32) + got_ref[chip].astype(F32)
        piece_ref[...] = total.astype(BF16)


def final_body(square_of_four, mine_ref, *refs):
    parts, (first_ref, second_ref) = refs[:-2], refs[-2:]
    total = mine_ref[...].astype(F32)
    if square_of_four:
        made_elsewhere = (lax.axis_index("space") >> 1) == (lax.axis_index("state") ^ 3)
        total = jnp.where(made_elsewhere, parts[0][...].astype(F32), total)
        parts = parts[1:]
    for part in parts:
        total = total + part[...].astype(F32)
    columns = first_ref.shape[0]
    first_ref[...] = total[:columns]
    second_ref[...] = total[columns:]


def swap(block, n_state, n_space, lead):
    route = []
    for s in range(n_state):
        for i in range(n_space):
            j = i + 1 if (i - lead) % 2 == 0 else i - 1
            if 0 <= j < n_space:
                route.append((s * n_space + i, s * n_space + j))
            elif (s ^ 1) < n_state:
                route.append((s * n_space + i, (s ^ 1) * n_space + i))
    return lax.ppermute(block, ("state", "space"), route)


def exchange(give_a, give_b, n_state, n_space):
    got_a = swap(give_a, n_state, n_space, 0)
    got_b = swap(give_b, n_state, n_space, 1)
    return got_a, got_b


def across(block, axis, distance):
    return lax.ppermute(block, axis, [(i, i ^ distance) for i in range(lax.axis_size(axis))])


def share_out(block, distance, n_state, n_space, square_of_four):
    route = []
    for s in range(n_state):
        for i in range(n_space):
            to_group, to_chip = s, (i >> 1) ^ distance
            if square_of_four and (distance == 0 or to_chip == s ^ 3):
                to_group, to_chip = s ^ 1, to_chip ^ 1
            route.append((s * n_space + i, to_group * n_space + 2 * to_chip + (i & 1)))
    return lax.ppermute(block, ("state", "space"), route)


def program(states_in, cell_matrices, connectivity, potential):
    count, owned = states_in.shape
    cells, nodes, _ = cell_matrices.shape
    rim = nodes // 4
    extent, inside = owned + 2 * rim, owned - 2 * rim
    n_state, n_space = lax.axis_size("state"), lax.axis_size("space")
    row = potential.reshape(1, owned)
    work = 2 * count * extent * extent
    inner = SHAPE((count, inside), BF16)
    zone, sums_of = SHAPE((count, 4 * rim), BF16), SHAPE((count, 4 * rim), F32)
    give = SHAPE((count, 2 * rim), BF16)

    halo = SHAPE((count + 16, rim), BF16)
    *gave, row, local = call(
        halo_body,
        (halo, halo, SHAPE(row.shape, F32), SHAPE(connectivity.shape, connectivity.dtype)),
        (states_in, row, connectivity), 0, raw=(0, 1, 2),
        scratch=[
            pltpu.VMEM((count, rim), BF16), pltpu.VMEM((count, rim), BF16), pltpu.SemaphoreType.DMA((4,)),
        ],
    )
    got = exchange(*gave, n_state, n_space)
    table = SHAPE((extent, cells * nodes), BF16)
    hot, wide, picked, states_here, cells_here = call(
        spread_body,
        (table, SHAPE((4 * rim, cells * nodes), BF16), SHAPE((count, cells * nodes), BF16),
         SHAPE(states_in.shape, BF16), SHAPE(cell_matrices.shape, BF16)),
        (local, states_in, cell_matrices), work, raw=(1, 2), scratch=[pltpu.SemaphoreType.DMA((2,))],
    )
    border_line, line = SHAPE((1, 4 * rim), F32), SHAPE((1, inside), F32)
    inner_0, zone_0, shift_inner, shift_zone, picked, sums, *gave = call(
        first_zone_body,
        (inner, zone, line, border_line, SHAPE((count, cells * nodes), BF16), sums_of, give, give),
        (states_here, *got, row, hot, wide, picked), work,
    )
    got = exchange(*gave, n_state, n_space)
    inner_1, wide_inner, border, border_diagonal, partial, picked = call(
        first_inner_body,
        (inner, SHAPE((inside, cells * nodes), BF16), SHAPE((4 * rim, 4 * rim), BF16), border_line, sums_of,
         SHAPE((count, cells * nodes), BF16)),
        (inner_0, picked, shift_inner, hot, wide, cells_here), 8 * extent * rim * cells * nodes,
        scratch=[pltpu.VMEM((4 * rim, cells * nodes), BF16)],
    )
    inners, zones = [inner_0, inner_1], [zone_0]
    for k in range(1, DEGREE):
        older = zones[-2:-1]
        scale = (2.0 if older else 1.0) / spectrum_half
        zone_k, sums, *gave = call(
            functools.partial(zone_body, bool(older), scale),
            (zone, sums_of, give, give),
            (sums, *got, shift_zone, zones[-1], *older, partial, border, border_diagonal), work // 6,
        )
        zones.append(zone_k)
        got = exchange(*gave, n_state, n_space)
        ins = (zone_k, inners[-1], inners[-2], shift_inner)
        if k == 1:
            inner_k, partial, columns, begun, begun_diagonal = call(
                second_inner_body,
                (inner, sums_of, SHAPE((inside, 4 * rim), BF16), SHAPE((2 * rim, inside), BF16), line),
                (*ins, picked, hot, wide_inner), 4 * extent * rim * cells * nodes,
                scratch=[pltpu.VMEM((4 * rim, cells * nodes), BF16)],
            )
        elif k == 2:
            square, diagonal, inner_k, partial, opened = call(
                third_inner_body,
                (SHAPE((inside, inside), BF16), line, inner, sums_of, SHAPE((count, inside), F32)),
                (*ins, columns, begun, begun_diagonal, hot, wide_inner), 4 * extent * rim * cells * nodes,
            )
        else:
            inner_k = call(last_inner_body, inner, (zone_k, opened, inners[-2], columns), work // 4)
        inners.append(inner_k)
    square_of_four = four(n_state, n_space)
    distances = (1, 2) if square_of_four else range(1, n_state)
    inner_blocks = [inner_k] + [across(inner_k, "state", d) for d in distances]
    zone_k = call(
        last_zone_body, zone, (sums, *got, shift_zone, zones[-1], zones[-2]), 0
    )
    zone_blocks = [zone_k] + [across(zone_k, "state", d) for d in distances]
    energy, energy_zone, filtered = call(
        energy_body, (inner, zone, SHAPE((count, owned), BF16)),
        (zone_k, inner_k, shift_inner, shift_zone, border, border_diagonal, columns, square, diagonal), work,
    )
    extra, scratch = (), []
    pair_of = SHAPE((count, count), F32)
    found_of = SHAPE((len(inner_blocks) * count, 2 * count), F32)
    if square_of_four:
        part_x, found, *other = call(
            neighbour_body, (sums_of, found_of, pair_of, pair_of, zone),
            (*inner_blocks, energy, shift_inner, columns, square, diagonal), work // 2,
        )
        extra = (part_x, *other, shift_zone, border, border_diagonal)
        scratch = [pltpu.VMEM((count, 4 * rim), BF16)]
    else:
        found = call(gram_body, found_of, (*inner_blocks, energy), work)
    share = count * n_state // n_space
    chips = n_space // 2
    mine, give_half = call(
        functools.partial(project_body, square_of_four, 1.0 / (owned * n_space)),
        (SHAPE((chips, 2, 2 * share, count), BF16), SHAPE((chips, 2 * share, count), BF16)),
        (energy_zone, found, *extra, *zone_blocks), work // 4, scratch=scratch,
    )
    got_half = swap(give_half, n_state, n_space, 0)
    piece = SHAPE((2 * share, count), BF16)
    pieces = call(halve_body, (piece,) * chips, (mine, got_half), 0)
    shares = [share_out(p, d, n_state, n_space, square_of_four) for d, p in enumerate(pieces) if d or square_of_four]
    turned = SHAPE((share, count), F32)
    intersection, projected = call(
        functools.partial(final_body, square_of_four), (turned, turned), (pieces[0], *shares), 0
    )
    return filtered, intersection.T, projected.T


def four(n_state, n_space):
    return n_state == 4 and n_space == 8


def solution(mesh):
    return jax.shard_map(
        program,
        mesh=mesh,
        in_specs=(P("state", "space"), P("space", None, None), P("space", None), P("space")),
        out_specs=(P("state", "space"), P("state", "space"), P("state", "space")),
        check_vma=False,
    )
```

```python
import functools

import jax
import jax.numpy as jnp
from jax import lax
from jax.experimental import pallas as pl
from jax.experimental.pallas import tpu as pltpu
from jax.sharding import PartitionSpec as P


DEGREE = 4

spectrum_center = 3.0
spectrum_half = 3.5

BF16 = jnp.bfloat16
F32 = jnp.float32
SHAPE = jax.ShapeDtypeStruct


def call(body, outs, ins, flops, scratch=(), raw=()):
    where = [
        pl.BlockSpec(memory_space=pltpu.HBM if i in raw else pltpu.VMEM) for i in range(len(ins))
    ]
    ins = [pltpu.with_memory_space_constraint(x, pltpu.HBM) if i in raw else x for i, x in enumerate(ins)]
    return pl.pallas_call(
        body,
        out_shape=outs,
        in_specs=where,
        out_specs=jax.tree.map(lambda _: pl.BlockSpec(memory_space=pltpu.VMEM), outs),
        scratch_shapes=list(scratch),
        compiler_params=pltpu.CompilerParams(vmem_limit_bytes=24 << 20),
        cost_estimate=pl.CostEstimate(flops=flops, bytes_accessed=4 << 20, transcendentals=0),
    )(*ins)


def mm(a, b):
    return jnp.dot(a, b, preferred_element_type=F32)


def mm_nt(a, b):
    return lax.dot_general(a, b, (((1,), (1,)), ((), ())), preferred_element_type=F32)


def is_odd():
    return (lax.axis_index("space") & 1) == 1


def sort_out(got_a, got_b):
    me, odd = lax.axis_index("space"), is_odd()
    got_a, got_b = got_a.astype(F32), got_b.astype(F32)
    low = jnp.where(me == 0, 0.0, jnp.where(odd, got_a, got_b))
    high = jnp.where(me == lax.axis_size("space") - 1, 0.0, jnp.where(odd, got_b, got_a))
    return low, high


def hand_out(low, high, give_a_ref, give_b_ref):
    odd = is_odd()
    give_a_ref[...] = jnp.where(odd, low, high).astype(give_a_ref.dtype)
    give_b_ref[...] = jnp.where(odd, high, low).astype(give_b_ref.dtype)


def halo_body(states_ref, potential_ref, index_ref,
              give_a_ref, give_b_ref, row_ref, local_ref, low_ref, high_ref, sem):
    count, owned = states_ref.shape
    rim = low_ref.shape[1]
    copies = [
        pltpu.make_async_copy(states_ref.at[:, pl.ds(0, rim)], low_ref, sem.at[0]),
        pltpu.make_async_copy(states_ref.at[:, pl.ds(owned - rim, rim)], high_ref, sem.at[1]),
        pltpu.make_async_copy(potential_ref, row_ref, sem.at[2]),
        pltpu.make_async_copy(index_ref, local_ref, sem.at[3]),
    ]
    for copy in copies:
        copy.start()
    for copy in copies:
        copy.wait()
    odd = is_odd()
    low, high = low_ref[...].astype(F32), high_ref[...].astype(F32)
    give_a_ref[:count, :] = jnp.where(odd, low, high).astype(BF16)
    give_b_ref[:count, :] = jnp.where(odd, high, low).astype(BF16)
    for take, give_ref in ((odd, give_a_ref), (jnp.logical_not(odd), give_b_ref)):
        row = jnp.where(take, row_ref[:, :rim], row_ref[:, owned - rim :])
        row = jnp.broadcast_to(row, (16, rim))
        at = lax.broadcasted_iota(jnp.int32, row.shape, 0)
        first = row.astype(BF16).astype(F32)
        second = (row - first).astype(BF16).astype(F32)
        third = (row - first) - second
        give_ref[count:, :] = jnp.where(
            at == 0, first, jnp.where(at == 1, second, jnp.where(at == 2, third, 0.0))
        ).astype(BF16)


def spread_body(index_ref, states_ref, cells_ref,
                hot_ref, outer_ref, wide_ref, picked_ref, here_ref, cells_out_ref, sem):
    states_copy = pltpu.make_async_copy(states_ref, here_ref, sem.at[0])
    cells_copy = pltpu.make_async_copy(cells_ref, cells_out_ref, sem.at[1])
    states_copy.start()
    cells_copy.start()
    number, nodes, _ = cells_ref.shape
    extent = hot_ref.shape[0]
    rim = nodes // 4
    width = 2 * rim
    offset = lax.axis_index("space") * (extent - width) - rim
    for c in range(number):
        index = index_ref[c : c + 1, :] - offset
        hot = lax.broadcasted_iota(jnp.int32, (extent, nodes), 0) == index
        hot_ref[:, c * nodes : (c + 1) * nodes] = hot.astype(BF16)
    outer_ref[:rim, :] = hot_ref[:rim, :]
    outer_ref[rim:, :] = hot_ref[extent - rim :, :]
    states_copy.wait()
    picked_ref[...] = mm(here_ref[...], hot_ref[rim : extent - rim, :]).astype(BF16)
    cells_copy.wait()
    for c in range(number):
        here = slice(c * nodes, (c + 1) * nodes)
        wide_ref[:width, here] = mm(hot_ref[:width, here], cells_out_ref[c]).astype(BF16)
        wide_ref[width:, here] = mm(hot_ref[extent - width :, here], cells_out_ref[c]).astype(BF16)


def first_zone_body(states_ref, halo_a_ref, halo_b_ref, potential_ref, outer_ref, wide_ref, owned_ref,
                    inner_ref, zone_ref, shift_inner_ref, shift_zone_ref, picked_ref, sums_ref, give_a_ref, give_b_ref):
    count, owned = states_ref.shape
    rim = halo_a_ref.shape[1]
    width = 2 * rim
    low, high = sort_out(halo_a_ref[...], halo_b_ref[...])
    zone_ref[:, :rim] = low[:count].astype(BF16)
    zone_ref[:, rim:width] = states_ref[:, :rim]
    zone_ref[:, width : width + rim] = states_ref[:, owned - rim :]
    zone_ref[:, width + rim :] = high[:count].astype(BF16)
    inner_ref[...] = states_ref[:, rim : owned - rim]
    row = potential_ref[...] - spectrum_center
    shift_inner_ref[...] = row[:, rim : owned - rim]
    shift_zone_ref[:, rim:width] = row[:, :rim]
    shift_zone_ref[:, width : width + rim] = row[:, owned - rim :]
    for got, at in ((low, 0), (high, width + rim)):
        part = got[count : count + 8]
        shift_zone_ref[:, at : at + rim] = (part[0:1] + part[1:2] + part[2:3]) - spectrum_center
    picked = (
        owned_ref[...].astype(F32)
        + mm(jnp.concatenate([zone_ref[:, :rim], zone_ref[:, width + rim :]], axis=1), outer_ref[...])
    ).astype(BF16)
    picked_ref[...] = picked
    sums = mm_nt(picked, wide_ref[...])
    sums_ref[...] = sums
    hand_out(sums[:, :width], sums[:, width:], give_a_ref, give_b_ref)


def take_diagonal(rows, start, matrix_ref, diagonal_ref, at):
    size = rows.shape[0]
    same = lax.broadcasted_iota(jnp.int32, (size, size), 0) == lax.broadcasted_iota(
        jnp.int32, (size, size), 1
    )
    square = rows[:, at : at + size]
    diagonal_ref[:, at : at + size] = jnp.sum(jnp.where(same, square, 0.0), axis=0, keepdims=True)
    matrix_ref[start : start + size, :] = rows.astype(BF16)
    matrix_ref[start : start + size, at : at + size] = jnp.where(same, 0.0, square).astype(BF16)


def first_inner_body(inner_ref, picked_ref, shift_inner_ref, hot_ref, wide_ref, cells_ref,
                     next_ref, wide_inner_ref, border_ref, diagonal_ref, part_ref, next_picked_ref, columns_ref):
    extent = hot_ref.shape[0]
    width = border_ref.shape[1] // 2
    inside = slice(width, extent - width)
    number, nodes, _ = cells_ref.shape
    for c in range(number):
        here = slice(c * nodes, (c + 1) * nodes)
        wide_inner_ref[:, here] = mm(hot_ref[inside, here], cells_ref[c]).astype(BF16)
    value = mm_nt(picked_ref[...], wide_inner_ref[...]) + shift_inner_ref[...] * inner_ref[...].astype(F32)
    next_ref[...] = (value * (1.0 / spectrum_half)).astype(BF16)
    columns_ref[:width, :] = hot_ref[:width, :]
    columns_ref[width:, :] = hot_ref[extent - width :, :]
    for at in (0, width):
        rows = mm_nt(wide_ref[at : at + width, :], columns_ref[...])
        take_diagonal(rows, at, border_ref, diagonal_ref, at)
    next_picked_ref[...] = mm(next_ref[...], hot_ref[inside, :]).astype(BF16)
    part_ref[...] = mm_nt(next_picked_ref[...], wide_ref[...])


def close_zones(sums_ref, got_a_ref, got_b_ref, shift_zone_ref, mid_ref, old_ref, scale, zone_ref):
    width = got_a_ref.shape[1]
    low, high = sort_out(got_a_ref[...], got_b_ref[...])
    for got, here in ((low, slice(0, width)), (high, slice(width, 2 * width))):
        value = sums_ref[:, here] + got + shift_zone_ref[:, here] * mid_ref[:, here].astype(F32)
        value = value * scale
        if old_ref is not None:
            value = value - old_ref[:, here].astype(F32)
        zone_ref[:, here] = value.astype(BF16)


def zone_sums(zone_ref, part, border_ref, border_diagonal_ref):
    width = zone_ref.shape[1] // 2
    sums = part + mm(zone_ref[...], border_ref[...]) + border_diagonal_ref[...] * zone_ref[...].astype(F32)
    return sums[:, :width], sums[:, width:]


def zone_body(has_old, scale, sums_ref, got_a_ref, got_b_ref, shift_zone_ref, mid_ref, *rest):
    old_ref, rest = (rest[0], rest[1:]) if has_old else (None, rest)
    part_ref, border_ref, border_diagonal_ref, zone_ref, next_sums_ref, give_a_ref, give_b_ref = rest
    close_zones(sums_ref, got_a_ref, got_b_ref, shift_zone_ref, mid_ref, old_ref, scale, zone_ref)
    low, high = zone_sums(zone_ref, part_ref[...], border_ref, border_diagonal_ref)
    width = low.shape[1]
    next_sums_ref[:, :width] = low
    next_sums_ref[:, width:] = high
    hand_out(low, high, give_a_ref, give_b_ref)


def inner_sums(zone_ref, inner_ref, columns_ref, square_ref, diagonal_ref):
    return (
        mm_nt(zone_ref[...], columns_ref[...])
        + mm(inner_ref[...], square_ref[...])
        + diagonal_ref[...] * inner_ref[...].astype(F32)
    )


def second_inner_body(zone_ref, inner_ref, old_ref, shift_inner_ref, picked_ref, hot_ref, wide_inner_ref,
                      next_ref, part_ref, columns_ref, square_ref, diagonal_ref, zone_hot_ref):
    extent = hot_ref.shape[0]
    width = zone_ref.shape[1] // 2
    zone_hot_ref[:width, :] = hot_ref[:width, :]
    zone_hot_ref[width:, :] = hot_ref[extent - width :, :]
    columns_ref[...] = mm_nt(wide_inner_ref[...], zone_hot_ref[...]).astype(BF16)
    picked = (picked_ref[...].astype(F32) + mm(zone_ref[...], zone_hot_ref[...])).astype(BF16)
    sums = mm_nt(picked, wide_inner_ref[...])
    value = (sums + shift_inner_ref[...] * inner_ref[...].astype(F32)) * (2.0 / spectrum_half)
    next_ref[...] = (value - old_ref[...].astype(F32)).astype(BF16)
    part_ref[...] = mm(next_ref[...], columns_ref[...])
    rows = mm_nt(wide_inner_ref[: square_ref.shape[0], :], hot_ref[width : extent - width, :])
    diagonal_ref[...] = jnp.zeros_like(diagonal_ref)
    take_diagonal(rows, 0, square_ref, diagonal_ref, 0)


def third_inner_body(zone_ref, inner_ref, old_ref, shift_inner_ref, columns_ref, begun_ref, begun_diagonal_ref,
                     hot_ref, wide_inner_ref, square_ref, diagonal_ref, next_ref, part_ref, open_ref):
    size, step = square_ref.shape[0], begun_ref.shape[0]
    width = (hot_ref.shape[0] - size) // 2
    square_ref[:step, :] = begun_ref[...]
    diagonal_ref[...] = begun_diagonal_ref[...]
    for start in range(step, size, step):
        rows = mm_nt(wide_inner_ref[start : start + step, :], hot_ref[width : width + size, :])
        take_diagonal(rows, start, square_ref, diagonal_ref, start)
    line = diagonal_ref[...] + shift_inner_ref[...]
    sums = (
        mm_nt(zone_ref[...], columns_ref[...])
        + mm(inner_ref[...], square_ref[...])
        + line * inner_ref[...].astype(F32)
    )
    next_ref[...] = (sums * (2.0 / spectrum_half) - old_ref[...].astype(F32)).astype(BF16)
    part_ref[...] = mm(next_ref[...], columns_ref[...])
    open_ref[...] = mm(next_ref[...], square_ref[...]) + line * next_ref[...].astype(F32)


def last_inner_body(zone_ref, open_ref, old_ref, columns_ref, next_ref):
    sums = open_ref[...] + mm_nt(zone_ref[...], columns_ref[...])
    value = sums * (2.0 / spectrum_half) - old_ref[...].astype(F32)
    next_ref[...] = value.astype(BF16)


def last_zone_body(sums_ref, got_a_ref, got_b_ref, shift_zone_ref, mid_ref, old_ref, zone_ref):
    close_zones(sums_ref, got_a_ref, got_b_ref, shift_zone_ref, mid_ref, old_ref,
                2.0 / spectrum_half, zone_ref)


def zone_energy(zone_ref, part, shift_zone_ref, border_ref, border_diagonal_ref, energy_ref):
    low, high = zone_sums(zone_ref, part, border_ref, border_diagonal_ref)
    width = low.shape[1]
    rim = width // 2
    own = (shift_zone_ref[:, rim : width + rim] + spectrum_center) * zone_ref[:, rim : width + rim].astype(F32)
    energy_ref[:, :rim] = low[:, :rim].astype(energy_ref.dtype)
    energy_ref[:, rim:width] = (low[:, rim:] + own[:, :rim]).astype(energy_ref.dtype)
    energy_ref[:, width : width + rim] = (high[:, :rim] + own[:, rim:]).astype(energy_ref.dtype)
    energy_ref[:, width + rim :] = high[:, rim:].astype(energy_ref.dtype)


def energy_body(zone_ref, inner_ref, shift_inner_ref, shift_zone_ref,
                border_ref, border_diagonal_ref, columns_ref, square_ref, diagonal_ref, energy_ref, energy_zone_ref, filtered_ref):
    sums = inner_sums(zone_ref, inner_ref, columns_ref, square_ref, diagonal_ref)
    own = (shift_inner_ref[...] + spectrum_center) * inner_ref[...].astype(F32)
    energy_ref[...] = (sums + own).astype(BF16)
    width = zone_ref.shape[1] // 2
    part = mm(inner_ref[...], columns_ref[...])
    zone_energy(zone_ref, part, shift_zone_ref, border_ref, border_diagonal_ref, energy_zone_ref)
    rim = width // 2
    owned = filtered_ref.shape[1]
    filtered_ref[:, :rim] = zone_ref[:, rim:width]
    filtered_ref[:, rim : owned - rim] = inner_ref[...]
    filtered_ref[:, owned - rim :] = zone_ref[:, width : width + rim]


def by_core(first_ref, second_ref):
    odd, first, second = is_odd(), first_ref[...], second_ref[...]
    return jnp.where(odd, second, first), jnp.where(odd, first, second)


def neighbour_body(inner_ref, first_ref, second_ref, energy_ref, shift_inner_ref, columns_ref, square_ref, diagonal_ref,
                   part_ref, found_ref, other_ref, other_energy_ref, toward_ref):
    beside, across = by_core(first_ref, second_ref)
    line = diagonal_ref[...] + (shift_inner_ref[...] + spectrum_center)
    energy = (mm(beside, square_ref[...]) + line * beside.astype(F32)).astype(BF16)
    part_ref[...] = mm(beside, columns_ref[...])
    toward_ref[...] = mm(across, columns_ref[...]).astype(BF16)
    inner_found(found_ref, (inner_ref[...], beside, across), inner_ref, energy_ref)
    other_ref[...] = mm_nt(across, beside)
    other_energy_ref[...] = mm_nt(across, energy)


def inner_found(found_ref, blocks, states_ref, energy_ref):
    count = states_ref.shape[0]
    for place, block in enumerate(blocks):
        here = slice(place * count, (place + 1) * count)
        found_ref[here, :count] = mm_nt(block, states_ref[...])
        found_ref[here, count:] = mm_nt(block, energy_ref[...])


def gram_body(*refs):
    *blocks, energy_ref, found_ref = refs
    inner_found(found_ref, [block[...] for block in blocks], blocks[0], energy_ref)


def zone_found(block_ref, zone_ref, energy_zone_ref):
    rim = zone_ref.shape[1] // 4
    here = slice(rim, 3 * rim)
    return mm_nt(block_ref[:, here], zone_ref[:, here]), mm_nt(block_ref[...], energy_zone_ref[...])


def project_body(square_of_four, scale, energy_zone_ref, found_ref, *refs):
    if square_of_four:
        (part_ref, other_ref, other_energy_ref, toward_ref, shift_zone_ref, border_ref, border_diagonal_ref), refs = refs[:7], refs[7:]
        *zones, out_ref, give_ref, other_zone_ref, beside_ref, across_ref = refs
        beside_ref[...], across_ref[...] = by_core(zones[1], zones[2])
        zones = [zones[0], beside_ref, across_ref]
    else:
        *zones, out_ref, give_ref = refs
    count = energy_zone_ref.shape[0]
    columns = out_ref.shape[2] // 2
    group = lax.axis_index("state")
    odd = is_odd()

    def put(distance, states, energy):
        at = group ^ distance
        for block, there in ((states * scale, slice(0, columns)), (energy * scale, slice(columns, 2 * columns))):
            parts = [block[:columns], block[columns:]]
            for core in range(2):
                out_ref[at, core, there] = parts[core].astype(BF16)
            if not square_of_four:
                give_ref[at, there] = jnp.where(odd, parts[0], parts[1]).astype(BF16)

    if square_of_four:
        zone_energy(zones[1], part_ref[...], shift_zone_ref, border_ref, border_diagonal_ref, other_zone_ref)
    for distance, zone in enumerate(zones):
        here = slice(distance * count, (distance + 1) * count)
        states, energy = zone_found(zone, zones[0], energy_zone_ref)
        put(distance, found_ref[here, :count] + states, found_ref[here, count:] + energy)
    if square_of_four:
        states, energy = zone_found(zones[2], zones[1], other_zone_ref)
        energy = energy + mm_nt(toward_ref[...], zones[1][...])
        put(3, other_ref[...] + states, other_energy_ref[...] + energy)
        for order, (even, uneven) in enumerate(CORE_WAYS):
            give_ref[order] = out_ref[chip_at(jnp.where(odd, even, uneven))]


CORE_WAYS = ((1, 3), (0, 2))


def chip_at(distance):
    return (lax.axis_index("space") >> 1) ^ distance


def split_body(mine_ref, got_ref, *pieces):
    odd = is_odd()
    for order, (even, uneven) in enumerate(CORE_WAYS):
        block = mine_ref[chip_at(jnp.where(odd, uneven, even))].astype(F32)
        pieces[order][...] = (block + got_ref[order].astype(F32)).astype(BF16)


def gather_body(mine_ref, first_ref, second_ref, keep_ref, give_ref):
    odd = is_odd()
    made_elsewhere = jnp.logical_or(odd, chip_at(0) == (lax.axis_index("state") ^ 3))
    second = jnp.where(made_elsewhere, second_ref[...].astype(F32), mine_ref[...].astype(F32))
    total = first_ref[...].astype(F32) + second
    keep_ref[...] = jnp.where(odd, total[1], total[0])
    give_ref[...] = jnp.where(odd, total[0], total[1]).astype(BF16)


def join_body(keep_ref, got_ref, first_ref, second_ref):
    total = keep_ref[...] + got_ref[...].astype(F32)
    columns = first_ref.shape[0]
    first_ref[...] = total[:columns]
    second_ref[...] = total[columns:]


def halve_body(mine_ref, got_ref, *pieces):
    for distance, piece_ref in enumerate(pieces):
        chip = (lax.axis_index("space") >> 1) ^ distance
        total = mine_ref[chip, lax.axis_index("space") & 1].astype(F32) + got_ref[chip].astype(F32)
        piece_ref[...] = total.astype(BF16)


def final_body(mine_ref, *refs):
    parts, (first_ref, second_ref) = refs[:-2], refs[-2:]
    total = mine_ref[...].astype(F32)
    for part in parts:
        total = total + part[...].astype(F32)
    columns = first_ref.shape[0]
    first_ref[...] = total[:columns]
    second_ref[...] = total[columns:]


def swap(block, n_state, n_space, lead):
    route = []
    for s in range(n_state):
        for i in range(n_space):
            j = i + 1 if (i - lead) % 2 == 0 else i - 1
            if 0 <= j < n_space:
                route.append((s * n_space + i, s * n_space + j))
            elif (s ^ 1) < n_state:
                route.append((s * n_space + i, (s ^ 1) * n_space + i))
    return lax.ppermute(block, ("state", "space"), route)


def exchange(give_a, give_b, n_state, n_space):
    got_a = swap(give_a, n_state, n_space, 0)
    got_b = swap(give_b, n_state, n_space, 1)
    return got_a, got_b


def across(block, axis, distance):
    return lax.ppermute(block, axis, [(i, i ^ distance) for i in range(lax.axis_size(axis))])


def beside(block, first, n_state, n_space):
    route = []
    for s in range(n_state):
        for i in range(n_space):
            distance = 1 if first == (i & 1 == 0) else 2
            route.append((s * n_space + i, (s ^ distance) * n_space + i))
    return lax.ppermute(block, ("state", "space"), route)


def share_out(block, order, n_state, n_space):
    route = []
    for s in range(n_state):
        for i in range(n_space):
            distance = CORE_WAYS[order][i & 1]
            to_group, to_chip = s, (i >> 1) ^ distance
            if distance == 0 or to_chip == s ^ 3:
                to_group, to_chip = s ^ 1, to_chip ^ 1
            route.append((s * n_space + i, to_group * n_space + 2 * to_chip + (i & 1)))
    return lax.ppermute(block, ("state", "space"), route)


def program(states_in, cell_matrices, connectivity, potential):
    count, owned = states_in.shape
    cells, nodes, _ = cell_matrices.shape
    rim = nodes // 4
    extent, inside = owned + 2 * rim, owned - 2 * rim
    n_state, n_space = lax.axis_size("state"), lax.axis_size("space")
    row = potential.reshape(1, owned)
    work = 2 * count * extent * extent
    inner = SHAPE((count, inside), BF16)
    zone, sums_of = SHAPE((count, 4 * rim), BF16), SHAPE((count, 4 * rim), F32)
    give = SHAPE((count, 2 * rim), BF16)

    halo = SHAPE((count + 16, rim), BF16)
    *gave, row, local = call(
        halo_body,
        (halo, halo, SHAPE(row.shape, F32), SHAPE(connectivity.shape, connectivity.dtype)),
        (states_in, row, connectivity), 0, raw=(0, 1, 2),
        scratch=[
            pltpu.VMEM((count, rim), BF16), pltpu.VMEM((count, rim), BF16), pltpu.SemaphoreType.DMA((4,)),
        ],
    )
    got = exchange(*gave, n_state, n_space)
    table = SHAPE((extent, cells * nodes), BF16)
    hot, outer, wide, picked, states_here, cells_here = call(
        spread_body,
        (table, SHAPE((2 * rim, cells * nodes), BF16), SHAPE((4 * rim, cells * nodes), BF16),
         SHAPE((count, cells * nodes), BF16), SHAPE(states_in.shape, BF16), SHAPE(cell_matrices.shape, BF16)),
        (local, states_in, cell_matrices), work, raw=(1, 2), scratch=[pltpu.SemaphoreType.DMA((2,))],
    )
    border_line, line = SHAPE((1, 4 * rim), F32), SHAPE((1, inside), F32)
    inner_0, zone_0, shift_inner, shift_zone, picked, sums, *gave = call(
        first_zone_body,
        (inner, zone, line, border_line, SHAPE((count, cells * nodes), BF16), sums_of, give, give),
        (states_here, *got, row, outer, wide, picked), work,
    )
    got = exchange(*gave, n_state, n_space)
    inner_1, wide_inner, border, border_diagonal, partial, picked = call(
        first_inner_body,
        (inner, SHAPE((inside, cells * nodes), BF16), SHAPE((4 * rim, 4 * rim), BF16), border_line, sums_of,
         SHAPE((count, cells * nodes), BF16)),
        (inner_0, picked, shift_inner, hot, wide, cells_here), 8 * extent * rim * cells * nodes,
        scratch=[pltpu.VMEM((4 * rim, cells * nodes), BF16)],
    )
    inners, zones = [inner_0, inner_1], [zone_0]
    for k in range(1, DEGREE):
        older = zones[-2:-1]
        scale = (2.0 if older else 1.0) / spectrum_half
        zone_k, sums, *gave = call(
            functools.partial(zone_body, bool(older), scale),
            (zone, sums_of, give, give),
            (sums, *got, shift_zone, zones[-1], *older, partial, border, border_diagonal), work // 6,
        )
        zones.append(zone_k)
        got = exchange(*gave, n_state, n_space)
        ins = (zone_k, inners[-1], inners[-2], shift_inner)
        if k == 1:
            inner_k, partial, columns, begun, begun_diagonal = call(
                second_inner_body,
                (inner, sums_of, SHAPE((inside, 4 * rim), BF16), SHAPE((2 * rim, inside), BF16), line),
                (*ins, picked, hot, wide_inner), 4 * extent * rim * cells * nodes,
                scratch=[pltpu.VMEM((4 * rim, cells * nodes), BF16)],
            )
        elif k == 2:
            square, diagonal, inner_k, partial, opened = call(
                third_inner_body,
                (SHAPE((inside, inside), BF16), line, inner, sums_of, SHAPE((count, inside), F32)),
                (*ins, columns, begun, begun_diagonal, hot, wide_inner), 4 * extent * rim * cells * nodes,
            )
        else:
            inner_k = call(last_inner_body, inner, (zone_k, opened, inners[-2], columns), work // 4)
        inners.append(inner_k)
    square_of_four = four(n_state, n_space)
    if square_of_four:
        inner_blocks = [inner_k] + [beside(inner_k, first, n_state, n_space) for first in (True, False)]
    else:
        inner_blocks = [inner_k] + [across(inner_k, "state", d) for d in range(1, n_state)]
    zone_k = call(
        last_zone_body, zone, (sums, *got, shift_zone, zones[-1], zones[-2]), 0
    )
    if square_of_four:
        zone_blocks = [zone_k] + [beside(zone_k, first, n_state, n_space) for first in (True, False)]
    else:
        zone_blocks = [zone_k] + [across(zone_k, "state", d) for d in range(1, n_state)]
    energy, energy_zone, filtered = call(
        energy_body, (inner, zone, SHAPE((count, owned), BF16)),
        (zone_k, inner_k, shift_inner, shift_zone, border, border_diagonal, columns, square, diagonal), work,
    )
    extra, scratch = (), []
    pair_of = SHAPE((count, count), F32)
    found_of = SHAPE((len(inner_blocks) * count, 2 * count), F32)
    if square_of_four:
        part_x, found, *other = call(
            neighbour_body, (sums_of, found_of, pair_of, pair_of, zone),
            (*inner_blocks, energy, shift_inner, columns, square, diagonal), work // 2,
        )
        extra = (part_x, *other, shift_zone, border, border_diagonal)
        scratch = [pltpu.VMEM((count, 4 * rim), BF16)] * 3
    else:
        found = call(gram_body, found_of, (*inner_blocks, energy), work)
    share = count * n_state // n_space
    chips = n_space // 2
    turned = SHAPE((share, count), F32)
    piece = SHAPE((2 * share, count), BF16)
    both_halves = SHAPE((2, 2 * share, count), BF16)
    mine, give_half = call(
        functools.partial(project_body, square_of_four, 1.0 / (owned * n_space)),
        (SHAPE((chips, 2, 2 * share, count), BF16),
         SHAPE((2, 2, 2 * share, count) if square_of_four else (chips, 2 * share, count), BF16)),
        (energy_zone, found, *extra, *zone_blocks), work // 4, scratch=scratch,
    )
    got_half = swap(give_half, n_state, n_space, 0)
    if square_of_four:
        pieces = call(split_body, (both_halves,) * 2, (mine, got_half), 0)
        shares = [share_out(p, order, n_state, n_space) for order, p in enumerate(pieces)]
        keep, give_last = call(
            gather_body, (SHAPE(piece.shape, F32), piece), (pieces[1], *shares), 0
        )
        got_last = swap(give_last, n_state, n_space, 0)
        intersection, projected = call(join_body, (turned, turned), (keep, got_last), 0)
    else:
        pieces = call(halve_body, (piece,) * chips, (mine, got_half), 0)
        shares = [across(p, "space", 2 * d) for d, p in enumerate(pieces) if d]
        intersection, projected = call(final_body, (turned, turned), (pieces[0], *shares), 0)
    return filtered, intersection.T, projected.T


def four(n_state, n_space):
    return n_state == 4 and n_space == 8


def solution(mesh):
    return jax.shard_map(
        program,
        mesh=mesh,
        in_specs=(P("state", "space"), P("space", None, None), P("space", None), P("space")),
        out_specs=(P("state", "space"), P("state", "space"), P("state", "space")),
        check_vma=False,
    )
```

```python
import functools

import jax
import jax.numpy as jnp
from jax import lax
from jax.experimental import pallas as pl
from jax.experimental.pallas import tpu as pltpu
from jax.sharding import PartitionSpec as P


DEGREE = 4

spectrum_center = 3.0
spectrum_half = 3.5

BF16 = jnp.bfloat16
F32 = jnp.float32
SHAPE = jax.ShapeDtypeStruct


def call(body, outs, ins, flops, scratch=(), raw=()):
    where = [
        pl.BlockSpec(memory_space=pltpu.HBM if i in raw else pltpu.VMEM) for i in range(len(ins))
    ]
    ins = [pltpu.with_memory_space_constraint(x, pltpu.HBM) if i in raw else x for i, x in enumerate(ins)]
    return pl.pallas_call(
        body,
        out_shape=outs,
        in_specs=where,
        out_specs=jax.tree.map(lambda _: pl.BlockSpec(memory_space=pltpu.VMEM), outs),
        scratch_shapes=list(scratch),
        compiler_params=pltpu.CompilerParams(vmem_limit_bytes=24 << 20),
        cost_estimate=pl.CostEstimate(flops=flops, bytes_accessed=4 << 20, transcendentals=0),
    )(*ins)


def mm(a, b):
    return jnp.dot(a, b, preferred_element_type=F32)


def mm_nt(a, b):
    return lax.dot_general(a, b, (((1,), (1,)), ((), ())), preferred_element_type=F32)


def is_odd():
    return (lax.axis_index("space") & 1) == 1


def sort_out(got_a, got_b):
    me, odd = lax.axis_index("space"), is_odd()
    got_a, got_b = got_a.astype(F32), got_b.astype(F32)
    low = jnp.where(me == 0, 0.0, jnp.where(odd, got_a, got_b))
    high = jnp.where(me == lax.axis_size("space") - 1, 0.0, jnp.where(odd, got_b, got_a))
    return low, high


def hand_out(low, high, give_a_ref, give_b_ref):
    odd = is_odd()
    give_a_ref[...] = jnp.where(odd, low, high).astype(give_a_ref.dtype)
    give_b_ref[...] = jnp.where(odd, high, low).astype(give_b_ref.dtype)


def halo_body(states_ref, potential_ref, index_ref,
              give_a_ref, give_b_ref, row_ref, local_ref, low_ref, high_ref, sem):
    count, owned = states_ref.shape
    rim = low_ref.shape[1]
    copies = [
        pltpu.make_async_copy(states_ref.at[:, pl.ds(0, rim)], low_ref, sem.at[0]),
        pltpu.make_async_copy(states_ref.at[:, pl.ds(owned - rim, rim)], high_ref, sem.at[1]),
        pltpu.make_async_copy(potential_ref, row_ref, sem.at[2]),
        pltpu.make_async_copy(index_ref, local_ref, sem.at[3]),
    ]
    for copy in copies:
        copy.start()
    for copy in copies:
        copy.wait()
    odd = is_odd()
    low, high = low_ref[...].astype(F32), high_ref[...].astype(F32)
    give_a_ref[:count, :] = jnp.where(odd, low, high).astype(BF16)
    give_b_ref[:count, :] = jnp.where(odd, high, low).astype(BF16)
    for take, give_ref in ((odd, give_a_ref), (jnp.logical_not(odd), give_b_ref)):
        row = jnp.where(take, row_ref[:, :rim], row_ref[:, owned - rim :])
        row = jnp.broadcast_to(row, (16, rim))
        at = lax.broadcasted_iota(jnp.int32, row.shape, 0)
        first = row.astype(BF16).astype(F32)
        second = (row - first).astype(BF16).astype(F32)
        third = (row - first) - second
        give_ref[count:, :] = jnp.where(
            at == 0, first, jnp.where(at == 1, second, jnp.where(at == 2, third, 0.0))
        ).astype(BF16)


def spread_body(index_ref, states_ref, cells_ref,
                hot_ref, outer_ref, wide_ref, picked_ref, here_ref, cells_out_ref, sem):
    states_copy = pltpu.make_async_copy(states_ref, here_ref, sem.at[0])
    cells_copy = pltpu.make_async_copy(cells_ref, cells_out_ref, sem.at[1])
    states_copy.start()
    cells_copy.start()
    number, nodes, _ = cells_ref.shape
    extent = hot_ref.shape[0]
    rim = nodes // 4
    width = 2 * rim
    offset = lax.axis_index("space") * (extent - width) - rim
    for c in range(number):
        index = index_ref[c : c + 1, :] - offset
        hot = lax.broadcasted_iota(jnp.int32, (extent, nodes), 0) == index
        hot_ref[:, c * nodes : (c + 1) * nodes] = hot.astype(BF16)
    outer_ref[:rim, :] = hot_ref[:rim, :]
    outer_ref[rim:, :] = hot_ref[extent - rim :, :]
    states_copy.wait()
    picked_ref[...] = mm(here_ref[...], hot_ref[rim : extent - rim, :]).astype(BF16)
    cells_copy.wait()
    for c in range(number):
        here = slice(c * nodes, (c + 1) * nodes)
        wide_ref[:width, here] = mm(hot_ref[:width, here], cells_out_ref[c]).astype(BF16)
        wide_ref[width:, here] = mm(hot_ref[extent - width :, here], cells_out_ref[c]).astype(BF16)


def first_zone_body(states_ref, halo_a_ref, halo_b_ref, potential_ref, outer_ref, wide_ref, owned_ref,
                    inner_ref, zone_ref, shift_inner_ref, shift_zone_ref, picked_ref, sums_ref, give_a_ref, give_b_ref):
    count, owned = states_ref.shape
    rim = halo_a_ref.shape[1]
    width = 2 * rim
    low, high = sort_out(halo_a_ref[...], halo_b_ref[...])
    zone_ref[:, :rim] = low[:count].astype(BF16)
    zone_ref[:, rim:width] = states_ref[:, :rim]
    zone_ref[:, width : width + rim] = states_ref[:, owned - rim :]
    zone_ref[:, width + rim :] = high[:count].astype(BF16)
    inner_ref[...] = states_ref[:, rim : owned - rim]
    row = potential_ref[...] - spectrum_center
    shift_inner_ref[...] = row[:, rim : owned - rim]
    shift_zone_ref[:, rim:width] = row[:, :rim]
    shift_zone_ref[:, width : width + rim] = row[:, owned - rim :]
    for got, at in ((low, 0), (high, width + rim)):
        part = got[count : count + 8]
        shift_zone_ref[:, at : at + rim] = (part[0:1] + part[1:2] + part[2:3]) - spectrum_center
    picked = (
        owned_ref[...].astype(F32)
        + mm(jnp.concatenate([zone_ref[:, :rim], zone_ref[:, width + rim :]], axis=1), outer_ref[...])
    ).astype(BF16)
    picked_ref[...] = picked
    sums = mm_nt(picked, wide_ref[...])
    sums_ref[...] = sums
    hand_out(sums[:, :width], sums[:, width:], give_a_ref, give_b_ref)


def take_diagonal(rows, start, matrix_ref, diagonal_ref, at):
    size = rows.shape[0]
    same = lax.broadcasted_iota(jnp.int32, (size, size), 0) == lax.broadcasted_iota(
        jnp.int32, (size, size), 1
    )
    square = rows[:, at : at + size]
    diagonal_ref[:, at : at + size] = jnp.sum(jnp.where(same, square, 0.0), axis=0, keepdims=True)
    matrix_ref[start : start + size, :] = rows.astype(BF16)
    matrix_ref[start : start + size, at : at + size] = jnp.where(same, 0.0, square).astype(BF16)


def first_inner_body(inner_ref, picked_ref, shift_inner_ref, hot_ref, wide_ref, cells_ref,
                     next_ref, wide_inner_ref, border_ref, diagonal_ref, part_ref, next_picked_ref, columns_ref):
    extent = hot_ref.shape[0]
    width = border_ref.shape[1] // 2
    inside = slice(width, extent - width)
    number, nodes, _ = cells_ref.shape
    for c in range(number):
        here = slice(c * nodes, (c + 1) * nodes)
        wide_inner_ref[:, here] = mm(hot_ref[inside, here], cells_ref[c]).astype(BF16)
    value = mm_nt(picked_ref[...], wide_inner_ref[...]) + shift_inner_ref[...] * inner_ref[...].astype(F32)
    next_ref[...] = (value * (1.0 / spectrum_half)).astype(BF16)
    columns_ref[:width, :] = hot_ref[:width, :]
    columns_ref[width:, :] = hot_ref[extent - width :, :]
    for at in (0, width):
        rows = mm_nt(wide_ref[at : at + width, :], columns_ref[...])
        take_diagonal(rows, at, border_ref, diagonal_ref, at)
    next_picked_ref[...] = mm(next_ref[...], hot_ref[inside, :]).astype(BF16)
    part_ref[...] = mm_nt(next_picked_ref[...], wide_ref[...])


def close_zones(sums_ref, got_a_ref, got_b_ref, shift_zone_ref, mid_ref, old_ref, scale, zone_ref):
    width = got_a_ref.shape[1]
    low, high = sort_out(got_a_ref[...], got_b_ref[...])
    for got, here in ((low, slice(0, width)), (high, slice(width, 2 * width))):
        value = sums_ref[:, here] + got + shift_zone_ref[:, here] * mid_ref[:, here].astype(F32)
        value = value * scale
        if old_ref is not None:
            value = value - old_ref[:, here].astype(F32)
        zone_ref[:, here] = value.astype(BF16)


def zone_sums(zone_ref, part, border_ref, border_diagonal_ref):
    width = zone_ref.shape[1] // 2
    sums = part + mm(zone_ref[...], border_ref[...]) + border_diagonal_ref[...] * zone_ref[...].astype(F32)
    return sums[:, :width], sums[:, width:]


def zone_body(has_old, scale, sums_ref, got_a_ref, got_b_ref, shift_zone_ref, mid_ref, *rest):
    old_ref, rest = (rest[0], rest[1:]) if has_old else (None, rest)
    part_ref, border_ref, border_diagonal_ref, zone_ref, next_sums_ref, give_a_ref, give_b_ref = rest
    close_zones(sums_ref, got_a_ref, got_b_ref, shift_zone_ref, mid_ref, old_ref, scale, zone_ref)
    low, high = zone_sums(zone_ref, part_ref[...], border_ref, border_diagonal_ref)
    width = low.shape[1]
    next_sums_ref[:, :width] = low
    next_sums_ref[:, width:] = high
    hand_out(low, high, give_a_ref, give_b_ref)


def inner_sums(zone_ref, inner_ref, columns_ref, square_ref, diagonal_ref):
    return (
        mm_nt(zone_ref[...], columns_ref[...])
        + mm(inner_ref[...], square_ref[...])
        + diagonal_ref[...] * inner_ref[...].astype(F32)
    )


def second_inner_body(zone_ref, inner_ref, old_ref, shift_inner_ref, picked_ref, hot_ref, wide_inner_ref,
                      next_ref, part_ref, columns_ref, square_ref, diagonal_ref, zone_hot_ref):
    extent = hot_ref.shape[0]
    width = zone_ref.shape[1] // 2
    zone_hot_ref[:width, :] = hot_ref[:width, :]
    zone_hot_ref[width:, :] = hot_ref[extent - width :, :]
    columns_ref[...] = mm_nt(wide_inner_ref[...], zone_hot_ref[...]).astype(BF16)
    picked = (picked_ref[...].astype(F32) + mm(zone_ref[...], zone_hot_ref[...])).astype(BF16)
    sums = mm_nt(picked, wide_inner_ref[...])
    value = (sums + shift_inner_ref[...] * inner_ref[...].astype(F32)) * (2.0 / spectrum_half)
    next_ref[...] = (value - old_ref[...].astype(F32)).astype(BF16)
    part_ref[...] = mm(next_ref[...], columns_ref[...])
    rows = mm_nt(wide_inner_ref[: square_ref.shape[0], :], hot_ref[width : extent - width, :])
    diagonal_ref[...] = jnp.zeros_like(diagonal_ref)
    take_diagonal(rows, 0, square_ref, diagonal_ref, 0)


def third_inner_body(zone_ref, inner_ref, old_ref, shift_inner_ref, columns_ref, begun_ref, begun_diagonal_ref,
                     hot_ref, wide_inner_ref, square_ref, diagonal_ref, next_ref, part_ref, open_ref):
    size, step = square_ref.shape[0], begun_ref.shape[0]
    width = (hot_ref.shape[0] - size) // 2
    square_ref[:step, :] = begun_ref[...]
    diagonal_ref[...] = begun_diagonal_ref[...]
    for start in range(step, size, step):
        rows = mm_nt(wide_inner_ref[start : start + step, :], hot_ref[width : width + size, :])
        take_diagonal(rows, start, square_ref, diagonal_ref, start)
    line = diagonal_ref[...] + shift_inner_ref[...]
    sums = (
        mm_nt(zone_ref[...], columns_ref[...])
        + mm(inner_ref[...], square_ref[...])
        + line * inner_ref[...].astype(F32)
    )
    next_ref[...] = (sums * (2.0 / spectrum_half) - old_ref[...].astype(F32)).astype(BF16)
    part_ref[...] = mm(next_ref[...], columns_ref[...])
    open_ref[...] = mm(next_ref[...], square_ref[...]) + line * next_ref[...].astype(F32)


def last_inner_body(zone_ref, open_ref, old_ref, columns_ref, next_ref):
    sums = open_ref[...] + mm_nt(zone_ref[...], columns_ref[...])
    value = sums * (2.0 / spectrum_half) - old_ref[...].astype(F32)
    next_ref[...] = value.astype(BF16)


def last_zone_body(sums_ref, got_a_ref, got_b_ref, shift_zone_ref, mid_ref, old_ref, zone_ref):
    close_zones(sums_ref, got_a_ref, got_b_ref, shift_zone_ref, mid_ref, old_ref,
                2.0 / spectrum_half, zone_ref)


def zone_energy(zone_ref, part, shift_zone_ref, border_ref, border_diagonal_ref, energy_ref):
    low, high = zone_sums(zone_ref, part, border_ref, border_diagonal_ref)
    width = low.shape[1]
    rim = width // 2
    own = (shift_zone_ref[:, rim : width + rim] + spectrum_center) * zone_ref[:, rim : width + rim].astype(F32)
    energy_ref[:, :rim] = low[:, :rim].astype(energy_ref.dtype)
    energy_ref[:, rim:width] = (low[:, rim:] + own[:, :rim]).astype(energy_ref.dtype)
    energy_ref[:, width : width + rim] = (high[:, :rim] + own[:, rim:]).astype(energy_ref.dtype)
    energy_ref[:, width + rim :] = high[:, rim:].astype(energy_ref.dtype)


def energy_body(zone_ref, inner_ref, shift_inner_ref, shift_zone_ref,
                border_ref, border_diagonal_ref, columns_ref, square_ref, diagonal_ref, energy_ref, energy_zone_ref, filtered_ref):
    sums = inner_sums(zone_ref, inner_ref, columns_ref, square_ref, diagonal_ref)
    own = (shift_inner_ref[...] + spectrum_center) * inner_ref[...].astype(F32)
    energy_ref[...] = (sums + own).astype(BF16)
    width = zone_ref.shape[1] // 2
    part = mm(inner_ref[...], columns_ref[...])
    zone_energy(zone_ref, part, shift_zone_ref, border_ref, border_diagonal_ref, energy_zone_ref)
    rim = width // 2
    owned = filtered_ref.shape[1]
    filtered_ref[:, :rim] = zone_ref[:, rim:width]
    filtered_ref[:, rim : owned - rim] = inner_ref[...]
    filtered_ref[:, owned - rim :] = zone_ref[:, width : width + rim]


def first_neighbour_body(inner_ref, first_ref, energy_ref, shift_inner_ref, columns_ref, square_ref, diagonal_ref,
                         first_energy_ref, part_ref, found_ref):
    first = first_ref[...]
    line = diagonal_ref[...] + (shift_inner_ref[...] + spectrum_center)
    first_energy_ref[...] = (mm(first, square_ref[...]) + line * first.astype(F32)).astype(BF16)
    part_ref[...] = mm(first, columns_ref[...])
    inner_found(found_ref, (inner_ref[...], first), inner_ref, energy_ref)


def turned(first, second):
    odd = is_odd()
    return mm_nt(jnp.where(odd, first, second), jnp.where(odd, second, first))


def second_neighbour_body(inner_ref, first_ref, second_ref, first_energy_ref, energy_ref, columns_ref,
                          found_ref, other_ref, other_energy_ref, toward_ref):
    second = second_ref[...]
    inner_found(found_ref, (second,), inner_ref, energy_ref)
    other_ref[...] = turned(first_ref[...], second)
    other_energy_ref[...] = turned(first_energy_ref[...], second)
    toward_ref[...] = mm(second, columns_ref[...]).astype(BF16)


def inner_found(found_ref, blocks, states_ref, energy_ref):
    count = states_ref.shape[0]
    for place, block in enumerate(blocks):
        here = slice(place * count, (place + 1) * count)
        found_ref[here, :count] = mm_nt(block, states_ref[...])
        found_ref[here, count:] = mm_nt(block, energy_ref[...])


def gram_body(*refs):
    *blocks, energy_ref, found_ref = refs
    inner_found(found_ref, [block[...] for block in blocks], blocks[0], energy_ref)


def zone_found(block_ref, zone_ref, energy_zone_ref):
    rim = zone_ref.shape[1] // 4
    here = slice(rim, 3 * rim)
    return mm_nt(block_ref[:, here], zone_ref[:, here]), mm_nt(block_ref[...], energy_zone_ref[...])


def project_body(square_of_four, scale, energy_zone_ref, found_ref, *refs):
    if square_of_four:
        (second_found_ref, part_ref, other_ref, other_energy_ref, toward_ref,
         shift_zone_ref, border_ref, border_diagonal_ref), refs = refs[:8], refs[8:]
        *zones, out_ref, give_ref, other_zone_ref = refs
    else:
        *zones, out_ref, give_ref = refs
    count = energy_zone_ref.shape[0]
    columns = out_ref.shape[2] // 2
    group = lax.axis_index("state")
    odd = is_odd()

    def put(distance, states, energy):
        at = group ^ distance
        for block, there in ((states * scale, slice(0, columns)), (energy * scale, slice(columns, 2 * columns))):
            parts = [block[:columns], block[columns:]]
            for core in range(2):
                out_ref[at, core, there] = parts[core].astype(BF16)
            if not square_of_four:
                give_ref[at, there] = jnp.where(odd, parts[0], parts[1]).astype(BF16)

    if square_of_four:
        zone_energy(zones[1], part_ref[...], shift_zone_ref, border_ref, border_diagonal_ref, other_zone_ref)
    for place, zone in enumerate(zones):
        distance, found, row = place, found_ref, place
        if square_of_four and place:
            distance = jnp.where(odd, 3 - place, place)
            if place == 2:
                found, row = second_found_ref, 0
        here = slice(row * count, (row + 1) * count)
        states, energy = zone_found(zone, zones[0], energy_zone_ref)
        put(distance, found[here, :count] + states, found[here, count:] + energy)
    if square_of_four:
        rim = zones[1].shape[1] // 4
        own = slice(rim, 3 * rim)
        states = turned(zones[1][:, own], zones[2][:, own])
        energy = turned(other_zone_ref[...], zones[2][...]) + turned(zones[1][...], toward_ref[...])
        put(3, other_ref[...] + states, other_energy_ref[...] + energy)
        for order, (even, uneven) in enumerate(CORE_WAYS):
            give_ref[order] = out_ref[chip_at(jnp.where(odd, even, uneven))]


CORE_WAYS = ((1, 3), (0, 2))


def chip_at(distance):
    return (lax.axis_index("space") >> 1) ^ distance


def split_body(mine_ref, got_ref, *pieces):
    odd = is_odd()
    for order, (even, uneven) in enumerate(CORE_WAYS):
        block = mine_ref[chip_at(jnp.where(odd, uneven, even))].astype(F32)
        pieces[order][...] = (block + got_ref[order].astype(F32)).astype(BF16)


def gather_body(mine_ref, first_ref, second_ref, keep_ref, give_ref):
    odd = is_odd()
    made_elsewhere = jnp.logical_or(odd, chip_at(0) == (lax.axis_index("state") ^ 3))
    second = jnp.where(made_elsewhere, second_ref[...].astype(F32), mine_ref[...].astype(F32))
    total = first_ref[...].astype(F32) + second
    keep_ref[...] = jnp.where(odd, total[1], total[0])
    give_ref[...] = jnp.where(odd, total[0], total[1]).astype(BF16)


def join_body(keep_ref, got_ref, first_ref, second_ref):
    total = keep_ref[...] + got_ref[...].astype(F32)
    columns = first_ref.shape[0]
    first_ref[...] = total[:columns]
    second_ref[...] = total[columns:]


def halve_body(mine_ref, got_ref, *pieces):
    for distance, piece_ref in enumerate(pieces):
        chip = (lax.axis_index("space") >> 1) ^ distance
        total = mine_ref[chip, lax.axis_index("space") & 1].astype(F32) + got_ref[chip].astype(F32)
        piece_ref[...] = total.astype(BF16)


def final_body(mine_ref, *refs):
    parts, (first_ref, second_ref) = refs[:-2], refs[-2:]
    total = mine_ref[...].astype(F32)
    for part in parts:
        total = total + part[...].astype(F32)
    columns = first_ref.shape[0]
    first_ref[...] = total[:columns]
    second_ref[...] = total[columns:]


def swap(block, n_state, n_space, lead):
    route = []
    for s in range(n_state):
        for i in range(n_space):
            j = i + 1 if (i - lead) % 2 == 0 else i - 1
            if 0 <= j < n_space:
                route.append((s * n_space + i, s * n_space + j))
            elif (s ^ 1) < n_state:
                route.append((s * n_space + i, (s ^ 1) * n_space + i))
    return lax.ppermute(block, ("state", "space"), route)


def exchange(give_a, give_b, n_state, n_space):
    got_a = swap(give_a, n_state, n_space, 0)
    got_b = swap(give_b, n_state, n_space, 1)
    return got_a, got_b


def across(block, axis, distance):
    return lax.ppermute(block, axis, [(i, i ^ distance) for i in range(lax.axis_size(axis))])


def beside(block, first, n_state, n_space):
    route = []
    for s in range(n_state):
        for i in range(n_space):
            distance = 1 if first == (i & 1 == 0) else 2
            route.append((s * n_space + i, (s ^ distance) * n_space + i))
    return lax.ppermute(block, ("state", "space"), route)


def share_out(block, order, n_state, n_space):
    route = []
    for s in range(n_state):
        for i in range(n_space):
            distance = CORE_WAYS[order][i & 1]
            to_group, to_chip = s, (i >> 1) ^ distance
            if distance == 0 or to_chip == s ^ 3:
                to_group, to_chip = s ^ 1, to_chip ^ 1
            route.append((s * n_space + i, to_group * n_space + 2 * to_chip + (i & 1)))
    return lax.ppermute(block, ("state", "space"), route)


def program(states_in, cell_matrices, connectivity, potential):
    count, owned = states_in.shape
    cells, nodes, _ = cell_matrices.shape
    rim = nodes // 4
    extent, inside = owned + 2 * rim, owned - 2 * rim
    n_state, n_space = lax.axis_size("state"), lax.axis_size("space")
    row = potential.reshape(1, owned)
    work = 2 * count * extent * extent
    inner = SHAPE((count, inside), BF16)
    zone, sums_of = SHAPE((count, 4 * rim), BF16), SHAPE((count, 4 * rim), F32)
    give = SHAPE((count, 2 * rim), BF16)

    halo = SHAPE((count + 16, rim), BF16)
    *gave, row, local = call(
        halo_body,
        (halo, halo, SHAPE(row.shape, F32), SHAPE(connectivity.shape, connectivity.dtype)),
        (states_in, row, connectivity), 0, raw=(0, 1, 2),
        scratch=[
            pltpu.VMEM((count, rim), BF16), pltpu.VMEM((count, rim), BF16), pltpu.SemaphoreType.DMA((4,)),
        ],
    )
    got = exchange(*gave, n_state, n_space)
    table = SHAPE((extent, cells * nodes), BF16)
    hot, outer, wide, picked, states_here, cells_here = call(
        spread_body,
        (table, SHAPE((2 * rim, cells * nodes), BF16), SHAPE((4 * rim, cells * nodes), BF16),
         SHAPE((count, cells * nodes), BF16), SHAPE(states_in.shape, BF16), SHAPE(cell_matrices.shape, BF16)),
        (local, states_in, cell_matrices), work, raw=(1, 2), scratch=[pltpu.SemaphoreType.DMA((2,))],
    )
    border_line, line = SHAPE((1, 4 * rim), F32), SHAPE((1, inside), F32)
    inner_0, zone_0, shift_inner, shift_zone, picked, sums, *gave = call(
        first_zone_body,
        (inner, zone, line, border_line, SHAPE((count, cells * nodes), BF16), sums_of, give, give),
        (states_here, *got, row, outer, wide, picked), work,
    )
    got = exchange(*gave, n_state, n_space)
    inner_1, wide_inner, border, border_diagonal, partial, picked = call(
        first_inner_body,
        (inner, SHAPE((inside, cells * nodes), BF16), SHAPE((4 * rim, 4 * rim), BF16), border_line, sums_of,
         SHAPE((count, cells * nodes), BF16)),
        (inner_0, picked, shift_inner, hot, wide, cells_here), 8 * extent * rim * cells * nodes,
        scratch=[pltpu.VMEM((4 * rim, cells * nodes), BF16)],
    )
    inners, zones = [inner_0, inner_1], [zone_0]
    for k in range(1, DEGREE):
        older = zones[-2:-1]
        scale = (2.0 if older else 1.0) / spectrum_half
        zone_k, sums, *gave = call(
            functools.partial(zone_body, bool(older), scale),
            (zone, sums_of, give, give),
            (sums, *got, shift_zone, zones[-1], *older, partial, border, border_diagonal), work // 6,
        )
        zones.append(zone_k)
        got = exchange(*gave, n_state, n_space)
        ins = (zone_k, inners[-1], inners[-2], shift_inner)
        if k == 1:
            inner_k, partial, columns, begun, begun_diagonal = call(
                second_inner_body,
                (inner, sums_of, SHAPE((inside, 4 * rim), BF16), SHAPE((2 * rim, inside), BF16), line),
                (*ins, picked, hot, wide_inner), 4 * extent * rim * cells * nodes,
                scratch=[pltpu.VMEM((4 * rim, cells * nodes), BF16)],
            )
        elif k == 2:
            square, diagonal, inner_k, partial, opened = call(
                third_inner_body,
                (SHAPE((inside, inside), BF16), line, inner, sums_of, SHAPE((count, inside), F32)),
                (*ins, columns, begun, begun_diagonal, hot, wide_inner), 4 * extent * rim * cells * nodes,
            )
        else:
            inner_k = call(last_inner_body, inner, (zone_k, opened, inners[-2], columns), work // 4)
        inners.append(inner_k)
    square_of_four = four(n_state, n_space)
    if square_of_four:
        inner_blocks = [inner_k] + [beside(inner_k, first, n_state, n_space) for first in (True, False)]
    else:
        inner_blocks = [inner_k] + [across(inner_k, "state", d) for d in range(1, n_state)]
    zone_k = call(
        last_zone_body, zone, (sums, *got, shift_zone, zones[-1], zones[-2]), 0
    )
    if square_of_four:
        zone_blocks = [zone_k] + [beside(zone_k, first, n_state, n_space) for first in (True, False)]
    else:
        zone_blocks = [zone_k] + [across(zone_k, "state", d) for d in range(1, n_state)]
    energy, energy_zone, filtered = call(
        energy_body, (inner, zone, SHAPE((count, owned), BF16)),
        (zone_k, inner_k, shift_inner, shift_zone, border, border_diagonal, columns, square, diagonal), work,
    )
    extra, scratch = (), []
    pair_of = SHAPE((count, count), F32)
    found_of = SHAPE((len(inner_blocks) * count, 2 * count), F32)
    if square_of_four:
        first_energy, part_1, found = call(
            first_neighbour_body, (inner, sums_of, SHAPE((2 * count, 2 * count), F32)),
            (*inner_blocks[:2], energy, shift_inner, columns, square, diagonal), work // 2,
        )
        second_found, *other = call(
            second_neighbour_body, (SHAPE((count, 2 * count), F32), pair_of, pair_of, zone),
            (*inner_blocks, first_energy, energy, columns), work // 4,
        )
        extra = (second_found, part_1, *other, shift_zone, border, border_diagonal)
        scratch = [pltpu.VMEM((count, 4 * rim), BF16)]
    else:
        found = call(gram_body, found_of, (*inner_blocks, energy), work)
    share = count * n_state // n_space
    chips = n_space // 2
    output = SHAPE((share, count), F32)
    piece = SHAPE((2 * share, count), BF16)
    both_halves = SHAPE((2, 2 * share, count), BF16)
    mine, give_half = call(
        functools.partial(project_body, square_of_four, 1.0 / (owned * n_space)),
        (SHAPE((chips, 2, 2 * share, count), BF16),
         SHAPE((2, 2, 2 * share, count) if square_of_four else (chips, 2 * share, count), BF16)),
        (energy_zone, found, *extra, *zone_blocks), work // 4, scratch=scratch,
    )
    got_half = swap(give_half, n_state, n_space, 0)
    if square_of_four:
        pieces = call(split_body, (both_halves,) * 2, (mine, got_half), 0)
        shares = [share_out(p, order, n_state, n_space) for order, p in enumerate(pieces)]
        keep, give_last = call(
            gather_body, (SHAPE(piece.shape, F32), piece), (pieces[1], *shares), 0
        )
        got_last = swap(give_last, n_state, n_space, 0)
        intersection, projected = call(join_body, (output, output), (keep, got_last), 0)
    else:
        pieces = call(halve_body, (piece,) * chips, (mine, got_half), 0)
        shares = [across(p, "space", 2 * d) for d, p in enumerate(pieces) if d]
        intersection, projected = call(final_body, (output, output), (pieces[0], *shares), 0)
    return filtered, intersection.T, projected.T


def four(n_state, n_space):
    return n_state == 4 and n_space == 8


def solution(mesh):
    return jax.shard_map(
        program,
        mesh=mesh,
        in_specs=(P("state", "space"), P("space", None, None), P("space", None), P("space")),
        out_specs=(P("state", "space"), P("state", "space"), P("state", "space")),
        check_vma=False,
    )
```

```python
import functools

import jax
import jax.numpy as jnp
from jax import lax
from jax.experimental import pallas as pl
from jax.experimental.pallas import tpu as pltpu
from jax.sharding import PartitionSpec as P


DEGREE = 4

spectrum_center = 3.0
spectrum_half = 3.5

BF16 = jnp.bfloat16
F32 = jnp.float32
SHAPE = jax.ShapeDtypeStruct


def call(body, outs, ins, flops, scratch=(), raw=()):
    where = [
        pl.BlockSpec(memory_space=pltpu.HBM if i in raw else pltpu.VMEM) for i in range(len(ins))
    ]
    ins = [pltpu.with_memory_space_constraint(x, pltpu.HBM) if i in raw else x for i, x in enumerate(ins)]
    return pl.pallas_call(
        body,
        out_shape=outs,
        in_specs=where,
        out_specs=jax.tree.map(lambda _: pl.BlockSpec(memory_space=pltpu.VMEM), outs),
        scratch_shapes=list(scratch),
        compiler_params=pltpu.CompilerParams(vmem_limit_bytes=24 << 20),
        cost_estimate=pl.CostEstimate(flops=flops, bytes_accessed=4 << 20, transcendentals=0),
    )(*ins)


def mm(a, b):
    return jnp.dot(a, b, preferred_element_type=F32)


def mm_nt(a, b):
    return lax.dot_general(a, b, (((1,), (1,)), ((), ())), preferred_element_type=F32)


def is_odd():
    return (lax.axis_index("space") & 1) == 1


def sort_out(got_a, got_b):
    me, odd = lax.axis_index("space"), is_odd()
    got_a, got_b = got_a.astype(F32), got_b.astype(F32)
    low = jnp.where(me == 0, 0.0, jnp.where(odd, got_a, got_b))
    high = jnp.where(me == lax.axis_size("space") - 1, 0.0, jnp.where(odd, got_b, got_a))
    return low, high


def hand_out(low, high, give_a_ref, give_b_ref):
    odd = is_odd()
    give_a_ref[...] = jnp.where(odd, low, high).astype(give_a_ref.dtype)
    give_b_ref[...] = jnp.where(odd, high, low).astype(give_b_ref.dtype)


def halo_body(states_ref, potential_ref, index_ref,
              give_a_ref, give_b_ref, row_ref, local_ref, low_ref, high_ref, sem):
    count, owned = states_ref.shape
    rim = low_ref.shape[1]
    copies = [
        pltpu.make_async_copy(states_ref.at[:, pl.ds(0, rim)], low_ref, sem.at[0]),
        pltpu.make_async_copy(states_ref.at[:, pl.ds(owned - rim, rim)], high_ref, sem.at[1]),
        pltpu.make_async_copy(potential_ref, row_ref, sem.at[2]),
        pltpu.make_async_copy(index_ref, local_ref, sem.at[3]),
    ]
    for copy in copies:
        copy.start()
    for copy in copies:
        copy.wait()
    odd = is_odd()
    low, high = low_ref[...].astype(F32), high_ref[...].astype(F32)
    give_a_ref[:count, :] = jnp.where(odd, low, high).astype(BF16)
    give_b_ref[:count, :] = jnp.where(odd, high, low).astype(BF16)
    for take, give_ref in ((odd, give_a_ref), (jnp.logical_not(odd), give_b_ref)):
        row = jnp.where(take, row_ref[:, :rim], row_ref[:, owned - rim :])
        row = jnp.broadcast_to(row, (16, rim))
        at = lax.broadcasted_iota(jnp.int32, row.shape, 0)
        first = row.astype(BF16).astype(F32)
        second = (row - first).astype(BF16).astype(F32)
        third = (row - first) - second
        give_ref[count:, :] = jnp.where(
            at == 0, first, jnp.where(at == 1, second, jnp.where(at == 2, third, 0.0))
        ).astype(BF16)


def spread_body(index_ref, states_ref, cells_ref,
                hot_ref, outer_ref, wide_ref, picked_ref, here_ref, cells_out_ref, sem):
    states_copy = pltpu.make_async_copy(states_ref, here_ref, sem.at[0])
    cells_copy = pltpu.make_async_copy(cells_ref, cells_out_ref, sem.at[1])
    states_copy.start()
    cells_copy.start()
    number, nodes, _ = cells_ref.shape
    extent = hot_ref.shape[0]
    rim = nodes // 4
    width = 2 * rim
    offset = lax.axis_index("space") * (extent - width) - rim
    for c in range(number):
        index = index_ref[c : c + 1, :] - offset
        hot = lax.broadcasted_iota(jnp.int32, (extent, nodes), 0) == index
        hot_ref[:, c * nodes : (c + 1) * nodes] = hot.astype(BF16)
    outer_ref[:rim, :] = hot_ref[:rim, :]
    outer_ref[rim:, :] = hot_ref[extent - rim :, :]
    states_copy.wait()
    picked_ref[...] = mm(here_ref[...], hot_ref[rim : extent - rim, :]).astype(BF16)
    cells_copy.wait()
    for c in range(number):
        here = slice(c * nodes, (c + 1) * nodes)
        wide_ref[:width, here] = mm(hot_ref[:width, here], cells_out_ref[c]).astype(BF16)
        wide_ref[width:, here] = mm(hot_ref[extent - width :, here], cells_out_ref[c]).astype(BF16)


def first_zone_body(states_ref, halo_a_ref, halo_b_ref, potential_ref, outer_ref, wide_ref, owned_ref,
                    inner_ref, zone_ref, shift_inner_ref, shift_zone_ref, picked_ref, sums_ref, give_a_ref, give_b_ref):
    count, owned = states_ref.shape
    rim = halo_a_ref.shape[1]
    width = 2 * rim
    low, high = sort_out(halo_a_ref[...], halo_b_ref[...])
    zone_ref[:, :rim] = low[:count].astype(BF16)
    zone_ref[:, rim:width] = states_ref[:, :rim]
    zone_ref[:, width : width + rim] = states_ref[:, owned - rim :]
    zone_ref[:, width + rim :] = high[:count].astype(BF16)
    inner_ref[...] = states_ref[:, rim : owned - rim]
    row = potential_ref[...] - spectrum_center
    shift_inner_ref[...] = row[:, rim : owned - rim]
    shift_zone_ref[:, rim:width] = row[:, :rim]
    shift_zone_ref[:, width : width + rim] = row[:, owned - rim :]
    for got, at in ((low, 0), (high, width + rim)):
        part = got[count : count + 8]
        shift_zone_ref[:, at : at + rim] = (part[0:1] + part[1:2] + part[2:3]) - spectrum_center
    picked = (
        owned_ref[...].astype(F32)
        + mm(jnp.concatenate([zone_ref[:, :rim], zone_ref[:, width + rim :]], axis=1), outer_ref[...])
    ).astype(BF16)
    picked_ref[...] = picked
    sums = mm_nt(picked, wide_ref[...])
    sums_ref[...] = sums
    hand_out(sums[:, :width], sums[:, width:], give_a_ref, give_b_ref)


def take_diagonal(rows, start, matrix_ref, diagonal_ref, at):
    size = rows.shape[0]
    same = lax.broadcasted_iota(jnp.int32, (size, size), 0) == lax.broadcasted_iota(
        jnp.int32, (size, size), 1
    )
    square = rows[:, at : at + size]
    diagonal_ref[:, at : at + size] = jnp.sum(jnp.where(same, square, 0.0), axis=0, keepdims=True)
    matrix_ref[start : start + size, :] = rows.astype(BF16)
    matrix_ref[start : start + size, at : at + size] = jnp.where(same, 0.0, square).astype(BF16)


def first_inner_body(inner_ref, picked_ref, shift_inner_ref, hot_ref, wide_ref, cells_ref,
                     next_ref, wide_inner_ref, border_ref, diagonal_ref, part_ref, next_picked_ref, columns_ref):
    extent = hot_ref.shape[0]
    width = border_ref.shape[1] // 2
    inside = slice(width, extent - width)
    number, nodes, _ = cells_ref.shape
    for c in range(number):
        here = slice(c * nodes, (c + 1) * nodes)
        wide_inner_ref[:, here] = mm(hot_ref[inside, here], cells_ref[c]).astype(BF16)
    value = mm_nt(picked_ref[...], wide_inner_ref[...]) + shift_inner_ref[...] * inner_ref[...].astype(F32)
    next_ref[...] = (value * (1.0 / spectrum_half)).astype(BF16)
    columns_ref[:width, :] = hot_ref[:width, :]
    columns_ref[width:, :] = hot_ref[extent - width :, :]
    for at in (0, width):
        rows = mm_nt(wide_ref[at : at + width, :], columns_ref[...])
        take_diagonal(rows, at, border_ref, diagonal_ref, at)
    next_picked_ref[...] = mm(next_ref[...], hot_ref[inside, :]).astype(BF16)
    part_ref[...] = mm_nt(next_picked_ref[...], wide_ref[...])


def close_zones(sums_ref, got_a_ref, got_b_ref, shift_zone_ref, mid_ref, old_ref, scale, zone_ref):
    width = got_a_ref.shape[1]
    low, high = sort_out(got_a_ref[...], got_b_ref[...])
    for got, here in ((low, slice(0, width)), (high, slice(width, 2 * width))):
        value = sums_ref[:, here] + got + shift_zone_ref[:, here] * mid_ref[:, here].astype(F32)
        value = value * scale
        if old_ref is not None:
            value = value - old_ref[:, here].astype(F32)
        zone_ref[:, here] = value.astype(BF16)


def zone_sums(zone_ref, part, border_ref, border_diagonal_ref):
    width = zone_ref.shape[1] // 2
    sums = part + mm(zone_ref[...], border_ref[...]) + border_diagonal_ref[...] * zone_ref[...].astype(F32)
    return sums[:, :width], sums[:, width:]


def zone_body(has_old, scale, sums_ref, got_a_ref, got_b_ref, shift_zone_ref, mid_ref, *rest):
    old_ref, rest = (rest[0], rest[1:]) if has_old else (None, rest)
    part_ref, border_ref, border_diagonal_ref, zone_ref, next_sums_ref, give_a_ref, give_b_ref = rest
    close_zones(sums_ref, got_a_ref, got_b_ref, shift_zone_ref, mid_ref, old_ref, scale, zone_ref)
    low, high = zone_sums(zone_ref, part_ref[...], border_ref, border_diagonal_ref)
    width = low.shape[1]
    next_sums_ref[:, :width] = low
    next_sums_ref[:, width:] = high
    hand_out(low, high, give_a_ref, give_b_ref)


def inner_sums(zone_ref, inner_ref, columns_ref, square_ref, diagonal_ref):
    return (
        mm_nt(zone_ref[...], columns_ref[...])
        + mm(inner_ref[...], square_ref[...])
        + diagonal_ref[...] * inner_ref[...].astype(F32)
    )


def second_inner_body(zone_ref, inner_ref, old_ref, shift_inner_ref, picked_ref, hot_ref, wide_inner_ref, zone_hot_ref,
                      next_ref, part_ref, columns_ref, square_ref, diagonal_ref):
    extent = hot_ref.shape[0]
    width = zone_ref.shape[1] // 2
    columns_ref[...] = mm_nt(wide_inner_ref[...], zone_hot_ref[...]).astype(BF16)
    picked = (picked_ref[...].astype(F32) + mm(zone_ref[...], zone_hot_ref[...])).astype(BF16)
    sums = mm_nt(picked, wide_inner_ref[...])
    value = (sums + shift_inner_ref[...] * inner_ref[...].astype(F32)) * (2.0 / spectrum_half)
    next_ref[...] = (value - old_ref[...].astype(F32)).astype(BF16)
    part_ref[...] = mm(next_ref[...], columns_ref[...])
    rows = mm_nt(wide_inner_ref[: square_ref.shape[0], :], hot_ref[width : extent - width, :])
    diagonal_ref[...] = jnp.zeros_like(diagonal_ref)
    take_diagonal(rows, 0, square_ref, diagonal_ref, 0)


def third_inner_body(zone_ref, inner_ref, old_ref, shift_inner_ref, columns_ref, begun_ref, begun_diagonal_ref,
                     hot_ref, wide_inner_ref, square_ref, diagonal_ref, next_ref, part_ref, open_ref):
    size, step = square_ref.shape[0], begun_ref.shape[0]
    width = (hot_ref.shape[0] - size) // 2
    square_ref[:step, :] = begun_ref[...]
    diagonal_ref[...] = begun_diagonal_ref[...]
    for start in range(step, size, step):
        rows = mm_nt(wide_inner_ref[start : start + step, :], hot_ref[width : width + size, :])
        take_diagonal(rows, start, square_ref, diagonal_ref, start)
    line = diagonal_ref[...] + shift_inner_ref[...]
    sums = (
        mm_nt(zone_ref[...], columns_ref[...])
        + mm(inner_ref[...], square_ref[...])
        + line * inner_ref[...].astype(F32)
    )
    next_ref[...] = (sums * (2.0 / spectrum_half) - old_ref[...].astype(F32)).astype(BF16)
    part_ref[...] = mm(next_ref[...], columns_ref[...])
    open_ref[...] = mm(next_ref[...], square_ref[...]) + line * next_ref[...].astype(F32)


def last_inner_body(zone_ref, open_ref, old_ref, columns_ref, next_ref):
    sums = open_ref[...] + mm_nt(zone_ref[...], columns_ref[...])
    value = sums * (2.0 / spectrum_half) - old_ref[...].astype(F32)
    next_ref[...] = value.astype(BF16)


def last_zone_body(sums_ref, got_a_ref, got_b_ref, shift_zone_ref, mid_ref, old_ref, zone_ref):
    close_zones(sums_ref, got_a_ref, got_b_ref, shift_zone_ref, mid_ref, old_ref,
                2.0 / spectrum_half, zone_ref)


def zone_energy(zone_ref, part, shift_zone_ref, border_ref, border_diagonal_ref, energy_ref):
    low, high = zone_sums(zone_ref, part, border_ref, border_diagonal_ref)
    width = low.shape[1]
    rim = width // 2
    own = (shift_zone_ref[:, rim : width + rim] + spectrum_center) * zone_ref[:, rim : width + rim].astype(F32)
    energy_ref[:, :rim] = low[:, :rim].astype(energy_ref.dtype)
    energy_ref[:, rim:width] = (low[:, rim:] + own[:, :rim]).astype(energy_ref.dtype)
    energy_ref[:, width : width + rim] = (high[:, :rim] + own[:, rim:]).astype(energy_ref.dtype)
    energy_ref[:, width + rim :] = high[:, rim:].astype(energy_ref.dtype)


def energy_body(zone_ref, inner_ref, shift_inner_ref, shift_zone_ref,
                border_ref, border_diagonal_ref, columns_ref, square_ref, diagonal_ref, energy_ref, energy_zone_ref, filtered_ref):
    sums = inner_sums(zone_ref, inner_ref, columns_ref, square_ref, diagonal_ref)
    own = (shift_inner_ref[...] + spectrum_center) * inner_ref[...].astype(F32)
    energy_ref[...] = (sums + own).astype(BF16)
    width = zone_ref.shape[1] // 2
    part = mm(inner_ref[...], columns_ref[...])
    zone_energy(zone_ref, part, shift_zone_ref, border_ref, border_diagonal_ref, energy_zone_ref)
    rim = width // 2
    owned = filtered_ref.shape[1]
    filtered_ref[:, :rim] = zone_ref[:, rim:width]
    filtered_ref[:, rim : owned - rim] = inner_ref[...]
    filtered_ref[:, owned - rim :] = zone_ref[:, width : width + rim]


def first_neighbour_body(inner_ref, first_ref, energy_ref, shift_inner_ref, columns_ref, square_ref, diagonal_ref,
                         first_energy_ref, part_ref, found_ref):
    first = first_ref[...]
    line = diagonal_ref[...] + (shift_inner_ref[...] + spectrum_center)
    first_energy_ref[...] = (mm(first, square_ref[...]) + line * first.astype(F32)).astype(BF16)
    part_ref[...] = mm(first, columns_ref[...])
    inner_found(found_ref, (inner_ref[...], first), inner_ref, energy_ref)


def turned(first, second):
    odd = is_odd()
    return mm_nt(jnp.where(odd, first, second), jnp.where(odd, second, first))


def second_neighbour_body(inner_ref, first_ref, second_ref, first_energy_ref, energy_ref, columns_ref,
                          found_ref, other_ref, other_energy_ref, toward_ref):
    second = second_ref[...]
    inner_found(found_ref, (second,), inner_ref, energy_ref)
    other_ref[...] = turned(first_ref[...], second)
    other_energy_ref[...] = turned(first_energy_ref[...], second)
    toward_ref[...] = mm(second, columns_ref[...]).astype(BF16)


def inner_found(found_ref, blocks, states_ref, energy_ref):
    count = states_ref.shape[0]
    for place, block in enumerate(blocks):
        here = slice(place * count, (place + 1) * count)
        found_ref[here, :count] = mm_nt(block, states_ref[...])
        found_ref[here, count:] = mm_nt(block, energy_ref[...])


def gram_body(*refs):
    *blocks, energy_ref, found_ref = refs
    inner_found(found_ref, [block[...] for block in blocks], blocks[0], energy_ref)


def zone_found(block_ref, zone_ref, energy_zone_ref):
    rim = zone_ref.shape[1] // 4
    here = slice(rim, 3 * rim)
    return mm_nt(block_ref[:, here], zone_ref[:, here]), mm_nt(block_ref[...], energy_zone_ref[...])


def project_body(square_of_four, scale, energy_zone_ref, found_ref, *refs):
    if square_of_four:
        (second_found_ref, part_ref, other_ref, other_energy_ref, toward_ref,
         shift_zone_ref, border_ref, border_diagonal_ref), refs = refs[:8], refs[8:]
        *zones, out_ref, give_ref, other_zone_ref = refs
    else:
        *zones, out_ref, give_ref = refs
    count = energy_zone_ref.shape[0]
    columns = out_ref.shape[2] // 2
    group = lax.axis_index("state")
    odd = is_odd()

    def put(distance, states, energy):
        at = group ^ distance
        for block, there in ((states * scale, slice(0, columns)), (energy * scale, slice(columns, 2 * columns))):
            parts = [block[:columns], block[columns:]]
            for core in range(2):
                out_ref[at, core, there] = parts[core].astype(BF16)
            if not square_of_four:
                give_ref[at, there] = jnp.where(odd, parts[0], parts[1]).astype(BF16)

    if square_of_four:
        zone_energy(zones[1], part_ref[...], shift_zone_ref, border_ref, border_diagonal_ref, other_zone_ref)
    for place, zone in enumerate(zones):
        distance, found, row = place, found_ref, place
        if square_of_four and place:
            distance = jnp.where(odd, 3 - place, place)
            if place == 2:
                found, row = second_found_ref, 0
        here = slice(row * count, (row + 1) * count)
        states, energy = zone_found(zone, zones[0], energy_zone_ref)
        put(distance, found[here, :count] + states, found[here, count:] + energy)
    if square_of_four:
        rim = zones[1].shape[1] // 4
        own = slice(rim, 3 * rim)
        states = turned(zones[1][:, own], zones[2][:, own])
        energy = turned(other_zone_ref[...], zones[2][...]) + turned(zones[1][...], toward_ref[...])
        put(3, other_ref[...] + states, other_energy_ref[...] + energy)
        for order, (even, uneven) in enumerate(CORE_WAYS):
            give_ref[order] = out_ref[chip_at(jnp.where(odd, even, uneven))]


CORE_WAYS = ((1, 3), (0, 2))


def chip_at(distance):
    return (lax.axis_index("space") >> 1) ^ distance


def split_body(mine_ref, got_ref, *pieces):
    odd = is_odd()
    for order, (even, uneven) in enumerate(CORE_WAYS):
        block = mine_ref[chip_at(jnp.where(odd, uneven, even))].astype(F32)
        pieces[order][...] = (block + got_ref[order].astype(F32)).astype(BF16)


def gather_body(mine_ref, first_ref, second_ref, keep_ref, give_ref):
    odd = is_odd()
    made_elsewhere = jnp.logical_or(odd, chip_at(0) == (lax.axis_index("state") ^ 3))
    second = jnp.where(made_elsewhere, second_ref[...].astype(F32), mine_ref[...].astype(F32))
    total = first_ref[...].astype(F32) + second
    keep_ref[...] = jnp.where(odd, total[1], total[0])
    give_ref[...] = jnp.where(odd, total[0], total[1]).astype(BF16)


def join_body(keep_ref, got_ref, first_ref, second_ref):
    total = keep_ref[...] + got_ref[...].astype(F32)
    columns = first_ref.shape[0]
    first_ref[...] = total[:columns]
    second_ref[...] = total[columns:]


def halve_body(mine_ref, got_ref, *pieces):
    for distance, piece_ref in enumerate(pieces):
        chip = (lax.axis_index("space") >> 1) ^ distance
        total = mine_ref[chip, lax.axis_index("space") & 1].astype(F32) + got_ref[chip].astype(F32)
        piece_ref[...] = total.astype(BF16)


def final_body(mine_ref, *refs):
    parts, (first_ref, second_ref) = refs[:-2], refs[-2:]
    total = mine_ref[...].astype(F32)
    for part in parts:
        total = total + part[...].astype(F32)
    columns = first_ref.shape[0]
    first_ref[...] = total[:columns]
    second_ref[...] = total[columns:]


def swap(block, n_state, n_space, lead):
    route = []
    for s in range(n_state):
        for i in range(n_space):
            j = i + 1 if (i - lead) % 2 == 0 else i - 1
            if 0 <= j < n_space:
                route.append((s * n_space + i, s * n_space + j))
            elif (s ^ 1) < n_state:
                route.append((s * n_space + i, (s ^ 1) * n_space + i))
    return lax.ppermute(block, ("state", "space"), route)


def exchange(give_a, give_b, n_state, n_space):
    got_a = swap(give_a, n_state, n_space, 0)
    got_b = swap(give_b, n_state, n_space, 1)
    return got_a, got_b


def across(block, axis, distance):
    return lax.ppermute(block, axis, [(i, i ^ distance) for i in range(lax.axis_size(axis))])


def beside(block, first, n_state, n_space):
    route = []
    for s in range(n_state):
        for i in range(n_space):
            distance = 1 if first == (i & 1 == 0) else 2
            route.append((s * n_space + i, (s ^ distance) * n_space + i))
    return lax.ppermute(block, ("state", "space"), route)


def share_out(block, order, n_state, n_space):
    route = []
    for s in range(n_state):
        for i in range(n_space):
            distance = CORE_WAYS[order][i & 1]
            to_group, to_chip = s, (i >> 1) ^ distance
            if distance == 0 or to_chip == s ^ 3:
                to_group, to_chip = s ^ 1, to_chip ^ 1
            route.append((s * n_space + i, to_group * n_space + 2 * to_chip + (i & 1)))
    return lax.ppermute(block, ("state", "space"), route)


def program(states_in, cell_matrices, connectivity, potential):
    count, owned = states_in.shape
    cells, nodes, _ = cell_matrices.shape
    rim = nodes // 4
    extent, inside = owned + 2 * rim, owned - 2 * rim
    n_state, n_space = lax.axis_size("state"), lax.axis_size("space")
    row = potential.reshape(1, owned)
    work = 2 * count * extent * extent
    inner = SHAPE((count, inside), BF16)
    zone, sums_of = SHAPE((count, 4 * rim), BF16), SHAPE((count, 4 * rim), F32)
    give = SHAPE((count, 2 * rim), BF16)

    halo = SHAPE((count + 16, rim), BF16)
    *gave, row, local = call(
        halo_body,
        (halo, halo, SHAPE(row.shape, F32), SHAPE(connectivity.shape, connectivity.dtype)),
        (states_in, row, connectivity), 0, raw=(0, 1, 2),
        scratch=[
            pltpu.VMEM((count, rim), BF16), pltpu.VMEM((count, rim), BF16), pltpu.SemaphoreType.DMA((4,)),
        ],
    )
    got = exchange(*gave, n_state, n_space)
    table = SHAPE((extent, cells * nodes), BF16)
    hot, outer, wide, picked, states_here, cells_here = call(
        spread_body,
        (table, SHAPE((2 * rim, cells * nodes), BF16), SHAPE((4 * rim, cells * nodes), BF16),
         SHAPE((count, cells * nodes), BF16), SHAPE(states_in.shape, BF16), SHAPE(cell_matrices.shape, BF16)),
        (local, states_in, cell_matrices), work, raw=(1, 2), scratch=[pltpu.SemaphoreType.DMA((2,))],
    )
    border_line, line = SHAPE((1, 4 * rim), F32), SHAPE((1, inside), F32)
    inner_0, zone_0, shift_inner, shift_zone, picked, sums, *gave = call(
        first_zone_body,
        (inner, zone, line, border_line, SHAPE((count, cells * nodes), BF16), sums_of, give, give),
        (states_here, *got, row, outer, wide, picked), work,
    )
    got = exchange(*gave, n_state, n_space)
    inner_1, wide_inner, border, border_diagonal, partial, picked, zone_hot = call(
        first_inner_body,
        (inner, SHAPE((inside, cells * nodes), BF16), SHAPE((4 * rim, 4 * rim), BF16), border_line, sums_of,
         SHAPE((count, cells * nodes), BF16), SHAPE((4 * rim, cells * nodes), BF16)),
        (inner_0, picked, shift_inner, hot, wide, cells_here), 8 * extent * rim * cells * nodes,
    )
    inners, zones = [inner_0, inner_1], [zone_0]
    for k in range(1, DEGREE):
        older = zones[-2:-1]
        scale = (2.0 if older else 1.0) / spectrum_half
        zone_k, sums, *gave = call(
            functools.partial(zone_body, bool(older), scale),
            (zone, sums_of, give, give),
            (sums, *got, shift_zone, zones[-1], *older, partial, border, border_diagonal), work // 6,
        )
        zones.append(zone_k)
        got = exchange(*gave, n_state, n_space)
        ins = (zone_k, inners[-1], inners[-2], shift_inner)
        if k == 1:
            inner_k, partial, columns, begun, begun_diagonal = call(
                second_inner_body,
                (inner, sums_of, SHAPE((inside, 4 * rim), BF16), SHAPE((2 * rim, inside), BF16), line),
                (*ins, picked, hot, wide_inner, zone_hot), 4 * extent * rim * cells * nodes,
            )
        elif k == 2:
            square, diagonal, inner_k, partial, opened = call(
                third_inner_body,
                (SHAPE((inside, inside), BF16), line, inner, sums_of, SHAPE((count, inside), F32)),
                (*ins, columns, begun, begun_diagonal, hot, wide_inner), 4 * extent * rim * cells * nodes,
            )
        else:
            inner_k = call(last_inner_body, inner, (zone_k, opened, inners[-2], columns), work // 4)
        inners.append(inner_k)
    square_of_four = four(n_state, n_space)
    if square_of_four:
        inner_blocks = [inner_k] + [beside(inner_k, first, n_state, n_space) for first in (True, False)]
    else:
        inner_blocks = [inner_k] + [across(inner_k, "state", d) for d in range(1, n_state)]
    zone_k = call(
        last_zone_body, zone, (sums, *got, shift_zone, zones[-1], zones[-2]), 0
    )
    if square_of_four:
        zone_blocks = [zone_k] + [beside(zone_k, first, n_state, n_space) for first in (True, False)]
    else:
        zone_blocks = [zone_k] + [across(zone_k, "state", d) for d in range(1, n_state)]
    energy, energy_zone, filtered = call(
        energy_body, (inner, zone, SHAPE((count, owned), BF16)),
        (zone_k, inner_k, shift_inner, shift_zone, border, border_diagonal, columns, square, diagonal), work,
    )
    extra, scratch = (), []
    pair_of = SHAPE((count, count), F32)
    found_of = SHAPE((len(inner_blocks) * count, 2 * count), F32)
    if square_of_four:
        first_energy, part_1, found = call(
            first_neighbour_body, (inner, sums_of, SHAPE((2 * count, 2 * count), F32)),
            (*inner_blocks[:2], energy, shift_inner, columns, square, diagonal), work // 2,
        )
        second_found, *other = call(
            second_neighbour_body, (SHAPE((count, 2 * count), F32), pair_of, pair_of, zone),
            (*inner_blocks, first_energy, energy, columns), work // 4,
        )
        extra = (second_found, part_1, *other, shift_zone, border, border_diagonal)
        scratch = [pltpu.VMEM((count, 4 * rim), BF16)]
    else:
        found = call(gram_body, found_of, (*inner_blocks, energy), work)
    share = count * n_state // n_space
    chips = n_space // 2
    output = SHAPE((share, count), F32)
    piece = SHAPE((2 * share, count), BF16)
    both_halves = SHAPE((2, 2 * share, count), BF16)
    mine, give_half = call(
        functools.partial(project_body, square_of_four, 1.0 / (owned * n_space)),
        (SHAPE((chips, 2, 2 * share, count), BF16),
         SHAPE((2, 2, 2 * share, count) if square_of_four else (chips, 2 * share, count), BF16)),
        (energy_zone, found, *extra, *zone_blocks), work // 4, scratch=scratch,
    )
    got_half = swap(give_half, n_state, n_space, 0)
    if square_of_four:
        pieces = call(split_body, (both_halves,) * 2, (mine, got_half), 0)
        shares = [share_out(p, order, n_state, n_space) for order, p in enumerate(pieces)]
        keep, give_last = call(
            gather_body, (SHAPE(piece.shape, F32), piece), (pieces[1], *shares), 0
        )
        got_last = swap(give_last, n_state, n_space, 0)
        intersection, projected = call(join_body, (output, output), (keep, got_last), 0)
    else:
        pieces = call(halve_body, (piece,) * chips, (mine, got_half), 0)
        shares = [across(p, "space", 2 * d) for d, p in enumerate(pieces) if d]
        intersection, projected = call(final_body, (output, output), (pieces[0], *shares), 0)
    return filtered, intersection.T, projected.T


def four(n_state, n_space):
    return n_state == 4 and n_space == 8


def solution(mesh):
    return jax.shard_map(
        program,
        mesh=mesh,
        in_specs=(P("state", "space"), P("space", None, None), P("space", None), P("space")),
        out_specs=(P("state", "space"), P("state", "space"), P("state", "space")),
        check_vma=False,
    )
```
